32 devices in a mesh: ctx: 8 (over z, x), tp: 4 (over y, core).
Axes of the slice: x: 2, y: 2, z: 4, core: 2. Of those that a mesh axis runs over, the one named last changes fastest.
Arguments:
- tokens: bfloat16 [4, 2048, 1024], P(None, ('ctx', 'tp')), may hold values from -6 to 6
- gain_one: bfloat16 [1024], replicated, may hold values from 0.099609375 to 1.8984375
- shift_one: bfloat16 [1024], replicated, may hold values from -3 to 3
- query_key_value_weight: bfloat16 [1024, 16, 192], P(None, 'tp'), may hold values from -0.1875 to 0.1875
- qv_bias: bfloat16 [16, 128], P('tp'), may hold values from -3 to 3
- attention_out_weight: bfloat16 [16, 64, 1024], P('tp'), may hold values from -0.75 to 0.75
- attention_out_bias: bfloat16 [1024], replicated, may hold values from -3 to 3
- gain_two: bfloat16 [1024], replicated, may hold values from 0.099609375 to 1.8984375
- shift_two: bfloat16 [1024], replicated, may hold values from -3 to 3
- expand_weight: bfloat16 [1024, 4096], P(None, 'tp'), may hold values from -0.1875 to 0.1875
- expand_bias: bfloat16 [4096], P('tp'), may hold values from -3 to 3
- contract_weight: bfloat16 [4096, 1024], P('tp'), may hold values from -0.09375 to 0.09375
- contract_bias: bfloat16 [1024], replicated, may hold values from -3 to 3
- doc_ids: int32 [4, 2048], P(None, 'ctx'), may hold values from 0 to 2, never falling along the last dimension, each value on 1 to 1536 neighbouring positions
- out_grad: bfloat16 [4, 2048, 1024], P(None, ('ctx', 'tp')), may hold values from -6 to 6
Outputs:
- layer_out: bfloat16 [4, 2048, 1024], P(None, ('ctx', 'tp'))
- grad_tokens: float32 [4, 2048, 1024], P(None, ('ctx', 'tp'))
- grad_gainone: float32 [1024], replicated
- grad_shiftone: float32 [1024], replicated
- grad_qkv: float32 [1024, 16, 192], P(None, 'tp')
- grad_qvbias: float32 [16, 128], P('tp')
- grad_outweight: float32 [16, 64, 1024], P('tp')
- grad_outbias: float32 [1024], replicated
- grad_gaintwo: float32 [1024], replicated
- grad_shifttwo: float32 [1024], replicated
- grad_fcweight: float32 [1024, 4096], P(None, 'tp')
- grad_fcbias: float32 [4096], P('tp')
- grad_projweight: float32 [4096, 1024], P('tp')
- grad_projbias: float32 [1024], replicated
The draws below stay inside these ranges and needn't reach their ends.
Inputs may be any that keep to these rules, and one draw needn't show every extreme that they name: `doc_ids`: in each sequence the document numbers never fall along positions; each of the 3 documents has 1 to 1536 positions, and one has exactly 1536.
All inputs are finite; a program needn't handle non-finite values.
Results may differ from the reference program's by a relative error of at most 0.02.
Values may be sent and summed in bfloat16 or wider, within the bound.
No kernel may reach another device: no remote copies, remote signals or barrier semaphores. Data moves between devices by JAX's collectives and lax.ppermute only.
A program may use at most 256 MiB of HBM per device.

```python
import math
import jax
import jax.numpy as jnp
import numpy as np
from jax import lax

D = 1024
HEADS = 16
HEAD_DIM = 64
FF = 4096
DOCS = 3
SEQS = 4
LENGTH = 2048


def steps_of(stream_key, extent, cuts, low, high):
    level = 1.0
    for axis_at, blocks in cuts:
        draws = jax.random.uniform(jax.random.fold_in(jax.random.fold_in(stream_key, 6), axis_at), (blocks,), jnp.float32, low / len(cuts), high / len(cuts))
        level = level * jnp.repeat(jnp.exp(draws), extent[axis_at] // blocks).reshape((-1,) + (1,) * (len(extent) - 1 - axis_at))
    return level


def length_profile(number_of, total, limit, skew):
    loads = [(1 << 20) // math.isqrt(rank ** skew) + 1 for rank in range(2, number_of + 1)]
    rest, given = total - limit - (number_of - 1), [1] * (number_of - 1)
    while rest > 0:
        candidates = [i for i in range(number_of - 1) if given[i] < limit]
        whole, remaining = sum([loads[i] for i in candidates]), rest
        for i in candidates:
            addition = min(limit - given[i], max(1, remaining * loads[i] // whole), rest)
            given[i] = given[i] + addition
            rest = rest - addition
    return np.array([limit] + given)


def uneven_parts(key, amount, total, limit, skew):
    if amount == 2:
        one = jax.random.randint(key, (), max(1, total - limit), min(limit, total - 1) + 1)
        return jnp.stack([one, total - one])
    tallies = jnp.asarray(length_profile(amount, total, limit, skew), jnp.int32)
    pairs = (amount - 1) // 2
    giver, receiver = tallies[1:1 + 2 * pairs:2], tallies[2:2 + 2 * pairs:2]
    room = jnp.minimum(giver - 1, limit - receiver)
    shifted = jax.random.randint(jax.random.fold_in(key, 1), (pairs,), 0, 1 << 20) % (room + 1)
    tallies = tallies.at[1:1 + 2 * pairs:2].set(giver - shifted).at[2:2 + 2 * pairs:2].set(receiver + shifted)
    return tallies[jax.random.permutation(jax.random.fold_in(key, 2), amount)]


def noise(rng, extent, width, most, pieces=(), kind=jnp.bfloat16):
    array = width * jax.random.normal(rng, extent, jnp.float32)
    if pieces:
        array = array * steps_of(rng, extent, pieces, -0.22, 0.18)
    return jnp.clip(array, -most, most).astype(kind)


def setup_inputs(seed: int = 0) -> dict:
    splits = jax.random.split(jax.random.key(seed), 16)
    return {
        "tokens": noise(splits[0], (SEQS, LENGTH, D), 1.0, 6.0, ((1, 32),)),
        "gain_one": jnp.clip(1.0 + 0.18 * jax.random.normal(splits[1], (D,), jnp.float32), 0.099609375, 1.8984375).astype(jnp.bfloat16),
        "shift_one": noise(splits[2], (D,), 0.5, 3.0),
        "query_key_value_weight": noise(splits[3], (D, HEADS, 3 * HEAD_DIM), D ** -0.5, 0.1875, ((1, 4),)),
        "qv_bias": noise(splits[4], (HEADS, 2 * HEAD_DIM), 0.5, 3.0, ((0, 4),)),
        "attention_out_weight": noise(splits[5], (HEADS, HEAD_DIM, D), HEAD_DIM ** -0.5, 0.75, ((0, 4),)),
        "attention_out_bias": noise(splits[6], (D,), 0.5, 3.0),
        "gain_two": jnp.clip(1.0 + 0.18 * jax.random.normal(splits[7], (D,), jnp.float32), 0.099609375, 1.8984375).astype(jnp.bfloat16),
        "shift_two": noise(splits[8], (D,), 0.5, 3.0),
        "expand_weight": noise(splits[9], (D, FF), D ** -0.5, 0.1875, ((1, 4),)),
        "expand_bias": noise(splits[10], (FF,), 0.5, 3.0, ((0, 4),)),
        "contract_weight": noise(splits[11], (FF, D), FF ** -0.5, 0.09375, ((0, 4),)),
        "contract_bias": noise(splits[12], (D,), 0.5, 3.0),
        "doc_ids": jax.vmap(lambda own: jnp.searchsorted(jnp.cumsum(uneven_parts(own, DOCS, LENGTH, 3 * LENGTH // 4, 0)), jnp.arange(LENGTH), side="right"))(jax.random.split(splits[13], SEQS)).reshape((SEQS, LENGTH)).astype(jnp.int32),
        "out_grad": noise(splits[14], (SEQS, LENGTH, D), 1.0, 6.0, ((1, 32),)),
    }


@jax.custom_vjp
def low(v):
    return lax.optimization_barrier(v.astype(jnp.bfloat16)).astype(jnp.float32)

@jax.custom_vjp
def reduced_backward(v):
    return v

def low_keep(v):
    return (low(v), None)

def low_pass(kept, grad):
    return (grad,)

def back_keep(v):
    return (v, None)

def back_low(kept, grad):
    return (low(grad),)
low.defvjp(low_keep, low_pass)
reduced_backward.defvjp(back_keep, back_low)
highest_score = lax.Precision.HIGHEST
eps = 1e-05
neg_fill = -1e+30

def layer_norm(values, gain, shift):
    centre = lax.optimization_barrier(jnp.mean(values, axis=-1, keepdims=True))
    centred = values - centre
    spread = lax.optimization_barrier(jnp.mean(centred * centred, axis=-1, keepdims=True))
    return centred * lax.rsqrt(spread + eps) * gain + shift

def attend_sequence(sequence_args):
    queries, all_keys, values, doc_row = sequence_args
    length = queries.shape[0]
    block_width = min(512, length)
    block_count = length // block_width
    score_scale = HEAD_DIM ** (-0.5)
    key_pos = jnp.arange(length, dtype=jnp.int32)

    @jax.checkpoint
    def one_block(block_args):
        query_rows, query_ids, first_row = block_args
        scores = jnp.einsum('qhe,khe->hqk', query_rows, all_keys, precision=highest_score) * score_scale
        scores = reduced_backward(scores)
        query_pos = first_row + jnp.arange(block_width, dtype=jnp.int32)
        allowed = jnp.logical_and(key_pos[None, :] <= query_pos[:, None], doc_row[None, :] == query_ids[:, None])
        scores = jnp.where(allowed[None], scores, neg_fill)
        softmax_weights = low(jax.nn.softmax(scores, axis=-1))
        return jnp.einsum('hqk,khe->qhe', softmax_weights, values, precision=highest_score)
    starts = jnp.arange(block_count, dtype=jnp.int32) * block_width
    blocks = lax.map(one_block, (queries.reshape(block_count, block_width, HEADS, HEAD_DIM), doc_row.reshape(block_count, block_width), starts))
    return blocks.reshape(length, HEADS, HEAD_DIM)

def forward(tokens, gain_one, shift_one, query_key_value_weight, qv_bias, attention_out_weight, attention_out_bias, gain_two, shift_two, expand_weight, expand_bias, contract_weight, contract_bias, doc_ids):
    first_normed = low(layer_norm(tokens, gain_one, shift_one))
    packed_values = jnp.einsum('uwj,jma->uwma', first_normed, query_key_value_weight, precision=highest_score)
    queries = reduced_backward(low(packed_values[..., :HEAD_DIM] + qv_bias[:, :HEAD_DIM]))
    keys_all = reduced_backward(low(packed_values[..., HEAD_DIM:2 * HEAD_DIM]))
    values = reduced_backward(low(packed_values[..., 2 * HEAD_DIM:] + qv_bias[:, HEAD_DIM:]))
    combined_heads = lax.map(attend_sequence, (queries, keys_all, values, doc_ids))
    combined_heads = reduced_backward(low(combined_heads))
    attention_branch = reduced_backward(jnp.einsum('gwvi,vip->gwp', combined_heads, attention_out_weight, precision=highest_score)) + attention_out_bias
    residual_one = tokens + attention_branch
    second_normed = low(layer_norm(residual_one, gain_two, shift_two))
    pre_activation = reduced_backward(jnp.einsum('vuw,wp->vup', second_normed, expand_weight, precision=highest_score) + expand_bias)
    active_rows = low(jax.nn.gelu(pre_activation, approximate=True))
    feedforward_branch = reduced_backward(jnp.einsum('hkp,pn->hkn', active_rows, contract_weight, precision=highest_score)) + contract_bias
    return residual_one + feedforward_branch

def reference(tokens, gain_one, shift_one, query_key_value_weight, qv_bias, attention_out_weight, attention_out_bias, gain_two, shift_two, expand_weight, expand_bias, contract_weight, contract_bias, doc_ids, out_grad):
    float_args = tuple((array_in.astype(jnp.float32) for array_in in (tokens, gain_one, shift_one, query_key_value_weight, qv_bias, attention_out_weight, attention_out_bias, gain_two, shift_two, expand_weight, expand_bias, contract_weight, contract_bias)))

    def run_layer(*float_vals):
        return forward(*float_vals, doc_ids)
    layer_out, pull_back = jax.vjp(run_layer, *float_args)
    gradients = pull_back(out_grad.astype(jnp.float32))
    return (layer_out.astype(jnp.bfloat16), gradients[0], gradients[1], gradients[2], gradients[3], gradients[4], gradients[5], gradients[6], gradients[7], gradients[8], gradients[9], gradients[10], gradients[11], gradients[12])
```

```python
import jax
import jax.numpy as jnp
from jax import lax
from jax.experimental import pallas as pl
from jax.experimental.pallas import tpu as pltpu
from jax.sharding import PartitionSpec as P

HEAD_DIM = 64


eps = 1e-05
neg_fill = -1e30


def layer_norm(values, gain, shift):
    centre = jnp.mean(values, axis=-1, keepdims=True)
    centred = values - centre
    spread = jnp.mean(centred * centred, axis=-1, keepdims=True)
    return centred * lax.rsqrt(spread + eps) * gain + shift


def gelu_tanh(values):
    return jax.nn.gelu(values, approximate=True)


def gather_attn(values):
    return lax.all_gather(values, "tp", axis=1, tiled=True)


def reduce_attn(values):
    return lax.psum_scatter(
        values.astype(jnp.bfloat16), "tp", scatter_dimension=1, tiled=True
    ).astype(jnp.float32)


def gather_mlp(values):
    return lax.all_gather(values, "tp", axis=1, tiled=True)


def reduce_mlp(values):
    return lax.psum_scatter(
        values.astype(jnp.bfloat16), "tp", scatter_dimension=1, tiled=True
    ).astype(jnp.float32)


def feed_forward(normed_rows, fc_full, fcb_full, proj_full, grad_in):
    pre_activation = jnp.einsum(
        "scd,df->scf", normed_rows, fc_full, preferred_element_type=jnp.float32
    ) + fcb_full.astype(jnp.float32)
    active_rows = gelu_tanh(pre_activation).astype(jnp.bfloat16)
    branch_part = jnp.einsum(
        "scf,fd->scd", active_rows, proj_full, preferred_element_type=jnp.float32
    )
    act_grad = jnp.einsum("scd,fd->scf", grad_in, proj_full, preferred_element_type=jnp.float32)
    pre_grad = jax.vjp(gelu_tanh, pre_activation)[1](act_grad)[0].astype(jnp.bfloat16)
    proj_grad = jnp.einsum("scf,scd->fd", active_rows, grad_in, preferred_element_type=jnp.float32)
    fc_grad = jnp.einsum("scd,scf->df", normed_rows, pre_grad, preferred_element_type=jnp.float32)
    fcb_grad = jnp.sum(pre_grad, axis=(0, 1), dtype=jnp.float32)
    normed_grad = jnp.einsum("scf,df->scd", pre_grad, fc_full, preferred_element_type=jnp.float32)
    return (branch_part, normed_grad, fc_grad, fcb_grad, proj_grad)


def shards_plain(
    tokens,
    gain_one,
    shift_one,
    query_key_value_weight,
    qv_bias,
    attention_out_weight,
    attention_out_bias,
    gain_two,
    shift_two,
    expand_weight,
    expand_bias,
    contract_weight,
    contract_bias,
    doc_ids,
    out_grad,
):
    score_scale = HEAD_DIM ** (-0.5)
    seq_count = tokens.shape[0]
    span_rows = doc_ids.shape[1]
    heads_here = query_key_value_weight.shape[1]
    full_length = span_rows * lax.axis_size("ctx")
    first_query = lax.axis_index("ctx") * span_rows
    query_pos = first_query + jnp.arange(span_rows, dtype=jnp.int32)
    last_query = first_query + span_rows - 1
    all_ids = lax.all_gather(doc_ids, "ctx", axis=1, tiled=True)

    def allowed_mask(offset, block_width):
        key_pos = offset + jnp.arange(block_width, dtype=jnp.int32)
        key_ids = lax.dynamic_slice_in_dim(all_ids, offset, block_width, 1)
        causal = key_pos[None, :] <= query_pos[:, None]
        same_doc = doc_ids[:, :, None] == key_ids[:, None, :]
        return jnp.logical_and(causal[None], same_doc)[:, None]

    def keep_state(carry_state):
        return carry_state

    gain_first = gain_one.astype(jnp.float32)
    shift_first = shift_one.astype(jnp.float32)
    gain_second = gain_two.astype(jnp.float32)
    shift_second = shift_two.astype(jnp.float32)
    inputs = tokens.astype(jnp.float32)
    first_normed = layer_norm(inputs, gain_first, shift_first)
    rows_one = gather_attn(first_normed.astype(jnp.bfloat16))
    packed_values = jnp.einsum(
        "scd,dhe->sche", rows_one, query_key_value_weight, preferred_element_type=jnp.float32
    )
    bias_pair = qv_bias.astype(jnp.float32)
    queries = (packed_values[..., :HEAD_DIM] + bias_pair[:, :HEAD_DIM]).astype(jnp.bfloat16)
    keys_here = packed_values[..., HEAD_DIM : 2 * HEAD_DIM].astype(jnp.bfloat16)
    values_here = (packed_values[..., 2 * HEAD_DIM :] + bias_pair[:, HEAD_DIM:]).astype(
        jnp.bfloat16
    )
    key_value = jnp.concatenate([keys_here, values_here], axis=-1)
    start_state = (
        jnp.full((seq_count, heads_here, span_rows), neg_fill, jnp.float32),
        jnp.zeros((seq_count, heads_here, span_rows), jnp.float32),
        jnp.zeros((seq_count, heads_here, span_rows, HEAD_DIM), jnp.float32),
    )
    folded = start_state
    piece_rows = lax.all_gather(key_value, "ctx", axis=1, tiled=True)
    piece_len = piece_rows.shape[1]
    block_width = min(piece_len, span_rows)

    def attend_block(carry_state, block_index):
        offset = block_index * block_width

        def attend_compute(inner_state):
            row_best, row_total, weighted = inner_state
            one_block = lax.dynamic_slice_in_dim(
                piece_rows, block_index * block_width, block_width, 1
            )
            scores = (
                jnp.einsum(
                    "sqhe,skhe->shqk",
                    queries,
                    one_block[..., :HEAD_DIM],
                    preferred_element_type=jnp.float32,
                )
                * score_scale
            )
            allowed = allowed_mask(offset, block_width)
            row_top = jnp.max(jnp.where(allowed, scores, neg_fill), axis=-1)
            new_best = jnp.maximum(row_best, row_top)
            soft_terms = jnp.where(allowed, jnp.exp(scores - new_best[..., None]), 0.0)
            rescale = jnp.exp(row_best - new_best)
            row_total = row_total * rescale + jnp.sum(soft_terms, axis=-1)
            weighted = weighted * rescale[..., None] + jnp.einsum(
                "shqk,skhe->shqe",
                soft_terms.astype(jnp.bfloat16),
                one_block[..., HEAD_DIM:],
                preferred_element_type=jnp.float32,
            )
            return (new_best, row_total, weighted)

        return (lax.cond(offset <= last_query, attend_compute, keep_state, carry_state), None)

    folded, _ = lax.scan(
        attend_block, folded, jnp.arange(piece_len // block_width, dtype=jnp.int32)
    )
    row_best, row_total, weighted = folded
    mixed_exact = weighted / row_total[..., None]
    log_total = row_best + jnp.log(row_total)
    mixed_low = jnp.transpose(mixed_exact, (0, 2, 1, 3)).astype(jnp.bfloat16)
    attn_part = jnp.einsum(
        "sche,hed->scd", mixed_low, attention_out_weight, preferred_element_type=jnp.float32
    )
    residual_one = inputs + reduce_attn(attn_part) + attention_out_bias.astype(jnp.float32)
    second_normed = layer_norm(residual_one, gain_second, shift_second)
    normed_low = second_normed.astype(jnp.bfloat16)
    grad_rows = out_grad.astype(jnp.float32)
    grad_low = grad_rows.astype(jnp.bfloat16)
    rows_two = gather_mlp(normed_low)
    grad_gathered = gather_mlp(grad_low)
    branch_part, normed_grad, fc_grad, fcb_grad, proj_grad = feed_forward(
        rows_two, expand_weight, expand_bias, contract_weight, grad_gathered
    )
    feedforward_branch = reduce_mlp(branch_part)
    dnormed_two = reduce_mlp(normed_grad)
    layer_out = (residual_one + feedforward_branch + contract_bias.astype(jnp.float32)).astype(
        jnp.bfloat16
    )
    pull_two = jax.vjp(layer_norm, residual_one, gain_second, shift_second)[1]
    res_extra, gain_two_grad, shift_two_grad = pull_two(dnormed_two)
    grad_res = grad_rows + res_extra
    attn_grad_rows = gather_attn(grad_res.astype(jnp.bfloat16))
    dmixed = jnp.einsum(
        "scd,hed->sche", attn_grad_rows, attention_out_weight, preferred_element_type=jnp.float32
    ).astype(jnp.bfloat16)
    outw_grad = jnp.einsum(
        "sche,scd->hed", mixed_low, attn_grad_rows, preferred_element_type=jnp.float32
    )
    dmixed_heads = jnp.transpose(dmixed, (0, 2, 1, 3))
    row_delta = jnp.sum(dmixed_heads.astype(jnp.float32) * mixed_exact, axis=-1)
    back_start = (
        jnp.zeros((seq_count, heads_here, span_rows, HEAD_DIM), jnp.float32),
        jnp.zeros((seq_count, full_length, heads_here, 2 * HEAD_DIM), jnp.float32),
    )
    folded = back_start
    back_piece_rows = lax.all_gather(key_value, "ctx", axis=1, tiled=True)
    piece_len = back_piece_rows.shape[1]
    back_block_width = min(piece_len, span_rows)

    def back_block(carry_state, block_index):
        offset = block_index * back_block_width

        def back_compute(inner_state):
            query_grad, pair_grads = inner_state
            one_block = lax.dynamic_slice_in_dim(
                back_piece_rows, block_index * back_block_width, back_block_width, 1
            )
            keys_block = one_block[..., :HEAD_DIM]
            values_block = one_block[..., HEAD_DIM:]
            scores = (
                jnp.einsum(
                    "sqhe,skhe->shqk", queries, keys_block, preferred_element_type=jnp.float32
                )
                * score_scale
            )
            allowed = allowed_mask(offset, back_block_width)
            soft_terms = jnp.where(allowed, jnp.exp(scores - log_total[..., None]), 0.0)
            soft_grad = jnp.einsum(
                "shqe,skhe->shqk", dmixed_heads, values_block, preferred_element_type=jnp.float32
            )
            score_grad = (soft_terms * (soft_grad - row_delta[..., None])).astype(jnp.bfloat16)
            query_grad = query_grad + score_scale * jnp.einsum(
                "shqk,skhe->shqe", score_grad, keys_block, preferred_element_type=jnp.float32
            )
            key_grad = score_scale * jnp.einsum(
                "shqk,sqhe->skhe", score_grad, queries, preferred_element_type=jnp.float32
            )
            value_grad = jnp.einsum(
                "shqk,shqe->skhe",
                soft_terms.astype(jnp.bfloat16),
                dmixed_heads,
                preferred_element_type=jnp.float32,
            )
            earlier = lax.dynamic_slice_in_dim(pair_grads, offset, back_block_width, 1)
            pair_grads = lax.dynamic_update_slice_in_dim(
                pair_grads, earlier + jnp.concatenate([key_grad, value_grad], axis=-1), offset, 1
            )
            return (query_grad, pair_grads)

        return (lax.cond(offset <= last_query, back_compute, keep_state, carry_state), None)

    folded, _ = lax.scan(
        back_block, folded, jnp.arange(piece_len // back_block_width, dtype=jnp.int32)
    )
    query_grad, pair_grads = folded
    pair_mine = lax.psum_scatter(
        pair_grads.astype(jnp.bfloat16), "ctx", scatter_dimension=1, tiled=True
    )
    query_low = jnp.transpose(query_grad, (0, 2, 1, 3)).astype(jnp.bfloat16)
    packed_grad = jnp.concatenate([query_low, pair_mine], axis=-1)
    qkv_grad = jnp.einsum(
        "scd,sche->dhe", rows_one, packed_grad, preferred_element_type=jnp.float32
    )
    qvb_grad = jnp.concatenate(
        [
            jnp.sum(query_low, axis=(0, 1), dtype=jnp.float32),
            jnp.sum(pair_mine[..., HEAD_DIM:], axis=(0, 1), dtype=jnp.float32),
        ],
        axis=-1,
    )
    normed_one_grad = reduce_attn(
        jnp.einsum(
            "sche,dhe->scd", packed_grad, query_key_value_weight, preferred_element_type=jnp.float32
        )
    )
    pull_one = jax.vjp(layer_norm, inputs, gain_first, shift_first)[1]
    input_extra, gain_one_grad, shift_one_grad = pull_one(normed_one_grad)
    grad_tokens = grad_res + input_extra
    small_sums = lax.psum(
        (
            gain_one_grad,
            shift_one_grad,
            jnp.sum(grad_res, axis=(0, 1)),
            gain_two_grad,
            shift_two_grad,
            jnp.sum(grad_rows, axis=(0, 1)),
        ),
        ("ctx", "tp"),
    )
    qkv_grad, qvb_grad, outw_grad, fc_grad, fcb_grad, proj_grad = (
        lax.psum(qkv_grad.astype(jnp.bfloat16), "ctx").astype(jnp.float32),
        lax.psum(qvb_grad.astype(jnp.bfloat16), "ctx").astype(jnp.float32),
        lax.psum(outw_grad.astype(jnp.bfloat16), "ctx").astype(jnp.float32),
        lax.psum(fc_grad.astype(jnp.bfloat16), "ctx").astype(jnp.float32),
        lax.psum(fcb_grad.astype(jnp.bfloat16), "ctx").astype(jnp.float32),
        lax.psum(proj_grad.astype(jnp.bfloat16), "ctx").astype(jnp.float32),
    )
    return (
        layer_out,
        grad_tokens,
        small_sums[0],
        small_sums[1],
        qkv_grad,
        qvb_grad,
        outw_grad,
        small_sums[2],
        small_sums[3],
        small_sums[4],
        fc_grad,
        fcb_grad,
        proj_grad,
        small_sums[5],
    )


bf16 = jnp.bfloat16
f32 = jnp.float32
BLK = 512
PAIR = 2 * HEAD_DIM
DOC_FAR = -(2.0**100)
CAUSAL_FAR = -2e30

TP_CORE = [(i, i ^ 1) for i in range(4)]
TP_ROW = [(i, i ^ 2) for i in range(4)]
CTX_X = [(i, i ^ 1) for i in range(8)]
CTX_Z1 = [(i, i ^ 2) for i in range(8)]
CTX_Z2 = [(i, i ^ 4) for i in range(8)]
CTX_PLANES = [[0, 2, 4, 6], [1, 3, 5, 7]]


def after(values, earlier):
    return lax.optimization_barrier((values, earlier))[0]


def contract(a, b, dims):
    return lax.dot_general(a, b, (dims, ((), ())), preferred_element_type=f32)


def lane_half(rows, head):
    lanes = lax.broadcasted_iota(jnp.int32, (rows, PAIR), 1)
    return (lanes >= HEAD_DIM) if head else (lanes < HEAD_DIM)


def attend_kernel(
    first_ref, mine_ref, other_ref, qdoc_ref, kdoc_ref, bias_ref,
    out_mine_ref, out_other_ref, exact_ref, log_ref, key_ref, value_ref, best_ref, total_ref, acc_ref,
):
    i = pl.program_id(0)
    half = BLK // 2
    rows = pl.ds(pl.multiple_of(i * half, half), half)
    block = pl.ds(pl.multiple_of(i * BLK, BLK), BLK)
    packed = jnp.concatenate([mine_ref[rows, :], other_ref[rows, :]], axis=0)
    queries = packed[:, :PAIR] * jnp.asarray(HEAD_DIM**-0.5, bf16)
    key_ref[block, :PAIR] = packed[:, PAIR : 2 * PAIR]
    key_ref[block, PAIR:] = kdoc_ref[block, :]
    value_ref[block, :] = packed[:, 2 * PAIR :]
    qdoc = qdoc_ref[block, :]
    query_heads = [
        jnp.concatenate([jnp.where(lane_half(BLK, h), queries, jnp.zeros_like(queries)), qdoc], axis=1)
        for h in range(2)
    ]
    best_ref[...] = jnp.full_like(best_ref, neg_fill)
    total_ref[...] = jnp.zeros_like(total_ref)
    acc_ref[...] = jnp.zeros_like(acc_ref)

    def visit(j, bias):
        keys = pl.ds(pl.multiple_of(j * BLK, BLK), BLK)
        key_block = key_ref[keys, :]
        value_block = value_ref[keys, :]
        for h in range(2):
            scores = contract(key_block, query_heads[h], ((1,), (1,)))
            if bias is not None:
                scores = scores + bias
            old = best_ref[h : h + 1, :]
            new = jnp.maximum(old, jnp.max(scores, axis=0, keepdims=True))
            weights = jnp.exp(scores - new)
            fade = jnp.exp(old - new)
            total_ref[h : h + 1, :] = total_ref[h : h + 1, :] * fade + jnp.sum(
                weights, axis=0, keepdims=True
            )
            product = contract(value_block, weights.astype(bf16), ((0,), (0,)))
            part = slice(h * HEAD_DIM, (h + 1) * HEAD_DIM)
            acc_ref[part, :] = acc_ref[part, :] * fade + product[part, :]
            best_ref[h : h + 1, :] = new

    def step(j, carry):
        visit(j, None)
        return carry

    lax.fori_loop(first_ref[i], i, step, 0)
    visit(i, bias_ref[...])
    for h in range(2):
        part = slice(h * HEAD_DIM, (h + 1) * HEAD_DIM)
        acc_ref[part, :] = acc_ref[part, :] / total_ref[h : h + 1, :]
        log_ref[h : h + 1, block] = best_ref[h : h + 1, :] + jnp.log(total_ref[h : h + 1, :])
    mixed = acc_ref[...]
    exact_ref[:, block] = mixed
    low = jnp.transpose(mixed).astype(bf16)
    out_mine_ref[rows, :] = low[:half]
    out_other_ref[rows, :] = low[half:]


def attend_back_kernel(
    first_ref, mine_ref, other_ref, qdoc_ref, kdoc_ref, bias_ref, exact_ref, log_ref, dmine_ref, dother_ref,
    out_mine_ref, out_other_ref, key_ref, value_ref, dkey_ref, dvalue_ref, dquery_ref,
):
    i = pl.program_id(0)
    half = BLK // 2
    rows = pl.ds(pl.multiple_of(i * half, half), half)
    block = pl.ds(pl.multiple_of(i * BLK, BLK), BLK)
    packed = jnp.concatenate([mine_ref[rows, :], other_ref[rows, :]], axis=0)
    scale = HEAD_DIM**-0.5
    queries = packed[:, :PAIR] * jnp.asarray(scale, bf16)
    key_ref[block, :PAIR] = packed[:, PAIR : 2 * PAIR]
    key_ref[block, PAIR:] = kdoc_ref[block, :]
    value_ref[block, :] = packed[:, 2 * PAIR :]
    dkey_ref[block, :] = jnp.zeros((BLK, PAIR), f32)
    dvalue_ref[block, :] = jnp.zeros((BLK, PAIR), f32)
    dquery_ref[...] = jnp.zeros_like(dquery_ref)
    dmixed = jnp.concatenate([dmine_ref[rows, :], dother_ref[rows, :]], axis=0)
    qdoc = qdoc_ref[block, :]
    masked = [jnp.where(lane_half(BLK, h), queries, jnp.zeros_like(queries)) for h in range(2)]
    dmasked = [jnp.where(lane_half(BLK, h), dmixed, jnp.zeros_like(dmixed)) for h in range(2)]
    query_heads = [jnp.concatenate([masked[h], qdoc], axis=1) for h in range(2)]
    product = jnp.transpose(dmixed.astype(f32)) * exact_ref[:, block]
    deltas = [
        jnp.sum(product[h * HEAD_DIM : (h + 1) * HEAD_DIM, :], axis=0, keepdims=True) for h in range(2)
    ]
    logs = [log_ref[h : h + 1, block] for h in range(2)]

    def visit(j, bias):
        keys = pl.ds(pl.multiple_of(j * BLK, BLK), BLK)
        key_block = key_ref[keys, :]
        value_block = value_ref[keys, :]
        dkey = dkey_ref[keys, :]
        dvalue = dvalue_ref[keys, :]
        for h in range(2):
            scores = contract(key_block, query_heads[h], ((1,), (1,)))
            if bias is not None:
                scores = scores + bias
            weights = jnp.exp(scores - logs[h])
            dweights = contract(value_block, dmasked[h], ((1,), (1,)))
            dscores = (weights * (dweights - deltas[h])).astype(bf16)
            dvalue = dvalue + contract(weights.astype(bf16), dmasked[h], ((1,), (0,)))
            dkey = dkey + contract(dscores, masked[h], ((1,), (0,)))
            part = slice(h * HEAD_DIM, (h + 1) * HEAD_DIM)
            turned = contract(key_block[:, :PAIR], dscores, ((0,), (0,)))
            dquery_ref[part, :] = dquery_ref[part, :] + turned[part, :]
        dkey_ref[keys, :] = dkey
        dvalue_ref[keys, :] = dvalue

    def step(j, carry):
        visit(j, None)
        return carry

    lax.fori_loop(first_ref[i], i, step, 0)
    visit(i, bias_ref[...])
    dquery = jnp.transpose(dquery_ref[...] * scale).astype(bf16)
    out_mine_ref[rows, :PAIR] = dquery[:half]
    out_other_ref[rows, :PAIR] = dquery[half:]

    @pl.when(i == pl.num_programs(0) - 1)
    def _():
        for b in range(4):
            for side, out in ((0, out_mine_ref), (1, out_other_ref)):
                source = slice(b * BLK + side * half, b * BLK + (side + 1) * half)
                target = slice(b * half, (b + 1) * half)
                out[target, PAIR : 2 * PAIR] = dkey_ref[source, :].astype(bf16)
                out[target, 2 * PAIR :] = dvalue_ref[source, :].astype(bf16)


def whole(shape):
    return pl.BlockSpec(shape, lambda i: (0,) * len(shape))


def attend(first, mine, other, qdoc, kdoc, bias):
    length = qdoc.shape[0]
    half = length // 2
    return pl.pallas_call(
        attend_kernel,
        grid=(length // BLK,),
        in_specs=[
            pl.BlockSpec(memory_space=pltpu.SMEM),
            whole(mine.shape), whole(other.shape), whole(qdoc.shape), whole(kdoc.shape), whole(bias.shape),
        ],
        out_specs=[whole((half, PAIR)), whole((half, PAIR)), whole((PAIR, length)), whole((2, length))],
        out_shape=[
            jax.ShapeDtypeStruct((half, PAIR), bf16),
            jax.ShapeDtypeStruct((half, PAIR), bf16),
            jax.ShapeDtypeStruct((PAIR, length), f32),
            jax.ShapeDtypeStruct((2, length), f32),
        ],
        scratch_shapes=[
            pltpu.VMEM((length, 2 * PAIR), bf16),
            pltpu.VMEM((length, PAIR), bf16),
            pltpu.VMEM((2, BLK), f32),
            pltpu.VMEM((2, BLK), f32),
            pltpu.VMEM((PAIR, BLK), f32),
        ],
        compiler_params=pltpu.CompilerParams(
            dimension_semantics=("arbitrary",), vmem_limit_bytes=40 << 20
        ),
        name="attend",
    )(first, mine, other, qdoc, kdoc, bias)


def attend_back(first, mine, other, qdoc, kdoc, bias, exact, log_total, dmine, dother):
    length = qdoc.shape[0]
    half = length // 2
    operands = (mine, other, qdoc, kdoc, bias, exact, log_total, dmine, dother)
    return pl.pallas_call(
        attend_back_kernel,
        grid=(length // BLK,),
        in_specs=[pl.BlockSpec(memory_space=pltpu.SMEM)] + [whole(o.shape) for o in operands],
        out_specs=[whole((half, 3 * PAIR)), whole((half, 3 * PAIR))],
        out_shape=[jax.ShapeDtypeStruct((half, 3 * PAIR), bf16)] * 2,
        scratch_shapes=[
            pltpu.VMEM((length, 2 * PAIR), bf16),
            pltpu.VMEM((length, PAIR), bf16),
            pltpu.VMEM((length, PAIR), f32),
            pltpu.VMEM((length, PAIR), f32),
            pltpu.VMEM((PAIR, BLK), f32),
        ],
        compiler_params=pltpu.CompilerParams(
            dimension_semantics=("arbitrary",), vmem_limit_bytes=48 << 20
        ),
        name="attend_back",
    )(first, *operands)


def planes_swap(values):
    return lax.all_to_all(values, "ctx", 0, 0, axis_index_groups=CTX_PLANES, tiled=False)


def tp_gather(values):
    core = lax.ppermute(values, "tp", TP_CORE)
    row = lax.ppermute(values, "tp", TP_ROW)
    both = lax.ppermute(row, "tp", TP_CORE)
    return [values, core, row, both]


def tp_gather_rows(values):
    return jnp.stack(tp_gather(values), axis=1)


def tp_scatter_rows(make_part):
    away = jnp.stack([make_part(3), make_part(1)]).astype(bf16)
    came = lax.ppermute(away, "tp", TP_CORE)
    across = (make_part(2) + came[0].astype(f32)).astype(bf16)
    arrived = lax.ppermute(across, "tp", TP_ROW)
    return make_part(0) + came[1].astype(f32) + arrived.astype(f32)


def tp_swap(pieces):
    return [
        pieces[0],
        lax.ppermute(pieces[1], "tp", TP_CORE),
        lax.ppermute(pieces[2], "tp", TP_ROW),
        lax.ppermute(pieces[3], "tp", [(i, i ^ 3) for i in range(4)]),
    ]


def sum_ctx(values):
    for perm in (CTX_X, CTX_Z1, CTX_Z2):
        values = values + lax.ppermute(values, "ctx", perm)
    return values


def sum_all(values):
    for perm in (TP_CORE, TP_ROW):
        values = values + lax.ppermute(values, "tp", perm)
    return sum_ctx(values)


def norm_stats(values):
    centred = values - jnp.mean(values, axis=-1, keepdims=True)
    rate = lax.rsqrt(jnp.mean(centred * centred, axis=-1, keepdims=True) + eps)
    return centred * rate, rate


def norm_back(hat, rate, gain, grad):
    dhat = grad * gain
    return rate * (
        dhat
        - jnp.mean(dhat, axis=-1, keepdims=True)
        - hat * jnp.mean(dhat * hat, axis=-1, keepdims=True)
    )


def order_pair(values, swapped, axis):
    first, second = jnp.split(values, 2, axis=axis)
    return jnp.where(
        swapped,
        jnp.concatenate([second, first], axis=axis),
        jnp.concatenate([first, second], axis=axis),
    )


def shards(
    tokens,
    gain_one,
    shift_one,
    query_key_value_weight,
    qv_bias,
    attention_out_weight,
    attention_out_bias,
    gain_two,
    shift_two,
    expand_weight,
    expand_bias,
    contract_weight,
    contract_bias,
    doc_ids,
    out_grad,
):
    width = tokens.shape[2]
    span = doc_ids.shape[1]
    piece = tokens.shape[1]
    planes = tokens.shape[0]
    here = planes * piece
    group = here * 4
    ctx_at = lax.axis_index("ctx")
    tp_at = lax.axis_index("tp")
    side = ctx_at % 2
    swapped = side == 1
    gain_first, shift_first = gain_one.astype(f32), shift_one.astype(f32)
    gain_second, shift_second = gain_two.astype(f32), shift_two.astype(f32)

    inputs = planes_swap(tokens).astype(f32)

    qkv_heads = query_key_value_weight.reshape(width, 4, 3, HEAD_DIM)
    qkv_heads = order_pair(qkv_heads, swapped, 1)
    qkv_rel = jnp.transpose(qkv_heads.reshape(width, 2, 2, 3, HEAD_DIM), (0, 1, 3, 2, 4)).reshape(
        width, 2, 3 * PAIR
    )
    bias_pairs = order_pair(qv_bias.astype(f32), swapped, 0).reshape(2, 2, 2, HEAD_DIM)
    bias_rel = jnp.concatenate(
        [
            bias_pairs[:, :, 0].reshape(2, PAIR),
            jnp.zeros((2, PAIR), f32),
            bias_pairs[:, :, 1].reshape(2, PAIR),
        ],
        axis=1,
    )
    out_rel = order_pair(attention_out_weight.reshape(4 * HEAD_DIM, width), swapped, 0)
    out_full = jnp.concatenate(tp_gather(out_rel), axis=0)

    ids = lax.all_to_all(doc_ids, "ctx", 0, 0, axis_index_groups=CTX_PLANES, tiled=False)
    ids = jnp.stack([ids, lax.ppermute(ids, "ctx", CTX_X)], axis=1).reshape(planes, 2, 2, 2, piece)
    ids = jnp.where(tp_at % 2 == 1, jnp.flip(ids, 3), ids)
    ids = jnp.where(tp_at // 2 == 1, jnp.flip(ids, 2), ids).reshape(planes, 2 * span)
    low_id, high_id = jnp.min(ids, axis=1), jnp.max(ids, axis=1)
    first_block = jnp.sum((high_id[None, :] < low_id[:, None]).astype(jnp.int32), axis=1)
    lanes = jnp.arange(PAIR, dtype=jnp.int32)
    same = ids.reshape(-1, 1) == lanes[None, :]
    kdoc = same.astype(bf16)
    qdoc = jnp.where(same, 0.0, DOC_FAR).astype(bf16)
    place = (
        ((side ^ jnp.arange(2, dtype=jnp.int32)) * span)[:, None, None]
        + ((tp_at ^ jnp.arange(4, dtype=jnp.int32)) * piece)[None, :, None]
        + jnp.arange(piece, dtype=jnp.int32)[None, None, :]
    ).reshape(-1)
    bias = jnp.where(place[:, None] <= place[None, :], 0.0, CAUSAL_FAR).astype(f32)

    hat_one, rate_one = norm_stats(inputs)
    rows_one = tp_gather_rows((hat_one * gain_first + shift_first).astype(bf16)).reshape(group, width)

    def project(j):
        return (
            jnp.dot(rows_one, qkv_rel[:, j], preferred_element_type=f32) + bias_rel[j]
        ).astype(bf16)

    qkv_other = lax.ppermute(project(1), "ctx", CTX_X)
    qkv_mine = project(0)

    grad_rows = planes_swap(after(out_grad, qkv_mine))
    grad_gathered = tp_gather_rows(grad_rows).reshape(group, width)
    grad_rows = grad_rows.astype(f32)
    act_grad = contract(grad_gathered, contract_weight, ((1,), (1,)))

    mixed_mine, mixed_other, exact, log_total = attend(
        first_block, qkv_mine, qkv_other, qdoc, kdoc, bias
    )
    mixed_heads = jnp.concatenate([mixed_mine, lax.ppermute(mixed_other, "ctx", CTX_X)], axis=1)
    by_tp = mixed_heads.reshape(planes, 4, piece, 2 * PAIR)
    mixed_rows = jnp.concatenate(tp_swap([by_tp[:, k] for k in range(4)]), axis=-1)
    attn_branch = jnp.dot(
        mixed_rows.reshape(here, width), out_full, preferred_element_type=f32
    ).reshape(planes, piece, width)
    residual_one = inputs + attn_branch + attention_out_bias.astype(f32)

    hat_two, rate_two = norm_stats(residual_one)
    rows_two = tp_gather_rows((hat_two * gain_second + shift_second).astype(bf16)).reshape(group, width)
    pre_act = jnp.dot(rows_two, expand_weight, preferred_element_type=f32) + expand_bias.astype(f32)
    active, pull_gelu = jax.vjp(gelu_tanh, pre_act)
    active = active.astype(bf16)
    dpre = pull_gelu(act_grad)[0].astype(bf16)
    dpre_parts = dpre.reshape(planes, 4, piece, -1)
    dnormed_two = tp_scatter_rows(
        lambda k: contract(
            dpre_parts[:, k].reshape(here, -1), expand_weight, ((1,), (1,))
        ).reshape(planes, piece, width)
    )
    fc_grad = contract(rows_two, dpre, ((0,), (0,)))
    proj_grad = contract(active, grad_gathered, ((0,), (0,)))
    fcb_grad = jnp.sum(dpre, axis=0, dtype=f32)
    fc_grad, proj_grad = lax.psum((fc_grad.astype(bf16), proj_grad.astype(bf16)), "ctx")

    grad_res = grad_rows + norm_back(hat_two, rate_two, gain_second, dnormed_two)
    attn_grad = grad_res.astype(bf16)
    dmixed = contract(attn_grad.reshape(here, width), out_full, ((1,), (1,))).astype(bf16)
    dmixed = dmixed.reshape(planes, piece, 4, 2 * PAIR)
    dmixed = jnp.stack(tp_swap([dmixed[:, :, k] for k in range(4)]), axis=1).reshape(group, 2 * PAIR)
    dmixed_other = lax.ppermute(dmixed[:, PAIR:], "ctx", CTX_X)
    grad_mine, grad_other = attend_back(
        first_block, qkv_mine, qkv_other, qdoc, kdoc, bias, exact, log_total, dmixed[:, :PAIR], dmixed_other
    )
    packed_grad = jnp.concatenate([grad_mine, lax.ppermute(grad_other, "ctx", CTX_X)], axis=1)

    branch_in = after(active, dmixed_other).reshape(planes, 4, piece, -1)
    feedforward_branch = tp_scatter_rows(
        lambda k: jnp.dot(
            branch_in[:, k].reshape(here, -1), contract_weight, preferred_element_type=f32
        ).reshape(planes, piece, width)
    )
    layer_out = planes_swap(
        (residual_one + feedforward_branch + contract_bias.astype(f32)).astype(bf16)
    )

    attn_grad_rows = tp_gather_rows(after(attn_grad, dmixed_other)).reshape(group, width)
    outw_grad = contract(mixed_heads, attn_grad_rows, ((0,), (0,)))
    outw_grad = order_pair(outw_grad.astype(bf16), swapped, 0)

    qkv_flat = qkv_rel.reshape(width, 6 * PAIR)
    packed_parts = packed_grad.reshape(planes, 4, piece, 6 * PAIR)
    dnormed_one = tp_scatter_rows(
        lambda k: contract(
            packed_parts[:, k].reshape(here, -1), qkv_flat, ((1,), (1,))
        ).reshape(planes, piece, width)
    )
    qkv_grad = contract(rows_one, packed_grad, ((0,), (0,))).astype(bf16)
    qkv_grad, outw_grad = lax.psum((qkv_grad_order(qkv_grad, swapped), outw_grad), "ctx")
    bias_sums = jnp.sum(packed_grad, axis=0, dtype=f32)[None]
    bias_sums = qkv_grad_order(bias_sums, swapped).reshape(4, 3, HEAD_DIM)
    qvb_grad = jnp.concatenate([bias_sums[:, 0], bias_sums[:, 2]], axis=-1)

    grad_tokens = grad_res + norm_back(hat_one, rate_one, gain_first, dnormed_one)
    grad_tokens = planes_swap(grad_tokens.astype(bf16)).astype(f32)

    early = sum_all(
        jnp.stack(
            [
                jnp.sum(grad_res, axis=(0, 1)),
                jnp.sum(dnormed_two * hat_two, axis=(0, 1)),
                jnp.sum(dnormed_two, axis=(0, 1)),
                jnp.sum(grad_rows, axis=(0, 1)),
            ]
        )
    )
    late = sum_all(
        jnp.stack([jnp.sum(dnormed_one * hat_one, axis=(0, 1)), jnp.sum(dnormed_one, axis=(0, 1))])
    )
    fcb_grad = sum_ctx(fcb_grad)
    qvb_grad = sum_ctx(qvb_grad)
    return (
        layer_out,
        grad_tokens,
        late[0],
        late[1],
        qkv_grad.astype(f32),
        qvb_grad,
        outw_grad.astype(f32).reshape(4, HEAD_DIM, width),
        early[0],
        early[1],
        early[2],
        fc_grad.astype(f32),
        fcb_grad,
        proj_grad.astype(f32),
        early[3],
    )


def qkv_grad_order(values, swapped):
    rows = values.shape[0]
    values = jnp.transpose(values.reshape(rows, 2, 3, 2, HEAD_DIM), (0, 1, 3, 2, 4))
    return order_pair(values, swapped, 1).reshape(rows, 4, 3 * HEAD_DIM)


def solution(mesh):
    sizes = dict(zip(mesh.axis_names, mesh.devices.shape))
    body = shards if (sizes["ctx"], sizes["tp"]) == (8, 4) else shards_plain
    return jax.shard_map(
        body,
        mesh=mesh,
        in_specs=(
            P(None, ("ctx", "tp"), None),
            P(),
            P(),
            P(None, "tp", None),
            P("tp", None),
            P("tp", None, None),
            P(),
            P(),
            P(),
            P(None, "tp"),
            P("tp"),
            P("tp", None),
            P(),
            P(None, "ctx"),
            P(None, ("ctx", "tp"), None),
        ),
        out_specs=(
            P(None, ("ctx", "tp"), None),
            P(None, ("ctx", "tp"), None),
            P(),
            P(),
            P(None, "tp", None),
            P("tp", None),
            P("tp", None, None),
            P(),
            P(),
            P(),
            P(None, "tp"),
            P("tp"),
            P("tp", None),
            P(),
        ),
        check_vma=False,
    )
```

```python
import jax
import jax.numpy as jnp
from jax import lax
from jax.experimental import pallas as pl
from jax.experimental.pallas import tpu as pltpu
from jax.sharding import PartitionSpec as P

HEAD_DIM = 64


eps = 1e-05
neg_fill = -1e30


def layer_norm(values, gain, shift):
    centre = jnp.mean(values, axis=-1, keepdims=True)
    centred = values - centre
    spread = jnp.mean(centred * centred, axis=-1, keepdims=True)
    return centred * lax.rsqrt(spread + eps) * gain + shift


def gelu_tanh(values):
    return jax.nn.gelu(values, approximate=True)


def gather_attn(values):
    return lax.all_gather(values, "tp", axis=1, tiled=True)


def reduce_attn(values):
    return lax.psum_scatter(
        values.astype(jnp.bfloat16), "tp", scatter_dimension=1, tiled=True
    ).astype(jnp.float32)


def gather_mlp(values):
    return lax.all_gather(values, "tp", axis=1, tiled=True)


def reduce_mlp(values):
    return lax.psum_scatter(
        values.astype(jnp.bfloat16), "tp", scatter_dimension=1, tiled=True
    ).astype(jnp.float32)


def feed_forward(normed_rows, fc_full, fcb_full, proj_full, grad_in):
    pre_activation = jnp.einsum(
        "scd,df->scf", normed_rows, fc_full, preferred_element_type=jnp.float32
    ) + fcb_full.astype(jnp.float32)
    active_rows = gelu_tanh(pre_activation).astype(jnp.bfloat16)
    branch_part = jnp.einsum(
        "scf,fd->scd", active_rows, proj_full, preferred_element_type=jnp.float32
    )
    act_grad = jnp.einsum("scd,fd->scf", grad_in, proj_full, preferred_element_type=jnp.float32)
    pre_grad = jax.vjp(gelu_tanh, pre_activation)[1](act_grad)[0].astype(jnp.bfloat16)
    proj_grad = jnp.einsum("scf,scd->fd", active_rows, grad_in, preferred_element_type=jnp.float32)
    fc_grad = jnp.einsum("scd,scf->df", normed_rows, pre_grad, preferred_element_type=jnp.float32)
    fcb_grad = jnp.sum(pre_grad, axis=(0, 1), dtype=jnp.float32)
    normed_grad = jnp.einsum("scf,df->scd", pre_grad, fc_full, preferred_element_type=jnp.float32)
    return (branch_part, normed_grad, fc_grad, fcb_grad, proj_grad)


def shards_plain(
    tokens,
    gain_one,
    shift_one,
    query_key_value_weight,
    qv_bias,
    attention_out_weight,
    attention_out_bias,
    gain_two,
    shift_two,
    expand_weight,
    expand_bias,
    contract_weight,
    contract_bias,
    doc_ids,
    out_grad,
):
    score_scale = HEAD_DIM ** (-0.5)
    seq_count = tokens.shape[0]
    span_rows = doc_ids.shape[1]
    heads_here = query_key_value_weight.shape[1]
    full_length = span_rows * lax.axis_size("ctx")
    first_query = lax.axis_index("ctx") * span_rows
    query_pos = first_query + jnp.arange(span_rows, dtype=jnp.int32)
    last_query = first_query + span_rows - 1
    all_ids = lax.all_gather(doc_ids, "ctx", axis=1, tiled=True)

    def allowed_mask(offset, block_width):
        key_pos = offset + jnp.arange(block_width, dtype=jnp.int32)
        key_ids = lax.dynamic_slice_in_dim(all_ids, offset, block_width, 1)
        causal = key_pos[None, :] <= query_pos[:, None]
        same_doc = doc_ids[:, :, None] == key_ids[:, None, :]
        return jnp.logical_and(causal[None], same_doc)[:, None]

    def keep_state(carry_state):
        return carry_state

    gain_first = gain_one.astype(jnp.float32)
    shift_first = shift_one.astype(jnp.float32)
    gain_second = gain_two.astype(jnp.float32)
    shift_second = shift_two.astype(jnp.float32)
    inputs = tokens.astype(jnp.float32)
    first_normed = layer_norm(inputs, gain_first, shift_first)
    rows_one = gather_attn(first_normed.astype(jnp.bfloat16))
    packed_values = jnp.einsum(
        "scd,dhe->sche", rows_one, query_key_value_weight, preferred_element_type=jnp.float32
    )
    bias_pair = qv_bias.astype(jnp.float32)
    queries = (packed_values[..., :HEAD_DIM] + bias_pair[:, :HEAD_DIM]).astype(jnp.bfloat16)
    keys_here = packed_values[..., HEAD_DIM : 2 * HEAD_DIM].astype(jnp.bfloat16)
    values_here = (packed_values[..., 2 * HEAD_DIM :] + bias_pair[:, HEAD_DIM:]).astype(
        jnp.bfloat16
    )
    key_value = jnp.concatenate([keys_here, values_here], axis=-1)
    start_state = (
        jnp.full((seq_count, heads_here, span_rows), neg_fill, jnp.float32),
        jnp.zeros((seq_count, heads_here, span_rows), jnp.float32),
        jnp.zeros((seq_count, heads_here, span_rows, HEAD_DIM), jnp.float32),
    )
    folded = start_state
    piece_rows = lax.all_gather(key_value, "ctx", axis=1, tiled=True)
    piece_len = piece_rows.shape[1]
    block_width = min(piece_len, span_rows)

    def attend_block(carry_state, block_index):
        offset = block_index * block_width

        def attend_compute(inner_state):
            row_best, row_total, weighted = inner_state
            one_block = lax.dynamic_slice_in_dim(
                piece_rows, block_index * block_width, block_width, 1
            )
            scores = (
                jnp.einsum(
                    "sqhe,skhe->shqk",
                    queries,
                    one_block[..., :HEAD_DIM],
                    preferred_element_type=jnp.float32,
                )
                * score_scale
            )
            allowed = allowed_mask(offset, block_width)
            row_top = jnp.max(jnp.where(allowed, scores, neg_fill), axis=-1)
            new_best = jnp.maximum(row_best, row_top)
            soft_terms = jnp.where(allowed, jnp.exp(scores - new_best[..., None]), 0.0)
            rescale = jnp.exp(row_best - new_best)
            row_total = row_total * rescale + jnp.sum(soft_terms, axis=-1)
            weighted = weighted * rescale[..., None] + jnp.einsum(
                "shqk,skhe->shqe",
                soft_terms.astype(jnp.bfloat16),
                one_block[..., HEAD_DIM:],
                preferred_element_type=jnp.float32,
            )
            return (new_best, row_total, weighted)

        return (lax.cond(offset <= last_query, attend_compute, keep_state, carry_state), None)

    folded, _ = lax.scan(
        attend_block, folded, jnp.arange(piece_len // block_width, dtype=jnp.int32)
    )
    row_best, row_total, weighted = folded
    mixed_exact = weighted / row_total[..., None]
    log_total = row_best + jnp.log(row_total)
    mixed_low = jnp.transpose(mixed_exact, (0, 2, 1, 3)).astype(jnp.bfloat16)
    attn_part = jnp.einsum(
        "sche,hed->scd", mixed_low, attention_out_weight, preferred_element_type=jnp.float32
    )
    residual_one = inputs + reduce_attn(attn_part) + attention_out_bias.astype(jnp.float32)
    second_normed = layer_norm(residual_one, gain_second, shift_second)
    normed_low = second_normed.astype(jnp.bfloat16)
    grad_rows = out_grad.astype(jnp.float32)
    grad_low = grad_rows.astype(jnp.bfloat16)
    rows_two = gather_mlp(normed_low)
    grad_gathered = gather_mlp(grad_low)
    branch_part, normed_grad, fc_grad, fcb_grad, proj_grad = feed_forward(
        rows_two, expand_weight, expand_bias, contract_weight, grad_gathered
    )
    feedforward_branch = reduce_mlp(branch_part)
    dnormed_two = reduce_mlp(normed_grad)
    layer_out = (residual_one + feedforward_branch + contract_bias.astype(jnp.float32)).astype(
        jnp.bfloat16
    )
    pull_two = jax.vjp(layer_norm, residual_one, gain_second, shift_second)[1]
    res_extra, gain_two_grad, shift_two_grad = pull_two(dnormed_two)
    grad_res = grad_rows + res_extra
    attn_grad_rows = gather_attn(grad_res.astype(jnp.bfloat16))
    dmixed = jnp.einsum(
        "scd,hed->sche", attn_grad_rows, attention_out_weight, preferred_element_type=jnp.float32
    ).astype(jnp.bfloat16)
    outw_grad = jnp.einsum(
        "sche,scd->hed", mixed_low, attn_grad_rows, preferred_element_type=jnp.float32
    )
    dmixed_heads = jnp.transpose(dmixed, (0, 2, 1, 3))
    row_delta = jnp.sum(dmixed_heads.astype(jnp.float32) * mixed_exact, axis=-1)
    back_start = (
        jnp.zeros((seq_count, heads_here, span_rows, HEAD_DIM), jnp.float32),
        jnp.zeros((seq_count, full_length, heads_here, 2 * HEAD_DIM), jnp.float32),
    )
    folded = back_start
    back_piece_rows = lax.all_gather(key_value, "ctx", axis=1, tiled=True)
    piece_len = back_piece_rows.shape[1]
    back_block_width = min(piece_len, span_rows)

    def back_block(carry_state, block_index):
        offset = block_index * back_block_width

        def back_compute(inner_state):
            query_grad, pair_grads = inner_state
            one_block = lax.dynamic_slice_in_dim(
                back_piece_rows, block_index * back_block_width, back_block_width, 1
            )
            keys_block = one_block[..., :HEAD_DIM]
            values_block = one_block[..., HEAD_DIM:]
            scores = (
                jnp.einsum(
                    "sqhe,skhe->shqk", queries, keys_block, preferred_element_type=jnp.float32
                )
                * score_scale
            )
            allowed = allowed_mask(offset, back_block_width)
            soft_terms = jnp.where(allowed, jnp.exp(scores - log_total[..., None]), 0.0)
            soft_grad = jnp.einsum(
                "shqe,skhe->shqk", dmixed_heads, values_block, preferred_element_type=jnp.float32
            )
            score_grad = (soft_terms * (soft_grad - row_delta[..., None])).astype(jnp.bfloat16)
            query_grad = query_grad + score_scale * jnp.einsum(
                "shqk,skhe->shqe", score_grad, keys_block, preferred_element_type=jnp.float32
            )
            key_grad = score_scale * jnp.einsum(
                "shqk,sqhe->skhe", score_grad, queries, preferred_element_type=jnp.float32
            )
            value_grad = jnp.einsum(
                "shqk,shqe->skhe",
                soft_terms.astype(jnp.bfloat16),
                dmixed_heads,
                preferred_element_type=jnp.float32,
            )
            earlier = lax.dynamic_slice_in_dim(pair_grads, offset, back_block_width, 1)
            pair_grads = lax.dynamic_update_slice_in_dim(
                pair_grads, earlier + jnp.concatenate([key_grad, value_grad], axis=-1), offset, 1
            )
            return (query_grad, pair_grads)

        return (lax.cond(offset <= last_query, back_compute, keep_state, carry_state), None)

    folded, _ = lax.scan(
        back_block, folded, jnp.arange(piece_len // back_block_width, dtype=jnp.int32)
    )
    query_grad, pair_grads = folded
    pair_mine = lax.psum_scatter(
        pair_grads.astype(jnp.bfloat16), "ctx", scatter_dimension=1, tiled=True
    )
    query_low = jnp.transpose(query_grad, (0, 2, 1, 3)).astype(jnp.bfloat16)
    packed_grad = jnp.concatenate([query_low, pair_mine], axis=-1)
    qkv_grad = jnp.einsum(
        "scd,sche->dhe", rows_one, packed_grad, preferred_element_type=jnp.float32
    )
    qvb_grad = jnp.concatenate(
        [
            jnp.sum(query_low, axis=(0, 1), dtype=jnp.float32),
            jnp.sum(pair_mine[..., HEAD_DIM:], axis=(0, 1), dtype=jnp.float32),
        ],
        axis=-1,
    )
    normed_one_grad = reduce_attn(
        jnp.einsum(
            "sche,dhe->scd", packed_grad, query_key_value_weight, preferred_element_type=jnp.float32
        )
    )
    pull_one = jax.vjp(layer_norm, inputs, gain_first, shift_first)[1]
    input_extra, gain_one_grad, shift_one_grad = pull_one(normed_one_grad)
    grad_tokens = grad_res + input_extra
    small_sums = lax.psum(
        (
            gain_one_grad,
            shift_one_grad,
            jnp.sum(grad_res, axis=(0, 1)),
            gain_two_grad,
            shift_two_grad,
            jnp.sum(grad_rows, axis=(0, 1)),
        ),
        ("ctx", "tp"),
    )
    qkv_grad, qvb_grad, outw_grad, fc_grad, fcb_grad, proj_grad = (
        lax.psum(qkv_grad.astype(jnp.bfloat16), "ctx").astype(jnp.float32),
        lax.psum(qvb_grad.astype(jnp.bfloat16), "ctx").astype(jnp.float32),
        lax.psum(outw_grad.astype(jnp.bfloat16), "ctx").astype(jnp.float32),
        lax.psum(fc_grad.astype(jnp.bfloat16), "ctx").astype(jnp.float32),
        lax.psum(fcb_grad.astype(jnp.bfloat16), "ctx").astype(jnp.float32),
        lax.psum(proj_grad.astype(jnp.bfloat16), "ctx").astype(jnp.float32),
    )
    return (
        layer_out,
        grad_tokens,
        small_sums[0],
        small_sums[1],
        qkv_grad,
        qvb_grad,
        outw_grad,
        small_sums[2],
        small_sums[3],
        small_sums[4],
        fc_grad,
        fcb_grad,
        proj_grad,
        small_sums[5],
    )


bf16 = jnp.bfloat16
f32 = jnp.float32
BLK = 512
PAIR = 2 * HEAD_DIM
DOC_FAR = -(2.0**100)
CAUSAL_FAR = -2e30

TP_CORE = [(i, i ^ 1) for i in range(4)]
TP_ROW = [(i, i ^ 2) for i in range(4)]
CTX_X = [(i, i ^ 1) for i in range(8)]
CTX_Z1 = [(i, i ^ 2) for i in range(8)]
CTX_Z2 = [(i, i ^ 4) for i in range(8)]
CTX_PLANES = [[0, 2, 4, 6], [1, 3, 5, 7]]


def tie(*values):
    return lax.optimization_barrier(values)


def contract(a, b, dims):
    return lax.dot_general(a, b, (dims, ((), ())), preferred_element_type=f32)


def head_pair(packed, part):
    low = part * HEAD_DIM
    high = (part + 3) * HEAD_DIM
    return jnp.concatenate(
        [packed[:, low : low + HEAD_DIM], packed[:, high : high + HEAD_DIM]], axis=1
    )


def lane_half(rows, head):
    lanes = lax.broadcasted_iota(jnp.int32, (rows, PAIR), 1)
    return (lanes >= HEAD_DIM) if head else (lanes < HEAD_DIM)


def attend_kernel(
    first_ref, mine_ref, other_ref, qdoc_ref, kdoc_ref, bias_ref,
    out_mine_ref, out_other_ref, exact_ref, log_ref, key_ref, value_ref, best_ref, total_ref, acc_ref,
):
    i = pl.program_id(0)
    half = BLK // 2
    rows = pl.ds(pl.multiple_of(i * half, half), half)
    block = pl.ds(pl.multiple_of(i * BLK, BLK), BLK)
    packed = jnp.concatenate([mine_ref[rows, :], other_ref[rows, :]], axis=0)
    queries = head_pair(packed, 0) * jnp.asarray(HEAD_DIM**-0.5, bf16)
    key_ref[block, :PAIR] = head_pair(packed, 1)
    key_ref[block, PAIR:] = kdoc_ref[block, :]
    value_ref[block, :] = head_pair(packed, 2)
    qdoc = qdoc_ref[block, :]
    query_heads = [
        jnp.concatenate([jnp.where(lane_half(BLK, h), queries, jnp.zeros_like(queries)), qdoc], axis=1)
        for h in range(2)
    ]
    best_ref[...] = jnp.full_like(best_ref, neg_fill)
    total_ref[...] = jnp.zeros_like(total_ref)
    acc_ref[...] = jnp.zeros_like(acc_ref)

    def visit(j, bias):
        keys = pl.ds(pl.multiple_of(j * BLK, BLK), BLK)
        key_block = key_ref[keys, :]
        value_block = value_ref[keys, :]
        for h in range(2):
            scores = contract(key_block, query_heads[h], ((1,), (1,)))
            if bias is not None:
                scores = scores + bias
            old = best_ref[h : h + 1, :]
            new = jnp.maximum(old, jnp.max(scores, axis=0, keepdims=True))
            weights = jnp.exp(scores - new)
            fade = jnp.exp(old - new)
            total_ref[h : h + 1, :] = total_ref[h : h + 1, :] * fade + jnp.sum(
                weights, axis=0, keepdims=True
            )
            product = contract(value_block, weights.astype(bf16), ((0,), (0,)))
            part = slice(h * HEAD_DIM, (h + 1) * HEAD_DIM)
            acc_ref[part, :] = acc_ref[part, :] * fade + product[part, :]
            best_ref[h : h + 1, :] = new

    def step(j, carry):
        visit(j, None)
        return carry

    lax.fori_loop(first_ref[i], i, step, 0)
    visit(i, bias_ref[...])
    for h in range(2):
        part = slice(h * HEAD_DIM, (h + 1) * HEAD_DIM)
        acc_ref[part, :] = acc_ref[part, :] / total_ref[h : h + 1, :]
        log_ref[h : h + 1, block] = best_ref[h : h + 1, :] + jnp.log(total_ref[h : h + 1, :])
    mixed = acc_ref[...]
    exact_ref[:, block] = mixed
    low = jnp.transpose(mixed).astype(bf16)
    out_mine_ref[rows, :] = low[:half]
    out_other_ref[rows, :] = low[half:]


def attend_back_kernel(
    first_ref, mine_ref, other_ref, qdoc_ref, kdoc_ref, bias_ref, exact_ref, log_ref, dmine_ref, dother_ref,
    out_mine_ref, out_other_ref, key_ref, value_ref, dkey_ref, dvalue_ref, dquery_ref, dquery_all_ref,
):
    i = pl.program_id(0)
    half = BLK // 2
    rows = pl.ds(pl.multiple_of(i * half, half), half)
    block = pl.ds(pl.multiple_of(i * BLK, BLK), BLK)
    packed = jnp.concatenate([mine_ref[rows, :], other_ref[rows, :]], axis=0)
    scale = HEAD_DIM**-0.5
    queries = head_pair(packed, 0) * jnp.asarray(scale, bf16)
    key_ref[block, :PAIR] = head_pair(packed, 1)
    key_ref[block, PAIR:] = kdoc_ref[block, :]
    value_ref[block, :] = head_pair(packed, 2)
    dkey_ref[block, :] = jnp.zeros((BLK, PAIR), f32)
    dvalue_ref[block, :] = jnp.zeros((BLK, PAIR), f32)
    dquery_ref[...] = jnp.zeros_like(dquery_ref)
    dmixed = jnp.concatenate([dmine_ref[rows, :], dother_ref[rows, :]], axis=0)
    qdoc = qdoc_ref[block, :]
    masked = [jnp.where(lane_half(BLK, h), queries, jnp.zeros_like(queries)) for h in range(2)]
    dmasked = [jnp.where(lane_half(BLK, h), dmixed, jnp.zeros_like(dmixed)) for h in range(2)]
    query_heads = [jnp.concatenate([masked[h], qdoc], axis=1) for h in range(2)]
    product = jnp.transpose(dmixed.astype(f32)) * exact_ref[:, block]
    deltas = [
        jnp.sum(product[h * HEAD_DIM : (h + 1) * HEAD_DIM, :], axis=0, keepdims=True) for h in range(2)
    ]
    logs = [log_ref[h : h + 1, block] for h in range(2)]

    def visit(j, bias):
        keys = pl.ds(pl.multiple_of(j * BLK, BLK), BLK)
        key_block = key_ref[keys, :]
        value_block = value_ref[keys, :]
        dkey = dkey_ref[keys, :]
        dvalue = dvalue_ref[keys, :]
        for h in range(2):
            scores = contract(key_block, query_heads[h], ((1,), (1,)))
            if bias is not None:
                scores = scores + bias
            weights = jnp.exp(scores - logs[h])
            dweights = contract(value_block, dmasked[h], ((1,), (1,)))
            dscores = (weights * (dweights - deltas[h])).astype(bf16)
            dvalue = dvalue + contract(weights.astype(bf16), dmasked[h], ((1,), (0,)))
            dkey = dkey + contract(dscores, masked[h], ((1,), (0,)))
            part = slice(h * HEAD_DIM, (h + 1) * HEAD_DIM)
            turned = contract(key_block[:, :PAIR], dscores, ((0,), (0,)))
            dquery_ref[part, :] = dquery_ref[part, :] + turned[part, :]
        dkey_ref[keys, :] = dkey
        dvalue_ref[keys, :] = dvalue

    def step(j, carry):
        visit(j, None)
        return carry

    lax.fori_loop(first_ref[i], i, step, 0)
    visit(i, bias_ref[...])
    dquery_all_ref[block, :] = jnp.transpose(dquery_ref[...] * scale)

    @pl.when(i == pl.num_programs(0) - 1)
    def _():
        for b in range(4):
            for side, out in ((0, out_mine_ref), (1, out_other_ref)):
                source = slice(b * BLK + side * half, b * BLK + (side + 1) * half)
                target = slice(b * half, (b + 1) * half)
                grads = [ref[source, :] for ref in (dquery_all_ref, dkey_ref, dvalue_ref)]
                out[target, :] = jnp.concatenate(
                    [g[:, h * HEAD_DIM : (h + 1) * HEAD_DIM] for h in range(2) for g in grads], axis=1
                ).astype(bf16)


def whole(shape):
    return pl.BlockSpec(shape, lambda i: (0,) * len(shape))


def attend(first, mine, other, qdoc, kdoc, bias):
    length = qdoc.shape[0]
    half = length // 2
    return pl.pallas_call(
        attend_kernel,
        grid=(length // BLK,),
        in_specs=[
            pl.BlockSpec(memory_space=pltpu.SMEM),
            whole(mine.shape), whole(other.shape), whole(qdoc.shape), whole(kdoc.shape), whole(bias.shape),
        ],
        out_specs=[whole((half, PAIR)), whole((half, PAIR)), whole((PAIR, length)), whole((2, length))],
        out_shape=[
            jax.ShapeDtypeStruct((half, PAIR), bf16),
            jax.ShapeDtypeStruct((half, PAIR), bf16),
            jax.ShapeDtypeStruct((PAIR, length), f32),
            jax.ShapeDtypeStruct((2, length), f32),
        ],
        scratch_shapes=[
            pltpu.VMEM((length, 2 * PAIR), bf16),
            pltpu.VMEM((length, PAIR), bf16),
            pltpu.VMEM((2, BLK), f32),
            pltpu.VMEM((2, BLK), f32),
            pltpu.VMEM((PAIR, BLK), f32),
        ],
        compiler_params=pltpu.CompilerParams(
            dimension_semantics=("arbitrary",), vmem_limit_bytes=40 << 20
        ),
        name="attend",
    )(first, mine, other, qdoc, kdoc, bias)


def attend_back(first, mine, other, qdoc, kdoc, bias, exact, log_total, dmine, dother):
    length = qdoc.shape[0]
    half = length // 2
    operands = (mine, other, qdoc, kdoc, bias, exact, log_total, dmine, dother)
    return pl.pallas_call(
        attend_back_kernel,
        grid=(length // BLK,),
        in_specs=[pl.BlockSpec(memory_space=pltpu.SMEM)] + [whole(o.shape) for o in operands],
        out_specs=[whole((half, 3 * PAIR)), whole((half, 3 * PAIR))],
        out_shape=[jax.ShapeDtypeStruct((half, 3 * PAIR), bf16)] * 2,
        scratch_shapes=[
            pltpu.VMEM((length, 2 * PAIR), bf16),
            pltpu.VMEM((length, PAIR), bf16),
            pltpu.VMEM((length, PAIR), f32),
            pltpu.VMEM((length, PAIR), f32),
            pltpu.VMEM((PAIR, BLK), f32),
            pltpu.VMEM((length, PAIR), f32),
        ],
        compiler_params=pltpu.CompilerParams(
            dimension_semantics=("arbitrary",), vmem_limit_bytes=48 << 20
        ),
        name="attend_back",
    )(first, *operands)


def planes_swap(values):
    return lax.all_to_all(values, "ctx", 0, 0, axis_index_groups=CTX_PLANES, tiled=False)


def tp_gather(values):
    core = lax.ppermute(values, "tp", TP_CORE)
    row = lax.ppermute(values, "tp", TP_ROW)
    both = lax.ppermute(row, "tp", TP_CORE)
    return [values, core, row, both]


def tp_gather_rows(values):
    return jnp.stack(tp_gather(values), axis=1)


def tp_scatter_rows(make_part, meanwhile):
    away = jnp.stack([make_part(3), make_part(1)]).astype(bf16)
    came = lax.ppermute(away, "tp", TP_CORE)
    across = (make_part(2) + came[0].astype(f32)).astype(bf16)
    across, filler = meanwhile(across)
    arrived = lax.ppermute(across, "tp", TP_ROW)
    own, filler = tie(make_part(0) + came[1].astype(f32), filler)
    return own + arrived.astype(f32), filler


def tp_swap(pieces):
    return [
        pieces[0],
        lax.ppermute(pieces[1], "tp", TP_CORE),
        lax.ppermute(pieces[2], "tp", TP_ROW),
        lax.ppermute(pieces[3], "tp", [(i, i ^ 3) for i in range(4)]),
    ]


def sum_ctx(values):
    for perm in (CTX_X, CTX_Z1, CTX_Z2):
        values = values + lax.ppermute(values, "ctx", perm)
    return values


def sum_tp(values):
    for perm in (TP_CORE, TP_ROW):
        values = values + lax.ppermute(values, "tp", perm)
    return values


def sum_all(values):
    return sum_ctx(sum_tp(values))


def norm_stats(values):
    centred = values - jnp.mean(values, axis=-1, keepdims=True)
    rate = lax.rsqrt(jnp.mean(centred * centred, axis=-1, keepdims=True) + eps)
    return centred * rate, rate


def norm_back(hat, rate, gain, grad):
    dhat = grad * gain
    return rate * (
        dhat
        - jnp.mean(dhat, axis=-1, keepdims=True)
        - hat * jnp.mean(dhat * hat, axis=-1, keepdims=True)
    )


def order_pair(values, swapped, axis):
    first, second = jnp.split(values, 2, axis=axis)
    return jnp.where(
        swapped,
        jnp.concatenate([second, first], axis=axis),
        jnp.concatenate([first, second], axis=axis),
    )


def shards(
    tokens,
    gain_one,
    shift_one,
    query_key_value_weight,
    qv_bias,
    attention_out_weight,
    attention_out_bias,
    gain_two,
    shift_two,
    expand_weight,
    expand_bias,
    contract_weight,
    contract_bias,
    doc_ids,
    out_grad,
):
    width = tokens.shape[2]
    span = doc_ids.shape[1]
    piece = tokens.shape[1]
    planes = tokens.shape[0]
    here = planes * piece
    group = here * 4
    ctx_at = lax.axis_index("ctx")
    tp_at = lax.axis_index("tp")
    side = ctx_at % 2
    plane = ctx_at // 2
    swapped = side == 1
    gain_first, shift_first = gain_one.astype(f32), shift_one.astype(f32)
    gain_second, shift_second = gain_two.astype(f32), shift_two.astype(f32)

    inputs, doc_ids = tie(planes_swap(tokens), doc_ids)
    inputs = inputs.astype(f32)

    qkv_rel = jnp.transpose(query_key_value_weight, (1, 2, 0)).reshape(12 * HEAD_DIM, width)
    qkv_rel = order_pair(qkv_rel, swapped, 0)
    zero_key = jnp.zeros((4, HEAD_DIM), f32)
    bias_all = qv_bias.astype(f32)
    bias_rel = jnp.concatenate([bias_all[:, :HEAD_DIM], zero_key, bias_all[:, HEAD_DIM:]], axis=1)
    bias_rel = order_pair(bias_rel.reshape(12 * HEAD_DIM), swapped, 0)
    out_rel = order_pair(attention_out_weight.reshape(4 * HEAD_DIM, width), swapped, 0)
    ids = planes_swap(doc_ids)
    ids = jnp.stack([ids, lax.ppermute(ids, "ctx", CTX_X)], axis=1).reshape(planes, 2, 2, 2, piece)
    ids = jnp.where(tp_at % 2 == 1, jnp.flip(ids, 3), ids)
    ids = jnp.where(tp_at // 2 == 1, jnp.flip(ids, 2), ids).reshape(planes, 2 * span)
    low_id, high_id = jnp.min(ids, axis=1), jnp.max(ids, axis=1)
    first_block = jnp.sum((high_id[None, :] < low_id[:, None]).astype(jnp.int32), axis=1)
    lanes = jnp.arange(PAIR, dtype=jnp.int32)
    same = ids.reshape(-1, 1) == lanes[None, :]
    kdoc = same.astype(bf16)
    qdoc = jnp.where(same, 0.0, DOC_FAR).astype(bf16)
    place = (
        ((side ^ jnp.arange(2, dtype=jnp.int32)) * span)[:, None, None]
        + ((tp_at ^ jnp.arange(4, dtype=jnp.int32)) * piece)[None, :, None]
        + jnp.arange(piece, dtype=jnp.int32)[None, None, :]
    ).reshape(-1)
    bias = jnp.where(place[:, None] <= place[None, :], 0.0, CAUSAL_FAR).astype(f32)

    hat_one, rate_one = norm_stats(inputs)
    rows_one = tp_gather_rows((hat_one * gain_first + shift_first).astype(bf16)).reshape(group, width)

    rows_one, out_rel, out_grad = tie(rows_one, out_rel, out_grad)

    def project(j):
        part = slice(j * 6 * HEAD_DIM, (j + 1) * 6 * HEAD_DIM)
        return (contract(rows_one, qkv_rel[part], ((1,), (1,))) + bias_rel[part]).astype(bf16)

    qkv_other = lax.ppermute(project(1), "ctx", CTX_X)
    qkv_mine = project(0)

    grad_rows = planes_swap(out_grad)
    out_full = tp_gather(out_rel)
    grad_gathered = tp_gather_rows(grad_rows).reshape(group, width)
    grad_rows = grad_rows.astype(f32)
    act_grad = contract(grad_gathered, contract_weight, ((1,), (1,)))

    mixed_mine, mixed_other, exact, log_total = attend(
        first_block, qkv_mine, qkv_other, qdoc, kdoc, bias
    )
    mixed_arrived = lax.ppermute(mixed_other, "ctx", CTX_X)
    mixed_arrived, rows_one = tie(mixed_arrived, rows_one)
    mixed_heads = jnp.concatenate([mixed_mine, mixed_arrived], axis=1)
    rows_one_x = lax.ppermute(rows_one, "ctx", CTX_X)
    by_tp = mixed_heads.reshape(planes, 4, piece, 2 * PAIR)
    mixed_pieces = tp_swap([by_tp[:, k] for k in range(4)])
    attn_branch = sum(
        contract(mixed_pieces[k].reshape(here, 2 * PAIR), out_full[k], ((1,), (0,))) for k in range(4)
    ).reshape(planes, piece, width)
    residual_one = inputs + attn_branch + attention_out_bias.astype(f32)

    hat_two, rate_two = norm_stats(residual_one)
    rows_two = tp_gather_rows((hat_two * gain_second + shift_second).astype(bf16)).reshape(group, width)
    pre_act = jnp.dot(rows_two, expand_weight, preferred_element_type=f32) + expand_bias.astype(f32)
    active, pull_gelu = jax.vjp(gelu_tanh, pre_act)
    active = active.astype(bf16)
    dpre = pull_gelu(act_grad)[0].astype(bf16)
    dpre_parts = dpre.reshape(planes, 4, piece, -1)
    def feed_forward_grads(sent):
        sent, normed, hidden = tie(sent, rows_two, active)
        fc_part = contract(normed, dpre, ((0,), (0,)))
        proj_part = contract(hidden, grad_gathered, ((0,), (0,)))
        return sent, (fc_part.astype(bf16), proj_part.astype(bf16))

    dnormed_two, (fc_grad, proj_grad) = tp_scatter_rows(
        lambda k: contract(
            dpre_parts[:, k].reshape(here, -1), expand_weight, ((1,), (1,))
        ).reshape(planes, piece, width),
        feed_forward_grads,
    )
    fcb_grad = jnp.sum(dpre, axis=0, dtype=f32)
    proj_grad, fc_grad = lax.psum((proj_grad, fc_grad), "ctx")

    grad_res = grad_rows + norm_back(hat_two, rate_two, gain_second, dnormed_two)
    attn_grad = grad_res.astype(bf16)
    attn_rows = attn_grad.reshape(here, width)
    dmixed = tp_swap(
        [
            contract(attn_rows, out_full[k], ((1,), (1,))).astype(bf16).reshape(planes, piece, 2 * PAIR)
            for k in range(4)
        ]
    )
    dmixed = jnp.stack(dmixed, axis=1).reshape(group, 2 * PAIR)
    dmixed, attn_grad, active = tie(dmixed, attn_grad, active)
    dmixed_other = lax.ppermute(dmixed[:, PAIR:], "ctx", CTX_X)
    grad_mine, grad_other = attend_back(
        first_block, qkv_mine, qkv_other, qdoc, kdoc, bias, exact, log_total, dmixed[:, :PAIR], dmixed_other
    )
    grad_mine, grad_other, mixed_heads = tie(grad_mine, grad_other, mixed_heads)
    packed_grad = jnp.concatenate([grad_mine, lax.ppermute(grad_other, "ctx", CTX_X)], axis=1)

    branch_in = active.reshape(planes, 4, piece, -1)
    feedforward_branch, _ = tp_scatter_rows(
        lambda k: jnp.dot(
            branch_in[:, k].reshape(here, -1), contract_weight, preferred_element_type=f32
        ).reshape(planes, piece, width),
        lambda sent: (sent, ()),
    )
    layer_low = (residual_one + feedforward_branch + contract_bias.astype(f32)).astype(bf16)

    attn_grad_rows = tp_gather_rows(attn_grad).reshape(group, width)
    outw = contract(mixed_heads, attn_grad_rows, ((0,), (0,)))
    outw_came = lax.ppermute(outw[PAIR:].astype(bf16), "ctx", CTX_X)
    qkv_part = contract(grad_mine, rows_one, ((0,), (0,))) + contract(grad_other, rows_one_x, ((0,), (0,)))
    outw_part = outw[:PAIR] + outw_came.astype(f32)
    parts = jnp.concatenate([qkv_part.astype(bf16), outw_part.astype(bf16)], axis=0)

    packed_parts = packed_grad.reshape(planes, 4, piece, 6 * PAIR)
    dnormed_one, parts = tp_scatter_rows(
        lambda k: jnp.dot(
            packed_parts[:, k].reshape(here, -1), qkv_rel, preferred_element_type=f32
        ).reshape(planes, piece, width),
        lambda sent: tie(sent, parts),
    )
    parts = parts.reshape(4, PAIR, width)
    moves = [[(i, i ^ (2 * d)) for i in range(8)] for d in range(4)]
    came = [
        lax.ppermute(lax.dynamic_index_in_dim(parts, plane ^ d, 0, keepdims=False), "ctx", moves[d])
        for d in range(1, 4)
    ]
    own = lax.dynamic_index_in_dim(parts, plane, 0, keepdims=False)
    grad_tokens = grad_res + norm_back(hat_one, rate_one, gain_first, dnormed_one)
    grad_tokens = planes_swap(grad_tokens.astype(bf16))
    grad_tokens, layer_low, own, came = tie(grad_tokens, layer_low, own, came)
    grad_tokens = grad_tokens.astype(f32)
    total = (own.astype(f32) + sum(c.astype(f32) for c in came)).astype(bf16)
    layer_out = planes_swap(layer_low)

    wide = jnp.zeros((2, 4, PAIR, width), bf16)
    for d in range(4):
        near = total if d == 0 else lax.ppermute(total, "ctx", moves[d])
        far = lax.ppermute(near, "ctx", CTX_X)
        wide = lax.dynamic_update_slice(wide, near[None, None], (side, plane ^ d, 0, 0))
        wide = lax.dynamic_update_slice(wide, far[None, None], (1 - side, plane ^ d, 0, 0))
    qkv_grad = wide[:, :3].astype(f32).reshape(4, 3 * HEAD_DIM, width)
    qkv_grad = jnp.transpose(qkv_grad, (2, 0, 1))
    outw_grad = wide[:, 3].astype(f32)
    small = sum_tp(
        jnp.stack(
            [
                jnp.sum(dnormed_one * hat_one, axis=(0, 1)),
                jnp.sum(dnormed_one, axis=(0, 1)),
                jnp.sum(grad_res, axis=(0, 1)),
                jnp.sum(dnormed_two * hat_two, axis=(0, 1)),
                jnp.sum(dnormed_two, axis=(0, 1)),
                jnp.sum(grad_rows, axis=(0, 1)),
            ]
        )
    )
    bias_sums = jnp.sum(packed_grad, axis=0, dtype=f32)[None]
    bias_sums = order_pair(bias_sums, swapped, 1)
    bias_sums = jnp.pad(bias_sums, ((0, 0), (0, width - 12 * HEAD_DIM)))
    small = sum_ctx(jnp.concatenate([small, fcb_grad[None], bias_sums]))
    bias_sums = small[7, : 12 * HEAD_DIM].reshape(4, 3, HEAD_DIM)
    qvb_grad = jnp.concatenate([bias_sums[:, 0], bias_sums[:, 2]], axis=-1)
    return (
        layer_out,
        grad_tokens,
        small[0],
        small[1],
        qkv_grad,
        qvb_grad,
        outw_grad.reshape(4, HEAD_DIM, width),
        small[2],
        small[3],
        small[4],
        fc_grad.astype(f32),
        small[6],
        proj_grad.astype(f32),
        small[5],
    )


def solution(mesh):
    sizes = dict(zip(mesh.axis_names, mesh.devices.shape))
    body = shards if (sizes["ctx"], sizes["tp"]) == (8, 4) else shards_plain
    return jax.shard_map(
        body,
        mesh=mesh,
        in_specs=(
            P(None, ("ctx", "tp"), None),
            P(),
            P(),
            P(None, "tp", None),
            P("tp", None),
            P("tp", None, None),
            P(),
            P(),
            P(),
            P(None, "tp"),
            P("tp"),
            P("tp", None),
            P(),
            P(None, "ctx"),
            P(None, ("ctx", "tp"), None),
        ),
        out_specs=(
            P(None, ("ctx", "tp"), None),
            P(None, ("ctx", "tp"), None),
            P(),
            P(),
            P(None, "tp", None),
            P("tp", None),
            P("tp", None, None),
            P(),
            P(),
            P(),
            P(None, "tp"),
            P("tp"),
            P("tp", None),
            P(),
        ),
        check_vma=False,
    )
```

```python
import jax
import jax.numpy as jnp
from jax import lax
from jax.experimental import pallas as pl
from jax.experimental.pallas import tpu as pltpu
from jax.sharding import PartitionSpec as P

HEAD_DIM = 64


eps = 1e-05
neg_fill = -1e30


def layer_norm(values, gain, shift):
    centre = jnp.mean(values, axis=-1, keepdims=True)
    centred = values - centre
    spread = jnp.mean(centred * centred, axis=-1, keepdims=True)
    return centred * lax.rsqrt(spread + eps) * gain + shift


def gelu_tanh(values):
    return jax.nn.gelu(values, approximate=True)


def gather_attn(values):
    return lax.all_gather(values, "tp", axis=1, tiled=True)


def reduce_attn(values):
    return lax.psum_scatter(
        values.astype(jnp.bfloat16), "tp", scatter_dimension=1, tiled=True
    ).astype(jnp.float32)


def gather_mlp(values):
    return lax.all_gather(values, "tp", axis=1, tiled=True)


def reduce_mlp(values):
    return lax.psum_scatter(
        values.astype(jnp.bfloat16), "tp", scatter_dimension=1, tiled=True
    ).astype(jnp.float32)


def feed_forward(normed_rows, fc_full, fcb_full, proj_full, grad_in):
    pre_activation = jnp.einsum(
        "scd,df->scf", normed_rows, fc_full, preferred_element_type=jnp.float32
    ) + fcb_full.astype(jnp.float32)
    active_rows = gelu_tanh(pre_activation).astype(jnp.bfloat16)
    branch_part = jnp.einsum(
        "scf,fd->scd", active_rows, proj_full, preferred_element_type=jnp.float32
    )
    act_grad = jnp.einsum("scd,fd->scf", grad_in, proj_full, preferred_element_type=jnp.float32)
    pre_grad = jax.vjp(gelu_tanh, pre_activation)[1](act_grad)[0].astype(jnp.bfloat16)
    proj_grad = jnp.einsum("scf,scd->fd", active_rows, grad_in, preferred_element_type=jnp.float32)
    fc_grad = jnp.einsum("scd,scf->df", normed_rows, pre_grad, preferred_element_type=jnp.float32)
    fcb_grad = jnp.sum(pre_grad, axis=(0, 1), dtype=jnp.float32)
    normed_grad = jnp.einsum("scf,df->scd", pre_grad, fc_full, preferred_element_type=jnp.float32)
    return (branch_part, normed_grad, fc_grad, fcb_grad, proj_grad)


def shards_plain(
    tokens,
    gain_one,
    shift_one,
    query_key_value_weight,
    qv_bias,
    attention_out_weight,
    attention_out_bias,
    gain_two,
    shift_two,
    expand_weight,
    expand_bias,
    contract_weight,
    contract_bias,
    doc_ids,
    out_grad,
):
    score_scale = HEAD_DIM ** (-0.5)
    seq_count = tokens.shape[0]
    span_rows = doc_ids.shape[1]
    heads_here = query_key_value_weight.shape[1]
    full_length = span_rows * lax.axis_size("ctx")
    first_query = lax.axis_index("ctx") * span_rows
    query_pos = first_query + jnp.arange(span_rows, dtype=jnp.int32)
    last_query = first_query + span_rows - 1
    all_ids = lax.all_gather(doc_ids, "ctx", axis=1, tiled=True)

    def allowed_mask(offset, block_width):
        key_pos = offset + jnp.arange(block_width, dtype=jnp.int32)
        key_ids = lax.dynamic_slice_in_dim(all_ids, offset, block_width, 1)
        causal = key_pos[None, :] <= query_pos[:, None]
        same_doc = doc_ids[:, :, None] == key_ids[:, None, :]
        return jnp.logical_and(causal[None], same_doc)[:, None]

    def keep_state(carry_state):
        return carry_state

    gain_first = gain_one.astype(jnp.float32)
    shift_first = shift_one.astype(jnp.float32)
    gain_second = gain_two.astype(jnp.float32)
    shift_second = shift_two.astype(jnp.float32)
    inputs = tokens.astype(jnp.float32)
    first_normed = layer_norm(inputs, gain_first, shift_first)
    rows_one = gather_attn(first_normed.astype(jnp.bfloat16))
    packed_values = jnp.einsum(
        "scd,dhe->sche", rows_one, query_key_value_weight, preferred_element_type=jnp.float32
    )
    bias_pair = qv_bias.astype(jnp.float32)
    queries = (packed_values[..., :HEAD_DIM] + bias_pair[:, :HEAD_DIM]).astype(jnp.bfloat16)
    keys_here = packed_values[..., HEAD_DIM : 2 * HEAD_DIM].astype(jnp.bfloat16)
    values_here = (packed_values[..., 2 * HEAD_DIM :] + bias_pair[:, HEAD_DIM:]).astype(
        jnp.bfloat16
    )
    key_value = jnp.concatenate([keys_here, values_here], axis=-1)
    start_state = (
        jnp.full((seq_count, heads_here, span_rows), neg_fill, jnp.float32),
        jnp.zeros((seq_count, heads_here, span_rows), jnp.float32),
        jnp.zeros((seq_count, heads_here, span_rows, HEAD_DIM), jnp.float32),
    )
    folded = start_state
    piece_rows = lax.all_gather(key_value, "ctx", axis=1, tiled=True)
    piece_len = piece_rows.shape[1]
    block_width = min(piece_len, span_rows)

    def attend_block(carry_state, block_index):
        offset = block_index * block_width

        def attend_compute(inner_state):
            row_best, row_total, weighted = inner_state
            one_block = lax.dynamic_slice_in_dim(
                piece_rows, block_index * block_width, block_width, 1
            )
            scores = (
                jnp.einsum(
                    "sqhe,skhe->shqk",
                    queries,
                    one_block[..., :HEAD_DIM],
                    preferred_element_type=jnp.float32,
                )
                * score_scale
            )
            allowed = allowed_mask(offset, block_width)
            row_top = jnp.max(jnp.where(allowed, scores, neg_fill), axis=-1)
            new_best = jnp.maximum(row_best, row_top)
            soft_terms = jnp.where(allowed, jnp.exp(scores - new_best[..., None]), 0.0)
            rescale = jnp.exp(row_best - new_best)
            row_total = row_total * rescale + jnp.sum(soft_terms, axis=-1)
            weighted = weighted * rescale[..., None] + jnp.einsum(
                "shqk,skhe->shqe",
                soft_terms.astype(jnp.bfloat16),
                one_block[..., HEAD_DIM:],
                preferred_element_type=jnp.float32,
            )
            return (new_best, row_total, weighted)

        return (lax.cond(offset <= last_query, attend_compute, keep_state, carry_state), None)

    folded, _ = lax.scan(
        attend_block, folded, jnp.arange(piece_len // block_width, dtype=jnp.int32)
    )
    row_best, row_total, weighted = folded
    mixed_exact = weighted / row_total[..., None]
    log_total = row_best + jnp.log(row_total)
    mixed_low = jnp.transpose(mixed_exact, (0, 2, 1, 3)).astype(jnp.bfloat16)
    attn_part = jnp.einsum(
        "sche,hed->scd", mixed_low, attention_out_weight, preferred_element_type=jnp.float32
    )
    residual_one = inputs + reduce_attn(attn_part) + attention_out_bias.astype(jnp.float32)
    second_normed = layer_norm(residual_one, gain_second, shift_second)
    normed_low = second_normed.astype(jnp.bfloat16)
    grad_rows = out_grad.astype(jnp.float32)
    grad_low = grad_rows.astype(jnp.bfloat16)
    rows_two = gather_mlp(normed_low)
    grad_gathered = gather_mlp(grad_low)
    branch_part, normed_grad, fc_grad, fcb_grad, proj_grad = feed_forward(
        rows_two, expand_weight, expand_bias, contract_weight, grad_gathered
    )
    feedforward_branch = reduce_mlp(branch_part)
    dnormed_two = reduce_mlp(normed_grad)
    layer_out = (residual_one + feedforward_branch + contract_bias.astype(jnp.float32)).astype(
        jnp.bfloat16
    )
    pull_two = jax.vjp(layer_norm, residual_one, gain_second, shift_second)[1]
    res_extra, gain_two_grad, shift_two_grad = pull_two(dnormed_two)
    grad_res = grad_rows + res_extra
    attn_grad_rows = gather_attn(grad_res.astype(jnp.bfloat16))
    dmixed = jnp.einsum(
        "scd,hed->sche", attn_grad_rows, attention_out_weight, preferred_element_type=jnp.float32
    ).astype(jnp.bfloat16)
    outw_grad = jnp.einsum(
        "sche,scd->hed", mixed_low, attn_grad_rows, preferred_element_type=jnp.float32
    )
    dmixed_heads = jnp.transpose(dmixed, (0, 2, 1, 3))
    row_delta = jnp.sum(dmixed_heads.astype(jnp.float32) * mixed_exact, axis=-1)
    back_start = (
        jnp.zeros((seq_count, heads_here, span_rows, HEAD_DIM), jnp.float32),
        jnp.zeros((seq_count, full_length, heads_here, 2 * HEAD_DIM), jnp.float32),
    )
    folded = back_start
    back_piece_rows = lax.all_gather(key_value, "ctx", axis=1, tiled=True)
    piece_len = back_piece_rows.shape[1]
    back_block_width = min(piece_len, span_rows)

    def back_block(carry_state, block_index):
        offset = block_index * back_block_width

        def back_compute(inner_state):
            query_grad, pair_grads = inner_state
            one_block = lax.dynamic_slice_in_dim(
                back_piece_rows, block_index * back_block_width, back_block_width, 1
            )
            keys_block = one_block[..., :HEAD_DIM]
            values_block = one_block[..., HEAD_DIM:]
            scores = (
                jnp.einsum(
                    "sqhe,skhe->shqk", queries, keys_block, preferred_element_type=jnp.float32
                )
                * score_scale
            )
            allowed = allowed_mask(offset, back_block_width)
            soft_terms = jnp.where(allowed, jnp.exp(scores - log_total[..., None]), 0.0)
            soft_grad = jnp.einsum(
                "shqe,skhe->shqk", dmixed_heads, values_block, preferred_element_type=jnp.float32
            )
            score_grad = (soft_terms * (soft_grad - row_delta[..., None])).astype(jnp.bfloat16)
            query_grad = query_grad + score_scale * jnp.einsum(
                "shqk,skhe->shqe", score_grad, keys_block, preferred_element_type=jnp.float32
            )
            key_grad = score_scale * jnp.einsum(
                "shqk,sqhe->skhe", score_grad, queries, preferred_element_type=jnp.float32
            )
            value_grad = jnp.einsum(
                "shqk,shqe->skhe",
                soft_terms.astype(jnp.bfloat16),
                dmixed_heads,
                preferred_element_type=jnp.float32,
            )
            earlier = lax.dynamic_slice_in_dim(pair_grads, offset, back_block_width, 1)
            pair_grads = lax.dynamic_update_slice_in_dim(
                pair_grads, earlier + jnp.concatenate([key_grad, value_grad], axis=-1), offset, 1
            )
            return (query_grad, pair_grads)

        return (lax.cond(offset <= last_query, back_compute, keep_state, carry_state), None)

    folded, _ = lax.scan(
        back_block, folded, jnp.arange(piece_len // back_block_width, dtype=jnp.int32)
    )
    query_grad, pair_grads = folded
    pair_mine = lax.psum_scatter(
        pair_grads.astype(jnp.bfloat16), "ctx", scatter_dimension=1, tiled=True
    )
    query_low = jnp.transpose(query_grad, (0, 2, 1, 3)).astype(jnp.bfloat16)
    packed_grad = jnp.concatenate([query_low, pair_mine], axis=-1)
    qkv_grad = jnp.einsum(
        "scd,sche->dhe", rows_one, packed_grad, preferred_element_type=jnp.float32
    )
    qvb_grad = jnp.concatenate(
        [
            jnp.sum(query_low, axis=(0, 1), dtype=jnp.float32),
            jnp.sum(pair_mine[..., HEAD_DIM:], axis=(0, 1), dtype=jnp.float32),
        ],
        axis=-1,
    )
    normed_one_grad = reduce_attn(
        jnp.einsum(
            "sche,dhe->scd", packed_grad, query_key_value_weight, preferred_element_type=jnp.float32
        )
    )
    pull_one = jax.vjp(layer_norm, inputs, gain_first, shift_first)[1]
    input_extra, gain_one_grad, shift_one_grad = pull_one(normed_one_grad)
    grad_tokens = grad_res + input_extra
    small_sums = lax.psum(
        (
            gain_one_grad,
            shift_one_grad,
            jnp.sum(grad_res, axis=(0, 1)),
            gain_two_grad,
            shift_two_grad,
            jnp.sum(grad_rows, axis=(0, 1)),
        ),
        ("ctx", "tp"),
    )
    qkv_grad, qvb_grad, outw_grad, fc_grad, fcb_grad, proj_grad = (
        lax.psum(qkv_grad.astype(jnp.bfloat16), "ctx").astype(jnp.float32),
        lax.psum(qvb_grad.astype(jnp.bfloat16), "ctx").astype(jnp.float32),
        lax.psum(outw_grad.astype(jnp.bfloat16), "ctx").astype(jnp.float32),
        lax.psum(fc_grad.astype(jnp.bfloat16), "ctx").astype(jnp.float32),
        lax.psum(fcb_grad.astype(jnp.bfloat16), "ctx").astype(jnp.float32),
        lax.psum(proj_grad.astype(jnp.bfloat16), "ctx").astype(jnp.float32),
    )
    return (
        layer_out,
        grad_tokens,
        small_sums[0],
        small_sums[1],
        qkv_grad,
        qvb_grad,
        outw_grad,
        small_sums[2],
        small_sums[3],
        small_sums[4],
        fc_grad,
        fcb_grad,
        proj_grad,
        small_sums[5],
    )


bf16 = jnp.bfloat16
f32 = jnp.float32
BLK = 512
PAIR = 2 * HEAD_DIM
DOC_FAR = -(2.0**100)
CAUSAL_FAR = -2e30

TP_CORE = [(i, i ^ 1) for i in range(4)]
TP_ROW = [(i, i ^ 2) for i in range(4)]
CTX_X = [(i, i ^ 1) for i in range(8)]
CTX_Z1 = [(i, i ^ 2) for i in range(8)]
CTX_Z2 = [(i, i ^ 4) for i in range(8)]
CTX_PLANES = [[0, 2, 4, 6], [1, 3, 5, 7]]


def tie(*values):
    return lax.optimization_barrier(values)


def contract(a, b, dims):
    return lax.dot_general(a, b, (dims, ((), ())), preferred_element_type=f32)


def head_pair(packed, part):
    low = part * HEAD_DIM
    high = (part + 3) * HEAD_DIM
    return jnp.concatenate(
        [packed[:, low : low + HEAD_DIM], packed[:, high : high + HEAD_DIM]], axis=1
    )


def lane_half(rows, head):
    lanes = lax.broadcasted_iota(jnp.int32, (rows, PAIR), 1)
    return (lanes >= HEAD_DIM) if head else (lanes < HEAD_DIM)


def attend_kernel(
    first_ref, mine_ref, other_ref, qdoc_ref, kdoc_ref, bias_ref,
    out_mine_ref, out_other_ref, exact_ref, log_ref, key_ref, value_ref, best_ref, total_ref, acc_ref,
):
    i = pl.program_id(0)
    half = BLK // 2
    block = pl.ds(pl.multiple_of(i * BLK, BLK), BLK)
    packed = jnp.concatenate([mine_ref[...], other_ref[...]], axis=0)
    queries = head_pair(packed, 0) * jnp.asarray(HEAD_DIM**-0.5, bf16)
    key_ref[block, :PAIR] = head_pair(packed, 1)
    key_ref[block, PAIR:] = kdoc_ref[...]
    value_ref[block, :] = head_pair(packed, 2)
    qdoc = qdoc_ref[...]
    query_heads = [
        jnp.concatenate([jnp.where(lane_half(BLK, h), queries, jnp.zeros_like(queries)), qdoc], axis=1)
        for h in range(2)
    ]
    best_ref[...] = jnp.full_like(best_ref, neg_fill)
    total_ref[...] = jnp.zeros_like(total_ref)
    acc_ref[...] = jnp.zeros_like(acc_ref)

    def visit(j, bias):
        keys = pl.ds(pl.multiple_of(j * BLK, BLK), BLK)
        key_block = key_ref[keys, :]
        value_block = value_ref[keys, :]
        for h in range(2):
            scores = contract(key_block, query_heads[h], ((1,), (1,)))
            if bias is not None:
                scores = scores + bias.astype(f32)
            old = best_ref[h : h + 1, :]
            new = jnp.maximum(old, jnp.max(scores, axis=0, keepdims=True))
            weights = jnp.exp(scores - new)
            fade = jnp.exp(old - new)
            total_ref[h : h + 1, :] = total_ref[h : h + 1, :] * fade + jnp.sum(
                weights, axis=0, keepdims=True
            )
            product = contract(value_block, weights.astype(bf16), ((0,), (0,)))
            part = slice(h * HEAD_DIM, (h + 1) * HEAD_DIM)
            acc_ref[part, :] = acc_ref[part, :] * fade + product[part, :]
            best_ref[h : h + 1, :] = new

    def step(j, carry):
        visit(j, None)
        return carry

    lax.fori_loop(first_ref[i], i, step, 0)
    visit(i, bias_ref[...])
    for h in range(2):
        part = slice(h * HEAD_DIM, (h + 1) * HEAD_DIM)
        acc_ref[part, :] = acc_ref[part, :] / total_ref[h : h + 1, :]
        log_ref[h : h + 1, :] = best_ref[h : h + 1, :] + jnp.log(total_ref[h : h + 1, :])
    mixed = acc_ref[...]
    exact_ref[...] = mixed
    low = jnp.transpose(mixed).astype(bf16)
    out_mine_ref[...] = low[:half]
    out_other_ref[...] = low[half:]


def attend_back_kernel(
    first_ref, mine_ref, other_ref, qdoc_ref, kdoc_ref, bias_ref, exact_ref, log_ref, dmine_ref, dother_ref,
    out_mine_ref, out_other_ref, key_ref, value_ref, dkey_ref, dvalue_ref, dquery_ref, dquery_all_ref,
):
    i = pl.program_id(0)
    half = BLK // 2
    block = pl.ds(pl.multiple_of(i * BLK, BLK), BLK)
    packed = jnp.concatenate([mine_ref[...], other_ref[...]], axis=0)
    scale = HEAD_DIM**-0.5
    queries = head_pair(packed, 0) * jnp.asarray(scale, bf16)
    key_ref[block, :PAIR] = head_pair(packed, 1)
    key_ref[block, PAIR:] = kdoc_ref[...]
    value_ref[block, :] = head_pair(packed, 2)
    dkey_ref[block, :] = jnp.zeros((BLK, PAIR), f32)
    dvalue_ref[block, :] = jnp.zeros((BLK, PAIR), f32)
    dquery_ref[...] = jnp.zeros_like(dquery_ref)
    dmixed = jnp.concatenate([dmine_ref[...], dother_ref[...]], axis=0)
    qdoc = qdoc_ref[...]
    masked = [jnp.where(lane_half(BLK, h), queries, jnp.zeros_like(queries)) for h in range(2)]
    dmasked = [jnp.where(lane_half(BLK, h), dmixed, jnp.zeros_like(dmixed)) for h in range(2)]
    query_heads = [jnp.concatenate([masked[h], qdoc], axis=1) for h in range(2)]
    product = jnp.transpose(dmixed.astype(f32)) * exact_ref[...]
    deltas = [
        jnp.sum(product[h * HEAD_DIM : (h + 1) * HEAD_DIM, :], axis=0, keepdims=True) for h in range(2)
    ]
    logs = [log_ref[h : h + 1, :] for h in range(2)]

    def visit(j, bias):
        keys = pl.ds(pl.multiple_of(j * BLK, BLK), BLK)
        key_block = key_ref[keys, :]
        value_block = value_ref[keys, :]
        dkey = dkey_ref[keys, :]
        dvalue = dvalue_ref[keys, :]
        for h in range(2):
            scores = contract(key_block, query_heads[h], ((1,), (1,)))
            if bias is not None:
                scores = scores + bias.astype(f32)
            weights = jnp.exp(scores - logs[h])
            dweights = contract(value_block, dmasked[h], ((1,), (1,)))
            dscores = (weights * (dweights - deltas[h])).astype(bf16)
            dvalue = dvalue + contract(weights.astype(bf16), dmasked[h], ((1,), (0,)))
            dkey = dkey + contract(dscores, masked[h], ((1,), (0,)))
            part = slice(h * HEAD_DIM, (h + 1) * HEAD_DIM)
            turned = contract(key_block[:, :PAIR], dscores, ((0,), (0,)))
            dquery_ref[part, :] = dquery_ref[part, :] + turned[part, :]
        dkey_ref[keys, :] = dkey
        dvalue_ref[keys, :] = dvalue

    def step(j, carry):
        visit(j, None)
        return carry

    lax.fori_loop(first_ref[i], i, step, 0)
    visit(i, bias_ref[...])
    dquery_all_ref[block, :] = jnp.transpose(dquery_ref[...] * scale)

    @pl.when(i == pl.num_programs(0) - 1)
    def _():
        for b in range(4):
            for side, out in ((0, out_mine_ref), (1, out_other_ref)):
                source = slice(b * BLK + side * half, b * BLK + (side + 1) * half)
                target = slice(b * half, (b + 1) * half)
                grads = [ref[source, :] for ref in (dquery_all_ref, dkey_ref, dvalue_ref)]
                out[target, :] = jnp.concatenate(
                    [g[:, h * HEAD_DIM : (h + 1) * HEAD_DIM] for h in range(2) for g in grads], axis=1
                ).astype(bf16)


def whole(shape):
    return pl.BlockSpec(shape, lambda i: (0,) * len(shape))


def down(rows, cols):
    return pl.BlockSpec((rows, cols), lambda i: (i, 0))


def along(rows, cols):
    return pl.BlockSpec((rows, cols), lambda i: (0, i))


def attend(first, mine, other, qdoc, kdoc, bias):
    length = qdoc.shape[0]
    half = length // 2
    return pl.pallas_call(
        attend_kernel,
        grid=(length // BLK,),
        in_specs=[
            pl.BlockSpec(memory_space=pltpu.SMEM),
            down(BLK // 2, 3 * PAIR), down(BLK // 2, 3 * PAIR), down(BLK, PAIR), down(BLK, PAIR),
            whole(bias.shape),
        ],
        out_specs=[down(BLK // 2, PAIR), down(BLK // 2, PAIR), along(PAIR, BLK), along(2, BLK)],
        out_shape=[
            jax.ShapeDtypeStruct((half, PAIR), bf16),
            jax.ShapeDtypeStruct((half, PAIR), bf16),
            jax.ShapeDtypeStruct((PAIR, length), f32),
            jax.ShapeDtypeStruct((2, length), f32),
        ],
        scratch_shapes=[
            pltpu.VMEM((length, 2 * PAIR), bf16),
            pltpu.VMEM((length, PAIR), bf16),
            pltpu.VMEM((2, BLK), f32),
            pltpu.VMEM((2, BLK), f32),
            pltpu.VMEM((PAIR, BLK), f32),
        ],
        compiler_params=pltpu.CompilerParams(
            dimension_semantics=("arbitrary",), vmem_limit_bytes=40 << 20
        ),
        name="attend",
    )(first, mine, other, qdoc, kdoc, bias)


def attend_back(first, mine, other, qdoc, kdoc, bias, exact, log_total, dmine, dother):
    length = qdoc.shape[0]
    half = length // 2
    operands = (mine, other, qdoc, kdoc, bias, exact, log_total, dmine, dother)
    return pl.pallas_call(
        attend_back_kernel,
        grid=(length // BLK,),
        in_specs=[
            pl.BlockSpec(memory_space=pltpu.SMEM),
            down(BLK // 2, 3 * PAIR), down(BLK // 2, 3 * PAIR), down(BLK, PAIR), down(BLK, PAIR),
            whole(bias.shape), along(PAIR, BLK), along(2, BLK), down(BLK // 2, PAIR), down(BLK // 2, PAIR),
        ],
        out_specs=[whole((half, 3 * PAIR)), whole((half, 3 * PAIR))],
        out_shape=[jax.ShapeDtypeStruct((half, 3 * PAIR), bf16)] * 2,
        scratch_shapes=[
            pltpu.VMEM((length, 2 * PAIR), bf16),
            pltpu.VMEM((length, PAIR), bf16),
            pltpu.VMEM((length, PAIR), f32),
            pltpu.VMEM((length, PAIR), f32),
            pltpu.VMEM((PAIR, BLK), f32),
            pltpu.VMEM((length, PAIR), f32),
        ],
        compiler_params=pltpu.CompilerParams(
            dimension_semantics=("arbitrary",), vmem_limit_bytes=48 << 20
        ),
        name="attend_back",
    )(first, *operands)


def planes_swap(values):
    return lax.all_to_all(values, "ctx", 0, 0, axis_index_groups=CTX_PLANES, tiled=False)


def tp_gather(values):
    core = lax.ppermute(values, "tp", TP_CORE)
    row = lax.ppermute(values, "tp", TP_ROW)
    both = lax.ppermute(row, "tp", TP_CORE)
    return [values, core, row, both]


def tp_gather_rows(values):
    return jnp.stack(tp_gather(values), axis=1)


def tp_scatter_rows(make_part, meanwhile):
    away = jnp.stack([make_part(3), make_part(1)]).astype(bf16)
    came = lax.ppermute(away, "tp", TP_CORE)
    across = (make_part(2) + came[0].astype(f32)).astype(bf16)
    across, filler = meanwhile(across)
    arrived = lax.ppermute(across, "tp", TP_ROW)
    own, filler = tie(make_part(0) + came[1].astype(f32), filler)
    return own + arrived.astype(f32), filler


def tp_swap(pieces):
    return [
        pieces[0],
        lax.ppermute(pieces[1], "tp", TP_CORE),
        lax.ppermute(pieces[2], "tp", TP_ROW),
        lax.ppermute(pieces[3], "tp", [(i, i ^ 3) for i in range(4)]),
    ]


def sum_ctx(values):
    for perm in (CTX_X, CTX_Z1, CTX_Z2):
        values = values + lax.ppermute(values, "ctx", perm)
    return values


def sum_tp(values):
    for perm in (TP_CORE, TP_ROW):
        values = values + lax.ppermute(values, "tp", perm)
    return values


def sum_all(values):
    return sum_ctx(sum_tp(values))


def norm_stats(values):
    centred = values - jnp.mean(values, axis=-1, keepdims=True)
    rate = lax.rsqrt(jnp.mean(centred * centred, axis=-1, keepdims=True) + eps)
    return centred * rate, rate


def norm_back(hat, rate, gain, grad):
    dhat = grad * gain
    return rate * (
        dhat
        - jnp.mean(dhat, axis=-1, keepdims=True)
        - hat * jnp.mean(dhat * hat, axis=-1, keepdims=True)
    )


def order_pair(values, swapped, axis):
    first, second = jnp.split(values, 2, axis=axis)
    return jnp.where(
        swapped,
        jnp.concatenate([second, first], axis=axis),
        jnp.concatenate([first, second], axis=axis),
    )


def shards(
    tokens,
    gain_one,
    shift_one,
    query_key_value_weight,
    qv_bias,
    attention_out_weight,
    attention_out_bias,
    gain_two,
    shift_two,
    expand_weight,
    expand_bias,
    contract_weight,
    contract_bias,
    doc_ids,
    out_grad,
):
    width = tokens.shape[2]
    span = doc_ids.shape[1]
    piece = tokens.shape[1]
    planes = tokens.shape[0]
    here = planes * piece
    group = here * 4
    ctx_at = lax.axis_index("ctx")
    tp_at = lax.axis_index("tp")
    side = ctx_at % 2
    plane = ctx_at // 2
    swapped = side == 1
    gain_first, shift_first = gain_one.astype(f32), shift_one.astype(f32)
    gain_second, shift_second = gain_two.astype(f32), shift_two.astype(f32)

    inputs = planes_swap(tokens).astype(f32)

    qkv_rel = jnp.transpose(query_key_value_weight, (1, 2, 0)).reshape(12 * HEAD_DIM, width)
    qkv_rel = order_pair(qkv_rel, swapped, 0)
    zero_key = jnp.zeros((4, HEAD_DIM), f32)
    bias_all = qv_bias.astype(f32)
    bias_rel = jnp.concatenate([bias_all[:, :HEAD_DIM], zero_key, bias_all[:, HEAD_DIM:]], axis=1)
    bias_rel = order_pair(bias_rel.reshape(12 * HEAD_DIM), swapped, 0)
    out_rel = order_pair(attention_out_weight.reshape(4 * HEAD_DIM, width), swapped, 0)
    hat_one, rate_one = norm_stats(inputs)
    rows_one = tp_gather_rows((hat_one * gain_first + shift_first).astype(bf16)).reshape(group, width)

    rows_one, out_rel = tie(rows_one, out_rel)

    def project(j):
        part = slice(j * 6 * HEAD_DIM, (j + 1) * 6 * HEAD_DIM)
        return (contract(rows_one, qkv_rel[part], ((1,), (1,))) + bias_rel[part]).astype(bf16)

    qkv_away, out_grad, doc_ids = tie(project(1), out_grad, doc_ids)
    qkv_other = lax.ppermute(qkv_away, "ctx", CTX_X)
    qkv_mine = project(0)

    ids = planes_swap(doc_ids)
    ids = jnp.stack([ids, lax.ppermute(ids, "ctx", CTX_X)], axis=1).reshape(planes, 2, 2, 2, piece)
    ids = jnp.where(tp_at % 2 == 1, jnp.flip(ids, 3), ids)
    ids = jnp.where(tp_at // 2 == 1, jnp.flip(ids, 2), ids).reshape(planes, 2 * span)
    low_id, high_id = jnp.min(ids, axis=1), jnp.max(ids, axis=1)
    first_block = jnp.sum((high_id[None, :] < low_id[:, None]).astype(jnp.int32), axis=1)
    lanes = jnp.arange(PAIR, dtype=jnp.int32)
    same = ids.reshape(-1, 1) == lanes[None, :]
    kdoc = same.astype(bf16)
    qdoc = jnp.where(same, 0.0, DOC_FAR).astype(bf16)
    place = (
        ((side ^ jnp.arange(2, dtype=jnp.int32)) * span)[:, None, None]
        + ((tp_at ^ jnp.arange(4, dtype=jnp.int32)) * piece)[None, :, None]
        + jnp.arange(piece, dtype=jnp.int32)[None, None, :]
    ).reshape(-1)
    bias = jnp.where(place[:, None] <= place[None, :], 0.0, CAUSAL_FAR).astype(bf16)

    grad_rows = planes_swap(out_grad)
    out_full = tp_gather(out_rel)
    grad_gathered = tp_gather_rows(grad_rows).reshape(group, width)
    grad_rows = grad_rows.astype(f32)
    act_grad = contract(grad_gathered, contract_weight, ((1,), (1,)))

    mixed_mine, mixed_other, exact, log_total = attend(
        first_block, qkv_mine, qkv_other, qdoc, kdoc, bias
    )
    mixed_arrived = lax.ppermute(mixed_other, "ctx", CTX_X)
    mixed_arrived, rows_one = tie(mixed_arrived, rows_one)
    mixed_heads = jnp.concatenate([mixed_mine, mixed_arrived], axis=1)
    rows_one_x = lax.ppermute(rows_one, "ctx", CTX_X)
    by_tp = mixed_heads.reshape(planes, 4, piece, 2 * PAIR)
    mixed_pieces = tp_swap([by_tp[:, k] for k in range(4)])
    attn_branch = sum(
        contract(mixed_pieces[k].reshape(here, 2 * PAIR), out_full[k], ((1,), (0,))) for k in range(4)
    ).reshape(planes, piece, width)
    residual_one = inputs + attn_branch + attention_out_bias.astype(f32)

    hat_two, rate_two = norm_stats(residual_one)
    rows_two = tp_gather_rows((hat_two * gain_second + shift_second).astype(bf16)).reshape(group, width)
    pre_act = jnp.dot(rows_two, expand_weight, preferred_element_type=f32) + expand_bias.astype(f32)
    active, pull_gelu = jax.vjp(gelu_tanh, pre_act)
    active = active.astype(bf16)
    dpre = pull_gelu(act_grad)[0].astype(bf16)
    fc_grad = contract(rows_two, dpre, ((0,), (0,))).astype(bf16)
    proj_grad = contract(active, grad_gathered, ((0,), (0,))).astype(bf16)
    fc_grad, proj_grad, dpre = tie(fc_grad, proj_grad, dpre)
    dpre_parts = dpre.reshape(planes, 4, piece, -1)
    dnormed_two, _ = tp_scatter_rows(
        lambda k: contract(
            dpre_parts[:, k].reshape(here, -1), expand_weight, ((1,), (1,))
        ).reshape(planes, piece, width),
        lambda sent: (sent, ()),
    )
    fcb_grad = jnp.sum(dpre, axis=0, dtype=f32)
    proj_grad, fc_grad = lax.psum((proj_grad, fc_grad), "ctx")

    grad_res = grad_rows + norm_back(hat_two, rate_two, gain_second, dnormed_two)
    attn_grad = grad_res.astype(bf16)
    attn_rows = attn_grad.reshape(here, width)
    dmixed = tp_swap(
        [
            contract(attn_rows, out_full[k], ((1,), (1,))).astype(bf16).reshape(planes, piece, 2 * PAIR)
            for k in range(4)
        ]
    )
    dmixed = jnp.stack(dmixed, axis=1).reshape(group, 2 * PAIR)
    dmixed, attn_grad, active = tie(dmixed, attn_grad, active)
    dmixed_other = lax.ppermute(dmixed[:, PAIR:], "ctx", CTX_X)
    grad_mine, grad_other = attend_back(
        first_block, qkv_mine, qkv_other, qdoc, kdoc, bias, exact, log_total, dmixed[:, :PAIR], dmixed_other
    )
    grad_mine, grad_other, mixed_heads = tie(grad_mine, grad_other, mixed_heads)
    packed_grad = jnp.concatenate([grad_mine, lax.ppermute(grad_other, "ctx", CTX_X)], axis=1)

    branch_in = active.reshape(planes, 4, piece, -1)
    feedforward_branch, _ = tp_scatter_rows(
        lambda k: jnp.dot(
            branch_in[:, k].reshape(here, -1), contract_weight, preferred_element_type=f32
        ).reshape(planes, piece, width),
        lambda sent: (sent, ()),
    )
    layer_low = (residual_one + feedforward_branch + contract_bias.astype(f32)).astype(bf16)

    attn_grad_rows = tp_gather_rows(attn_grad).reshape(group, width)
    outw = contract(mixed_heads, attn_grad_rows, ((0,), (0,)))
    outw_came = lax.ppermute(outw[PAIR:].astype(bf16), "ctx", CTX_X)
    qkv_part = contract(grad_mine, rows_one, ((0,), (0,))) + contract(grad_other, rows_one_x, ((0,), (0,)))
    outw_part = outw[:PAIR] + outw_came.astype(f32)
    parts = jnp.concatenate([qkv_part.astype(bf16), outw_part.astype(bf16)], axis=0)

    packed_parts = packed_grad.reshape(planes, 4, piece, 6 * PAIR)
    dnormed_one, parts = tp_scatter_rows(
        lambda k: jnp.dot(
            packed_parts[:, k].reshape(here, -1), qkv_rel, preferred_element_type=f32
        ).reshape(planes, piece, width),
        lambda sent: tie(sent, parts),
    )
    parts = parts.reshape(4, PAIR, width)
    moves = [[(i, i ^ (2 * d)) for i in range(8)] for d in range(4)]
    came = [
        lax.ppermute(lax.dynamic_index_in_dim(parts, plane ^ d, 0, keepdims=False), "ctx", moves[d])
        for d in range(1, 4)
    ]
    own = lax.dynamic_index_in_dim(parts, plane, 0, keepdims=False)
    grad_tokens = grad_res + norm_back(hat_one, rate_one, gain_first, dnormed_one)
    grad_tokens = planes_swap(grad_tokens.astype(bf16))
    grad_tokens, layer_low, own, came = tie(grad_tokens, layer_low, own, came)
    grad_tokens = grad_tokens.astype(f32)
    total = (own.astype(f32) + sum(c.astype(f32) for c in came)).astype(bf16)
    layer_out = planes_swap(layer_low)

    wide = jnp.zeros((2, 4, PAIR, width), bf16)
    for d in range(4):
        near = total if d == 0 else lax.ppermute(total, "ctx", moves[d])
        far = lax.ppermute(near, "ctx", CTX_X)
        wide = lax.dynamic_update_slice(wide, near[None, None], (side, plane ^ d, 0, 0))
        wide = lax.dynamic_update_slice(wide, far[None, None], (1 - side, plane ^ d, 0, 0))
    qkv_grad = wide[:, :3].astype(f32).reshape(4, 3 * HEAD_DIM, width)
    qkv_grad = jnp.transpose(qkv_grad, (2, 0, 1))
    outw_grad = wide[:, 3].astype(f32)
    small = sum_tp(
        jnp.stack(
            [
                jnp.sum(dnormed_one * hat_one, axis=(0, 1)),
                jnp.sum(dnormed_one, axis=(0, 1)),
                jnp.sum(grad_res, axis=(0, 1)),
                jnp.sum(dnormed_two * hat_two, axis=(0, 1)),
                jnp.sum(dnormed_two, axis=(0, 1)),
                jnp.sum(grad_rows, axis=(0, 1)),
            ]
        )
    )
    bias_sums = jnp.sum(packed_grad, axis=0, dtype=f32)[None]
    bias_sums = order_pair(bias_sums, swapped, 1)
    bias_sums = jnp.pad(bias_sums, ((0, 0), (0, width - 12 * HEAD_DIM)))
    small = sum_ctx(jnp.concatenate([small, fcb_grad[None], bias_sums]))
    bias_sums = small[7, : 12 * HEAD_DIM].reshape(4, 3, HEAD_DIM)
    qvb_grad = jnp.concatenate([bias_sums[:, 0], bias_sums[:, 2]], axis=-1)
    return (
        layer_out,
        grad_tokens,
        small[0],
        small[1],
        qkv_grad,
        qvb_grad,
        outw_grad.reshape(4, HEAD_DIM, width),
        small[2],
        small[3],
        small[4],
        fc_grad.astype(f32),
        small[6],
        proj_grad.astype(f32),
        small[5],
    )


def solution(mesh):
    sizes = dict(zip(mesh.axis_names, mesh.devices.shape))
    body = shards if (sizes["ctx"], sizes["tp"]) == (8, 4) else shards_plain
    return jax.shard_map(
        body,
        mesh=mesh,
        in_specs=(
            P(None, ("ctx", "tp"), None),
            P(),
            P(),
            P(None, "tp", None),
            P("tp", None),
            P("tp", None, None),
            P(),
            P(),
            P(),
            P(None, "tp"),
            P("tp"),
            P("tp", None),
            P(),
            P(None, "ctx"),
            P(None, ("ctx", "tp"), None),
        ),
        out_specs=(
            P(None, ("ctx", "tp"), None),
            P(None, ("ctx", "tp"), None),
            P(),
            P(),
            P(None, "tp", None),
            P("tp", None),
            P("tp", None, None),
            P(),
            P(),
            P(),
            P(None, "tp"),
            P("tp"),
            P("tp", None),
            P(),
        ),
        check_vma=False,
    )
```

```python
import jax
import jax.numpy as jnp
from jax import lax
from jax.experimental import pallas as pl
from jax.experimental.pallas import tpu as pltpu
from jax.sharding import PartitionSpec as P

HEAD_DIM = 64


eps = 1e-05
neg_fill = -1e30


def layer_norm(values, gain, shift):
    centre = jnp.mean(values, axis=-1, keepdims=True)
    centred = values - centre
    spread = jnp.mean(centred * centred, axis=-1, keepdims=True)
    return centred * lax.rsqrt(spread + eps) * gain + shift


def gelu_tanh(values):
    return jax.nn.gelu(values, approximate=True)


def gather_attn(values):
    return lax.all_gather(values, "tp", axis=1, tiled=True)


def reduce_attn(values):
    return lax.psum_scatter(
        values.astype(jnp.bfloat16), "tp", scatter_dimension=1, tiled=True
    ).astype(jnp.float32)


def gather_mlp(values):
    return lax.all_gather(values, "tp", axis=1, tiled=True)


def reduce_mlp(values):
    return lax.psum_scatter(
        values.astype(jnp.bfloat16), "tp", scatter_dimension=1, tiled=True
    ).astype(jnp.float32)


def feed_forward(normed_rows, fc_full, fcb_full, proj_full, grad_in):
    pre_activation = jnp.einsum(
        "scd,df->scf", normed_rows, fc_full, preferred_element_type=jnp.float32
    ) + fcb_full.astype(jnp.float32)
    active_rows = gelu_tanh(pre_activation).astype(jnp.bfloat16)
    branch_part = jnp.einsum(
        "scf,fd->scd", active_rows, proj_full, preferred_element_type=jnp.float32
    )
    act_grad = jnp.einsum("scd,fd->scf", grad_in, proj_full, preferred_element_type=jnp.float32)
    pre_grad = jax.vjp(gelu_tanh, pre_activation)[1](act_grad)[0].astype(jnp.bfloat16)
    proj_grad = jnp.einsum("scf,scd->fd", active_rows, grad_in, preferred_element_type=jnp.float32)
    fc_grad = jnp.einsum("scd,scf->df", normed_rows, pre_grad, preferred_element_type=jnp.float32)
    fcb_grad = jnp.sum(pre_grad, axis=(0, 1), dtype=jnp.float32)
    normed_grad = jnp.einsum("scf,df->scd", pre_grad, fc_full, preferred_element_type=jnp.float32)
    return (branch_part, normed_grad, fc_grad, fcb_grad, proj_grad)


def shards_plain(
    tokens,
    gain_one,
    shift_one,
    query_key_value_weight,
    qv_bias,
    attention_out_weight,
    attention_out_bias,
    gain_two,
    shift_two,
    expand_weight,
    expand_bias,
    contract_weight,
    contract_bias,
    doc_ids,
    out_grad,
):
    score_scale = HEAD_DIM ** (-0.5)
    seq_count = tokens.shape[0]
    span_rows = doc_ids.shape[1]
    heads_here = query_key_value_weight.shape[1]
    full_length = span_rows * lax.axis_size("ctx")
    first_query = lax.axis_index("ctx") * span_rows
    query_pos = first_query + jnp.arange(span_rows, dtype=jnp.int32)
    last_query = first_query + span_rows - 1
    all_ids = lax.all_gather(doc_ids, "ctx", axis=1, tiled=True)

    def allowed_mask(offset, block_width):
        key_pos = offset + jnp.arange(block_width, dtype=jnp.int32)
        key_ids = lax.dynamic_slice_in_dim(all_ids, offset, block_width, 1)
        causal = key_pos[None, :] <= query_pos[:, None]
        same_doc = doc_ids[:, :, None] == key_ids[:, None, :]
        return jnp.logical_and(causal[None], same_doc)[:, None]

    def keep_state(carry_state):
        return carry_state

    gain_first = gain_one.astype(jnp.float32)
    shift_first = shift_one.astype(jnp.float32)
    gain_second = gain_two.astype(jnp.float32)
    shift_second = shift_two.astype(jnp.float32)
    inputs = tokens.astype(jnp.float32)
    first_normed = layer_norm(inputs, gain_first, shift_first)
    rows_one = gather_attn(first_normed.astype(jnp.bfloat16))
    packed_values = jnp.einsum(
        "scd,dhe->sche", rows_one, query_key_value_weight, preferred_element_type=jnp.float32
    )
    bias_pair = qv_bias.astype(jnp.float32)
    queries = (packed_values[..., :HEAD_DIM] + bias_pair[:, :HEAD_DIM]).astype(jnp.bfloat16)
    keys_here = packed_values[..., HEAD_DIM : 2 * HEAD_DIM].astype(jnp.bfloat16)
    values_here = (packed_values[..., 2 * HEAD_DIM :] + bias_pair[:, HEAD_DIM:]).astype(
        jnp.bfloat16
    )
    key_value = jnp.concatenate([keys_here, values_here], axis=-1)
    start_state = (
        jnp.full((seq_count, heads_here, span_rows), neg_fill, jnp.float32),
        jnp.zeros((seq_count, heads_here, span_rows), jnp.float32),
        jnp.zeros((seq_count, heads_here, span_rows, HEAD_DIM), jnp.float32),
    )
    folded = start_state
    piece_rows = lax.all_gather(key_value, "ctx", axis=1, tiled=True)
    piece_len = piece_rows.shape[1]
    block_width = min(piece_len, span_rows)

    def attend_block(carry_state, block_index):
        offset = block_index * block_width

        def attend_compute(inner_state):
            row_best, row_total, weighted = inner_state
            one_block = lax.dynamic_slice_in_dim(
                piece_rows, block_index * block_width, block_width, 1
            )
            scores = (
                jnp.einsum(
                    "sqhe,skhe->shqk",
                    queries,
                    one_block[..., :HEAD_DIM],
                    preferred_element_type=jnp.float32,
                )
                * score_scale
            )
            allowed = allowed_mask(offset, block_width)
            row_top = jnp.max(jnp.where(allowed, scores, neg_fill), axis=-1)
            new_best = jnp.maximum(row_best, row_top)
            soft_terms = jnp.where(allowed, jnp.exp(scores - new_best[..., None]), 0.0)
            rescale = jnp.exp(row_best - new_best)
            row_total = row_total * rescale + jnp.sum(soft_terms, axis=-1)
            weighted = weighted * rescale[..., None] + jnp.einsum(
                "shqk,skhe->shqe",
                soft_terms.astype(jnp.bfloat16),
                one_block[..., HEAD_DIM:],
                preferred_element_type=jnp.float32,
            )
            return (new_best, row_total, weighted)

        return (lax.cond(offset <= last_query, attend_compute, keep_state, carry_state), None)

    folded, _ = lax.scan(
        attend_block, folded, jnp.arange(piece_len // block_width, dtype=jnp.int32)
    )
    row_best, row_total, weighted = folded
    mixed_exact = weighted / row_total[..., None]
    log_total = row_best + jnp.log(row_total)
    mixed_low = jnp.transpose(mixed_exact, (0, 2, 1, 3)).astype(jnp.bfloat16)
    attn_part = jnp.einsum(
        "sche,hed->scd", mixed_low, attention_out_weight, preferred_element_type=jnp.float32
    )
    residual_one = inputs + reduce_attn(attn_part) + attention_out_bias.astype(jnp.float32)
    second_normed = layer_norm(residual_one, gain_second, shift_second)
    normed_low = second_normed.astype(jnp.bfloat16)
    grad_rows = out_grad.astype(jnp.float32)
    grad_low = grad_rows.astype(jnp.bfloat16)
    rows_two = gather_mlp(normed_low)
    grad_gathered = gather_mlp(grad_low)
    branch_part, normed_grad, fc_grad, fcb_grad, proj_grad = feed_forward(
        rows_two, expand_weight, expand_bias, contract_weight, grad_gathered
    )
    feedforward_branch = reduce_mlp(branch_part)
    dnormed_two = reduce_mlp(normed_grad)
    layer_out = (residual_one + feedforward_branch + contract_bias.astype(jnp.float32)).astype(
        jnp.bfloat16
    )
    pull_two = jax.vjp(layer_norm, residual_one, gain_second, shift_second)[1]
    res_extra, gain_two_grad, shift_two_grad = pull_two(dnormed_two)
    grad_res = grad_rows + res_extra
    attn_grad_rows = gather_attn(grad_res.astype(jnp.bfloat16))
    dmixed = jnp.einsum(
        "scd,hed->sche", attn_grad_rows, attention_out_weight, preferred_element_type=jnp.float32
    ).astype(jnp.bfloat16)
    outw_grad = jnp.einsum(
        "sche,scd->hed", mixed_low, attn_grad_rows, preferred_element_type=jnp.float32
    )
    dmixed_heads = jnp.transpose(dmixed, (0, 2, 1, 3))
    row_delta = jnp.sum(dmixed_heads.astype(jnp.float32) * mixed_exact, axis=-1)
    back_start = (
        jnp.zeros((seq_count, heads_here, span_rows, HEAD_DIM), jnp.float32),
        jnp.zeros((seq_count, full_length, heads_here, 2 * HEAD_DIM), jnp.float32),
    )
    folded = back_start
    back_piece_rows = lax.all_gather(key_value, "ctx", axis=1, tiled=True)
    piece_len = back_piece_rows.shape[1]
    back_block_width = min(piece_len, span_rows)

    def back_block(carry_state, block_index):
        offset = block_index * back_block_width

        def back_compute(inner_state):
            query_grad, pair_grads = inner_state
            one_block = lax.dynamic_slice_in_dim(
                back_piece_rows, block_index * back_block_width, back_block_width, 1
            )
            keys_block = one_block[..., :HEAD_DIM]
            values_block = one_block[..., HEAD_DIM:]
            scores = (
                jnp.einsum(
                    "sqhe,skhe->shqk", queries, keys_block, preferred_element_type=jnp.float32
                )
                * score_scale
            )
            allowed = allowed_mask(offset, back_block_width)
            soft_terms = jnp.where(allowed, jnp.exp(scores - log_total[..., None]), 0.0)
            soft_grad = jnp.einsum(
                "shqe,skhe->shqk", dmixed_heads, values_block, preferred_element_type=jnp.float32
            )
            score_grad = (soft_terms * (soft_grad - row_delta[..., None])).astype(jnp.bfloat16)
            query_grad = query_grad + score_scale * jnp.einsum(
                "shqk,skhe->shqe", score_grad, keys_block, preferred_element_type=jnp.float32
            )
            key_grad = score_scale * jnp.einsum(
                "shqk,sqhe->skhe", score_grad, queries, preferred_element_type=jnp.float32
            )
            value_grad = jnp.einsum(
                "shqk,shqe->skhe",
                soft_terms.astype(jnp.bfloat16),
                dmixed_heads,
                preferred_element_type=jnp.float32,
            )
            earlier = lax.dynamic_slice_in_dim(pair_grads, offset, back_block_width, 1)
            pair_grads = lax.dynamic_update_slice_in_dim(
                pair_grads, earlier + jnp.concatenate([key_grad, value_grad], axis=-1), offset, 1
            )
            return (query_grad, pair_grads)

        return (lax.cond(offset <= last_query, back_compute, keep_state, carry_state), None)

    folded, _ = lax.scan(
        back_block, folded, jnp.arange(piece_len // back_block_width, dtype=jnp.int32)
    )
    query_grad, pair_grads = folded
    pair_mine = lax.psum_scatter(
        pair_grads.astype(jnp.bfloat16), "ctx", scatter_dimension=1, tiled=True
    )
    query_low = jnp.transpose(query_grad, (0, 2, 1, 3)).astype(jnp.bfloat16)
    packed_grad = jnp.concatenate([query_low, pair_mine], axis=-1)
    qkv_grad = jnp.einsum(
        "scd,sche->dhe", rows_one, packed_grad, preferred_element_type=jnp.float32
    )
    qvb_grad = jnp.concatenate(
        [
            jnp.sum(query_low, axis=(0, 1), dtype=jnp.float32),
            jnp.sum(pair_mine[..., HEAD_DIM:], axis=(0, 1), dtype=jnp.float32),
        ],
        axis=-1,
    )
    normed_one_grad = reduce_attn(
        jnp.einsum(
            "sche,dhe->scd", packed_grad, query_key_value_weight, preferred_element_type=jnp.float32
        )
    )
    pull_one = jax.vjp(layer_norm, inputs, gain_first, shift_first)[1]
    input_extra, gain_one_grad, shift_one_grad = pull_one(normed_one_grad)
    grad_tokens = grad_res + input_extra
    small_sums = lax.psum(
        (
            gain_one_grad,
            shift_one_grad,
            jnp.sum(grad_res, axis=(0, 1)),
            gain_two_grad,
            shift_two_grad,
            jnp.sum(grad_rows, axis=(0, 1)),
        ),
        ("ctx", "tp"),
    )
    qkv_grad, qvb_grad, outw_grad, fc_grad, fcb_grad, proj_grad = (
        lax.psum(qkv_grad.astype(jnp.bfloat16), "ctx").astype(jnp.float32),
        lax.psum(qvb_grad.astype(jnp.bfloat16), "ctx").astype(jnp.float32),
        lax.psum(outw_grad.astype(jnp.bfloat16), "ctx").astype(jnp.float32),
        lax.psum(fc_grad.astype(jnp.bfloat16), "ctx").astype(jnp.float32),
        lax.psum(fcb_grad.astype(jnp.bfloat16), "ctx").astype(jnp.float32),
        lax.psum(proj_grad.astype(jnp.bfloat16), "ctx").astype(jnp.float32),
    )
    return (
        layer_out,
        grad_tokens,
        small_sums[0],
        small_sums[1],
        qkv_grad,
        qvb_grad,
        outw_grad,
        small_sums[2],
        small_sums[3],
        small_sums[4],
        fc_grad,
        fcb_grad,
        proj_grad,
        small_sums[5],
    )


bf16 = jnp.bfloat16
f32 = jnp.float32
BLK = 512
PAIR = 2 * HEAD_DIM
DOC_FAR = -(2.0**100)
CAUSAL_FAR = -2e30

TP_CORE = [(i, i ^ 1) for i in range(4)]
TP_ROW = [(i, i ^ 2) for i in range(4)]
CTX_X = [(i, i ^ 1) for i in range(8)]
CTX_Z1 = [(i, i ^ 2) for i in range(8)]
CTX_Z2 = [(i, i ^ 4) for i in range(8)]
CTX_PLANES = [[0, 2, 4, 6], [1, 3, 5, 7]]


def tie(*values):
    return lax.optimization_barrier(values)


def contract(a, b, dims):
    return lax.dot_general(a, b, (dims, ((), ())), preferred_element_type=f32)


def head_pair(packed, part):
    low = part * HEAD_DIM
    high = (part + 3) * HEAD_DIM
    return jnp.concatenate(
        [packed[:, low : low + HEAD_DIM], packed[:, high : high + HEAD_DIM]], axis=1
    )


def lane_half(rows, head):
    lanes = lax.broadcasted_iota(jnp.int32, (rows, PAIR), 1)
    return (lanes >= HEAD_DIM) if head else (lanes < HEAD_DIM)


def attend_kernel(
    first_ref, mine_ref, other_ref, qdoc_ref, kdoc_ref, bias_ref,
    out_mine_ref, out_other_ref, exact_ref, log_ref, key_ref, value_ref, best_ref, total_ref, acc_ref,
):
    i = pl.program_id(0)
    half = BLK // 2
    block = pl.ds(pl.multiple_of(i * BLK, BLK), BLK)
    packed = jnp.concatenate([mine_ref[...], other_ref[...]], axis=0)
    queries = head_pair(packed, 0) * jnp.asarray(HEAD_DIM**-0.5, bf16)
    key_ref[block, :PAIR] = head_pair(packed, 1)
    key_ref[block, PAIR:] = kdoc_ref[...]
    value_ref[block, :] = head_pair(packed, 2)
    qdoc = qdoc_ref[...]
    query_heads = [
        jnp.concatenate([jnp.where(lane_half(BLK, h), queries, jnp.zeros_like(queries)), qdoc], axis=1)
        for h in range(2)
    ]
    best_ref[...] = jnp.full_like(best_ref, neg_fill)
    total_ref[...] = jnp.zeros_like(total_ref)
    acc_ref[...] = jnp.zeros_like(acc_ref)

    def visit(j, bias):
        keys = pl.ds(pl.multiple_of(j * BLK, BLK), BLK)
        key_block = key_ref[keys, :]
        value_block = value_ref[keys, :]
        for h in range(2):
            scores = contract(key_block, query_heads[h], ((1,), (1,)))
            if bias is not None:
                scores = scores + bias.astype(f32)
            old = best_ref[h : h + 1, :]
            new = jnp.maximum(old, jnp.max(scores, axis=0, keepdims=True))
            weights = jnp.exp(scores - new)
            fade = jnp.exp(old - new)
            total_ref[h : h + 1, :] = total_ref[h : h + 1, :] * fade + jnp.sum(
                weights, axis=0, keepdims=True
            )
            product = contract(value_block, weights.astype(bf16), ((0,), (0,)))
            part = slice(h * HEAD_DIM, (h + 1) * HEAD_DIM)
            acc_ref[part, :] = acc_ref[part, :] * fade + product[part, :]
            best_ref[h : h + 1, :] = new

    def step(j, carry):
        visit(j, None)
        return carry

    lax.fori_loop(first_ref[i], i, step, 0)
    visit(i, bias_ref[...])
    for h in range(2):
        part = slice(h * HEAD_DIM, (h + 1) * HEAD_DIM)
        acc_ref[part, :] = acc_ref[part, :] / total_ref[h : h + 1, :]
        log_ref[h : h + 1, :] = best_ref[h : h + 1, :] + jnp.log(total_ref[h : h + 1, :])
    mixed = acc_ref[...]
    exact_ref[...] = mixed
    low = jnp.transpose(mixed).astype(bf16)
    out_mine_ref[...] = low[:half]
    out_other_ref[...] = low[half:]


def attend_back_kernel(
    first_ref, mine_ref, other_ref, qdoc_ref, kdoc_ref, bias_ref, exact_ref, log_ref, dmine_ref, dother_ref,
    out_mine_ref, out_other_ref, key_ref, value_ref, dkey_ref, dvalue_ref, dquery_ref, dquery_all_ref,
):
    i = pl.program_id(0)
    half = BLK // 2
    block = pl.ds(pl.multiple_of(i * BLK, BLK), BLK)
    packed = jnp.concatenate([mine_ref[...], other_ref[...]], axis=0)
    scale = HEAD_DIM**-0.5
    queries = head_pair(packed, 0) * jnp.asarray(scale, bf16)
    key_ref[block, :PAIR] = head_pair(packed, 1)
    key_ref[block, PAIR:] = kdoc_ref[...]
    value_ref[block, :] = head_pair(packed, 2)
    dkey_ref[block, :] = jnp.zeros((BLK, PAIR), f32)
    dvalue_ref[block, :] = jnp.zeros((BLK, PAIR), f32)
    dquery_ref[...] = jnp.zeros_like(dquery_ref)
    dmixed = jnp.concatenate([dmine_ref[...], dother_ref[...]], axis=0)
    qdoc = qdoc_ref[...]
    masked = [jnp.where(lane_half(BLK, h), queries, jnp.zeros_like(queries)) for h in range(2)]
    dmasked = [jnp.where(lane_half(BLK, h), dmixed, jnp.zeros_like(dmixed)) for h in range(2)]
    query_heads = [jnp.concatenate([masked[h], qdoc], axis=1) for h in range(2)]
    product = jnp.transpose(dmixed.astype(f32)) * exact_ref[...]
    deltas = [
        jnp.sum(product[h * HEAD_DIM : (h + 1) * HEAD_DIM, :], axis=0, keepdims=True) for h in range(2)
    ]
    logs = [log_ref[h : h + 1, :] for h in range(2)]

    def visit(j, bias):
        keys = pl.ds(pl.multiple_of(j * BLK, BLK), BLK)
        key_block = key_ref[keys, :]
        value_block = value_ref[keys, :]
        dkey = dkey_ref[keys, :]
        dvalue = dvalue_ref[keys, :]
        for h in range(2):
            scores = contract(key_block, query_heads[h], ((1,), (1,)))
            if bias is not None:
                scores = scores + bias.astype(f32)
            weights = jnp.exp(scores - logs[h])
            dweights = contract(value_block, dmasked[h], ((1,), (1,)))
            dscores = (weights * (dweights - deltas[h])).astype(bf16)
            dvalue = dvalue + contract(weights.astype(bf16), dmasked[h], ((1,), (0,)))
            dkey = dkey + contract(dscores, masked[h], ((1,), (0,)))
            part = slice(h * HEAD_DIM, (h + 1) * HEAD_DIM)
            turned = contract(key_block[:, :PAIR], dscores, ((0,), (0,)))
            dquery_ref[part, :] = dquery_ref[part, :] + turned[part, :]
        dkey_ref[keys, :] = dkey
        dvalue_ref[keys, :] = dvalue

    def step(j, carry):
        visit(j, None)
        return carry

    lax.fori_loop(first_ref[i], i, step, 0)
    visit(i, bias_ref[...])
    dquery_all_ref[block, :] = jnp.transpose(dquery_ref[...] * scale)

    @pl.when(i == pl.num_programs(0) - 1)
    def _():
        for b in range(4):
            for side, out in ((0, out_mine_ref), (1, out_other_ref)):
                source = slice(b * BLK + side * half, b * BLK + (side + 1) * half)
                target = slice(b * half, (b + 1) * half)
                grads = [ref[source, :] for ref in (dquery_all_ref, dkey_ref, dvalue_ref)]
                out[target, :] = jnp.concatenate(
                    [g[:, h * HEAD_DIM : (h + 1) * HEAD_DIM] for h in range(2) for g in grads], axis=1
                ).astype(bf16)


def whole(shape):
    return pl.BlockSpec(shape, lambda i: (0,) * len(shape))


def down(rows, cols):
    return pl.BlockSpec((rows, cols), lambda i: (i, 0))


def along(rows, cols):
    return pl.BlockSpec((rows, cols), lambda i: (0, i))


def attend(first, mine, other, qdoc, kdoc, bias):
    length = qdoc.shape[0]
    half = length // 2
    return pl.pallas_call(
        attend_kernel,
        grid=(length // BLK,),
        in_specs=[
            pl.BlockSpec(memory_space=pltpu.SMEM),
            down(BLK // 2, 3 * PAIR), down(BLK // 2, 3 * PAIR), down(BLK, PAIR), down(BLK, PAIR),
            whole(bias.shape),
        ],
        out_specs=[down(BLK // 2, PAIR), down(BLK // 2, PAIR), along(PAIR, BLK), along(2, BLK)],
        out_shape=[
            jax.ShapeDtypeStruct((half, PAIR), bf16),
            jax.ShapeDtypeStruct((half, PAIR), bf16),
            jax.ShapeDtypeStruct((PAIR, length), f32),
            jax.ShapeDtypeStruct((2, length), f32),
        ],
        scratch_shapes=[
            pltpu.VMEM((length, 2 * PAIR), bf16),
            pltpu.VMEM((length, PAIR), bf16),
            pltpu.VMEM((2, BLK), f32),
            pltpu.VMEM((2, BLK), f32),
            pltpu.VMEM((PAIR, BLK), f32),
        ],
        compiler_params=pltpu.CompilerParams(
            dimension_semantics=("arbitrary",), vmem_limit_bytes=40 << 20
        ),
        name="attend",
    )(first, mine, other, qdoc, kdoc, bias)


def attend_back(first, mine, other, qdoc, kdoc, bias, exact, log_total, dmine, dother):
    length = qdoc.shape[0]
    half = length // 2
    operands = (mine, other, qdoc, kdoc, bias, exact, log_total, dmine, dother)
    return pl.pallas_call(
        attend_back_kernel,
        grid=(length // BLK,),
        in_specs=[
            pl.BlockSpec(memory_space=pltpu.SMEM),
            down(BLK // 2, 3 * PAIR), down(BLK // 2, 3 * PAIR), down(BLK, PAIR), down(BLK, PAIR),
            whole(bias.shape), along(PAIR, BLK), along(2, BLK), down(BLK // 2, PAIR), down(BLK // 2, PAIR),
        ],
        out_specs=[whole((half, 3 * PAIR)), whole((half, 3 * PAIR))],
        out_shape=[jax.ShapeDtypeStruct((half, 3 * PAIR), bf16)] * 2,
        scratch_shapes=[
            pltpu.VMEM((length, 2 * PAIR), bf16),
            pltpu.VMEM((length, PAIR), bf16),
            pltpu.VMEM((length, PAIR), f32),
            pltpu.VMEM((length, PAIR), f32),
            pltpu.VMEM((PAIR, BLK), f32),
            pltpu.VMEM((length, PAIR), f32),
        ],
        compiler_params=pltpu.CompilerParams(
            dimension_semantics=("arbitrary",), vmem_limit_bytes=48 << 20
        ),
        name="attend_back",
    )(first, *operands)


def planes_swap(values):
    return lax.all_to_all(values, "ctx", 0, 0, axis_index_groups=CTX_PLANES, tiled=False)


def tp_gather(values):
    core = lax.ppermute(values, "tp", TP_CORE)
    row = lax.ppermute(values, "tp", TP_ROW)
    both = lax.ppermute(row, "tp", TP_CORE)
    return [values, core, row, both]


def tp_gather_rows(values):
    return jnp.stack(tp_gather(values), axis=1)


def tp_scatter_rows(make_part, meanwhile):
    away = jnp.stack([make_part(3), make_part(1)]).astype(bf16)
    came = lax.ppermute(away, "tp", TP_CORE)
    across = (make_part(2) + came[0].astype(f32)).astype(bf16)
    across, filler = meanwhile(across)
    arrived = lax.ppermute(across, "tp", TP_ROW)
    own, filler = tie(make_part(0) + came[1].astype(f32), filler)
    return own + arrived.astype(f32), filler


def tp_swap(pieces):
    return [
        pieces[0],
        lax.ppermute(pieces[1], "tp", TP_CORE),
        lax.ppermute(pieces[2], "tp", TP_ROW),
        lax.ppermute(pieces[3], "tp", [(i, i ^ 3) for i in range(4)]),
    ]


def sum_ctx(values):
    for perm in (CTX_X, CTX_Z1, CTX_Z2):
        values = values + lax.ppermute(values, "ctx", perm)
    return values


def sum_tp(values):
    for perm in (TP_CORE, TP_ROW):
        values = values + lax.ppermute(values, "tp", perm)
    return values


def sum_all(values):
    return sum_ctx(sum_tp(values))


def norm_stats(values):
    centred = values - jnp.mean(values, axis=-1, keepdims=True)
    rate = lax.rsqrt(jnp.mean(centred * centred, axis=-1, keepdims=True) + eps)
    return centred * rate, rate


def norm_back(hat, rate, gain, grad):
    dhat = grad * gain
    return rate * (
        dhat
        - jnp.mean(dhat, axis=-1, keepdims=True)
        - hat * jnp.mean(dhat * hat, axis=-1, keepdims=True)
    )


def order_pair(values, swapped, axis):
    first, second = jnp.split(values, 2, axis=axis)
    return jnp.where(
        swapped,
        jnp.concatenate([second, first], axis=axis),
        jnp.concatenate([first, second], axis=axis),
    )


def shards(
    tokens,
    gain_one,
    shift_one,
    query_key_value_weight,
    qv_bias,
    attention_out_weight,
    attention_out_bias,
    gain_two,
    shift_two,
    expand_weight,
    expand_bias,
    contract_weight,
    contract_bias,
    doc_ids,
    out_grad,
):
    width = tokens.shape[2]
    span = doc_ids.shape[1]
    piece = tokens.shape[1]
    planes = tokens.shape[0]
    here = planes * piece
    group = here * 4
    ctx_at = lax.axis_index("ctx")
    tp_at = lax.axis_index("tp")
    side = ctx_at % 2
    plane = ctx_at // 2
    swapped = side == 1
    gain_first, shift_first = gain_one.astype(f32), shift_one.astype(f32)
    gain_second, shift_second = gain_two.astype(f32), shift_two.astype(f32)

    ids = jnp.pad(doc_ids.astype(bf16), ((0, 0), (0, width - span)))
    ids = jnp.broadcast_to(ids[:, None], (planes, 16, width))
    arrived = planes_swap(jnp.concatenate([tokens, ids], axis=1))
    inputs = arrived[:, :piece].astype(f32)
    ids = arrived[:, piece, :span]
    ids = jnp.stack([ids, lax.ppermute(ids, "ctx", CTX_X)], axis=1).astype(jnp.int32)

    qkv_rel = jnp.transpose(query_key_value_weight, (1, 2, 0)).reshape(12 * HEAD_DIM, width)
    qkv_rel = order_pair(qkv_rel, swapped, 0)
    zero_key = jnp.zeros((4, HEAD_DIM), f32)
    bias_all = qv_bias.astype(f32)
    bias_rel = jnp.concatenate([bias_all[:, :HEAD_DIM], zero_key, bias_all[:, HEAD_DIM:]], axis=1)
    bias_rel = order_pair(bias_rel.reshape(12 * HEAD_DIM), swapped, 0)
    out_rel = order_pair(attention_out_weight.reshape(4 * HEAD_DIM, width), swapped, 0)
    hat_one, rate_one = norm_stats(inputs)
    rows_one = tp_gather_rows((hat_one * gain_first + shift_first).astype(bf16)).reshape(group, width)

    rows_one, out_rel = tie(rows_one, out_rel)

    def project(rows, j):
        part = slice(j * 6 * HEAD_DIM, (j + 1) * 6 * HEAD_DIM)
        return (contract(rows, qkv_rel[part], ((1,), (1,))) + bias_rel[part]).astype(bf16)

    qkv_away, rows_one = tie(project(rows_one, 1), rows_one)
    qkv_other = lax.ppermute(qkv_away, "ctx", CTX_X)
    qkv_mine, out_grad = tie(project(rows_one, 0), out_grad)

    ids = ids.reshape(planes, 2, 2, 2, piece)
    ids = jnp.where(tp_at % 2 == 1, jnp.flip(ids, 3), ids)
    ids = jnp.where(tp_at // 2 == 1, jnp.flip(ids, 2), ids).reshape(planes, 2 * span)
    low_id, high_id = jnp.min(ids, axis=1), jnp.max(ids, axis=1)
    first_block = jnp.sum((high_id[None, :] < low_id[:, None]).astype(jnp.int32), axis=1)
    lanes = jnp.arange(PAIR, dtype=jnp.int32)
    same = ids.reshape(-1, 1) == lanes[None, :]
    kdoc = same.astype(bf16)
    qdoc = jnp.where(same, 0.0, DOC_FAR).astype(bf16)
    place = (
        ((side ^ jnp.arange(2, dtype=jnp.int32)) * span)[:, None, None]
        + ((tp_at ^ jnp.arange(4, dtype=jnp.int32)) * piece)[None, :, None]
        + jnp.arange(piece, dtype=jnp.int32)[None, None, :]
    ).reshape(-1)
    bias = jnp.where(place[:, None] <= place[None, :], 0.0, CAUSAL_FAR).astype(bf16)

    grad_rows = planes_swap(out_grad)
    out_full = tp_gather(out_rel)
    grad_gathered = tp_gather_rows(grad_rows).reshape(group, width)
    grad_rows = grad_rows.astype(f32)
    act_grad = contract(grad_gathered, contract_weight, ((1,), (1,)))

    mixed_mine, mixed_other, exact, log_total = attend(
        first_block, qkv_mine, qkv_other, qdoc, kdoc, bias
    )
    mixed_arrived = lax.ppermute(mixed_other, "ctx", CTX_X)
    mixed_arrived, rows_one = tie(mixed_arrived, rows_one)
    mixed_heads = jnp.concatenate([mixed_mine, mixed_arrived], axis=1)
    rows_one_x = lax.ppermute(rows_one, "ctx", CTX_X)
    by_tp = mixed_heads.reshape(planes, 4, piece, 2 * PAIR)
    mixed_pieces = tp_swap([by_tp[:, k] for k in range(4)])
    attn_branch = sum(
        contract(mixed_pieces[k].reshape(here, 2 * PAIR), out_full[k], ((1,), (0,))) for k in range(4)
    ).reshape(planes, piece, width)
    residual_one = inputs + attn_branch + attention_out_bias.astype(f32)

    hat_two, rate_two = norm_stats(residual_one)
    rows_two = tp_gather_rows((hat_two * gain_second + shift_second).astype(bf16)).reshape(group, width)
    pre_act = jnp.dot(rows_two, expand_weight, preferred_element_type=f32) + expand_bias.astype(f32)
    active, pull_gelu = jax.vjp(gelu_tanh, pre_act)
    active = active.astype(bf16)
    dpre = pull_gelu(act_grad)[0].astype(bf16)
    fc_grad = contract(rows_two, dpre, ((0,), (0,))).astype(bf16)
    proj_grad = contract(active, grad_gathered, ((0,), (0,))).astype(bf16)
    fc_grad, proj_grad, dpre = tie(fc_grad, proj_grad, dpre)
    dpre_parts = dpre.reshape(planes, 4, piece, -1)
    dnormed_two, _ = tp_scatter_rows(
        lambda k: contract(
            dpre_parts[:, k].reshape(here, -1), expand_weight, ((1,), (1,))
        ).reshape(planes, piece, width),
        lambda sent: (sent, ()),
    )
    fcb_grad = jnp.sum(dpre, axis=0, dtype=f32)
    proj_grad, fc_grad = lax.psum((proj_grad, fc_grad), "ctx")

    grad_res = grad_rows + norm_back(hat_two, rate_two, gain_second, dnormed_two)
    attn_grad = grad_res.astype(bf16)
    attn_rows = attn_grad.reshape(here, width)
    dmixed = tp_swap(
        [
            contract(attn_rows, out_full[k], ((1,), (1,))).astype(bf16).reshape(planes, piece, 2 * PAIR)
            for k in range(4)
        ]
    )
    dmixed = jnp.stack(dmixed, axis=1).reshape(group, 2 * PAIR)
    dmixed, attn_grad, active = tie(dmixed, attn_grad, active)
    dmixed_other = lax.ppermute(dmixed[:, PAIR:], "ctx", CTX_X)
    grad_mine, grad_other = attend_back(
        first_block, qkv_mine, qkv_other, qdoc, kdoc, bias, exact, log_total, dmixed[:, :PAIR], dmixed_other
    )
    grad_mine, grad_other, mixed_heads = tie(grad_mine, grad_other, mixed_heads)
    packed_grad = jnp.concatenate([grad_mine, lax.ppermute(grad_other, "ctx", CTX_X)], axis=1)

    branch_in = active.reshape(planes, 4, piece, -1)
    feedforward_branch, _ = tp_scatter_rows(
        lambda k: jnp.dot(
            branch_in[:, k].reshape(here, -1), contract_weight, preferred_element_type=f32
        ).reshape(planes, piece, width),
        lambda sent: (sent, ()),
    )
    layer_low = (residual_one + feedforward_branch + contract_bias.astype(f32)).astype(bf16)

    attn_grad_rows = tp_gather_rows(attn_grad).reshape(group, width)
    outw = contract(mixed_heads, attn_grad_rows, ((0,), (0,)))
    outw_came = lax.ppermute(outw[PAIR:].astype(bf16), "ctx", CTX_X)
    qkv_part = contract(grad_mine, rows_one, ((0,), (0,))) + contract(grad_other, rows_one_x, ((0,), (0,)))
    outw_part = outw[:PAIR] + outw_came.astype(f32)
    parts = jnp.concatenate([qkv_part.astype(bf16), outw_part.astype(bf16)], axis=0)

    packed_parts = packed_grad.reshape(planes, 4, piece, 6 * PAIR)
    dnormed_one, parts = tp_scatter_rows(
        lambda k: jnp.dot(
            packed_parts[:, k].reshape(here, -1), qkv_rel, preferred_element_type=f32
        ).reshape(planes, piece, width),
        lambda sent: tie(sent, parts),
    )
    parts = parts.reshape(4, PAIR, width)
    moves = [[(i, i ^ (2 * d)) for i in range(8)] for d in range(4)]
    came = [
        lax.ppermute(lax.dynamic_index_in_dim(parts, plane ^ d, 0, keepdims=False), "ctx", moves[d])
        for d in range(1, 4)
    ]
    own = lax.dynamic_index_in_dim(parts, plane, 0, keepdims=False)
    grad_tokens = grad_res + norm_back(hat_one, rate_one, gain_first, dnormed_one)
    grad_tokens = planes_swap(grad_tokens.astype(bf16))
    grad_tokens, layer_low, own, came = tie(grad_tokens, layer_low, own, came)
    grad_tokens = grad_tokens.astype(f32)
    total = (own.astype(f32) + sum(c.astype(f32) for c in came)).astype(bf16)
    layer_out = planes_swap(layer_low)

    wide = jnp.zeros((2, 4, PAIR, width), bf16)
    for d in range(4):
        near = total if d == 0 else lax.ppermute(total, "ctx", moves[d])
        far = lax.ppermute(near, "ctx", CTX_X)
        wide = lax.dynamic_update_slice(wide, near[None, None], (side, plane ^ d, 0, 0))
        wide = lax.dynamic_update_slice(wide, far[None, None], (1 - side, plane ^ d, 0, 0))
    qkv_grad = wide[:, :3].astype(f32).reshape(4, 3 * HEAD_DIM, width)
    qkv_grad = jnp.transpose(qkv_grad, (2, 0, 1))
    outw_grad = wide[:, 3].astype(f32)
    small = sum_tp(
        jnp.stack(
            [
                jnp.sum(dnormed_one * hat_one, axis=(0, 1)),
                jnp.sum(dnormed_one, axis=(0, 1)),
                jnp.sum(grad_res, axis=(0, 1)),
                jnp.sum(dnormed_two * hat_two, axis=(0, 1)),
                jnp.sum(dnormed_two, axis=(0, 1)),
                jnp.sum(grad_rows, axis=(0, 1)),
            ]
        )
    )
    bias_sums = jnp.sum(packed_grad, axis=0, dtype=f32)[None]
    bias_sums = order_pair(bias_sums, swapped, 1)
    bias_sums = jnp.pad(bias_sums, ((0, 0), (0, width - 12 * HEAD_DIM)))
    small = sum_ctx(jnp.concatenate([small, fcb_grad[None], bias_sums]))
    bias_sums = small[7, : 12 * HEAD_DIM].reshape(4, 3, HEAD_DIM)
    qvb_grad = jnp.concatenate([bias_sums[:, 0], bias_sums[:, 2]], axis=-1)
    return (
        layer_out,
        grad_tokens,
        small[0],
        small[1],
        qkv_grad,
        qvb_grad,
        outw_grad.reshape(4, HEAD_DIM, width),
        small[2],
        small[3],
        small[4],
        fc_grad.astype(f32),
        small[6],
        proj_grad.astype(f32),
        small[5],
    )


def solution(mesh):
    sizes = dict(zip(mesh.axis_names, mesh.devices.shape))
    body = shards if (sizes["ctx"], sizes["tp"]) == (8, 4) else shards_plain
    return jax.shard_map(
        body,
        mesh=mesh,
        in_specs=(
            P(None, ("ctx", "tp"), None),
            P(),
            P(),
            P(None, "tp", None),
            P("tp", None),
            P("tp", None, None),
            P(),
            P(),
            P(),
            P(None, "tp"),
            P("tp"),
            P("tp", None),
            P(),
            P(None, "ctx"),
            P(None, ("ctx", "tp"), None),
        ),
        out_specs=(
            P(None, ("ctx", "tp"), None),
            P(None, ("ctx", "tp"), None),
            P(),
            P(),
            P(None, "tp", None),
            P("tp", None),
            P("tp", None, None),
            P(),
            P(),
            P(),
            P(None, "tp"),
            P("tp"),
            P("tp", None),
            P(),
        ),
        check_vma=False,
    )
```

```python
import jax
import jax.numpy as jnp
from jax import lax
from jax.experimental import pallas as pl
from jax.experimental.pallas import tpu as pltpu
from jax.sharding import PartitionSpec as P

HEAD_DIM = 64


eps = 1e-05
neg_fill = -1e30


def layer_norm(values, gain, shift):
    centre = jnp.mean(values, axis=-1, keepdims=True)
    centred = values - centre
    spread = jnp.mean(centred * centred, axis=-1, keepdims=True)
    return centred * lax.rsqrt(spread + eps) * gain + shift


def gelu_tanh(values):
    return jax.nn.gelu(values, approximate=True)


def gather_attn(values):
    return lax.all_gather(values, "tp", axis=1, tiled=True)


def reduce_attn(values):
    return lax.psum_scatter(
        values.astype(jnp.bfloat16), "tp", scatter_dimension=1, tiled=True
    ).astype(jnp.float32)


def gather_mlp(values):
    return lax.all_gather(values, "tp", axis=1, tiled=True)


def reduce_mlp(values):
    return lax.psum_scatter(
        values.astype(jnp.bfloat16), "tp", scatter_dimension=1, tiled=True
    ).astype(jnp.float32)


def feed_forward(normed_rows, fc_full, fcb_full, proj_full, grad_in):
    pre_activation = jnp.einsum(
        "scd,df->scf", normed_rows, fc_full, preferred_element_type=jnp.float32
    ) + fcb_full.astype(jnp.float32)
    active_rows = gelu_tanh(pre_activation).astype(jnp.bfloat16)
    branch_part = jnp.einsum(
        "scf,fd->scd", active_rows, proj_full, preferred_element_type=jnp.float32
    )
    act_grad = jnp.einsum("scd,fd->scf", grad_in, proj_full, preferred_element_type=jnp.float32)
    pre_grad = jax.vjp(gelu_tanh, pre_activation)[1](act_grad)[0].astype(jnp.bfloat16)
    proj_grad = jnp.einsum("scf,scd->fd", active_rows, grad_in, preferred_element_type=jnp.float32)
    fc_grad = jnp.einsum("scd,scf->df", normed_rows, pre_grad, preferred_element_type=jnp.float32)
    fcb_grad = jnp.sum(pre_grad, axis=(0, 1), dtype=jnp.float32)
    normed_grad = jnp.einsum("scf,df->scd", pre_grad, fc_full, preferred_element_type=jnp.float32)
    return (branch_part, normed_grad, fc_grad, fcb_grad, proj_grad)


def shards_plain(
    tokens,
    gain_one,
    shift_one,
    query_key_value_weight,
    qv_bias,
    attention_out_weight,
    attention_out_bias,
    gain_two,
    shift_two,
    expand_weight,
    expand_bias,
    contract_weight,
    contract_bias,
    doc_ids,
    out_grad,
):
    score_scale = HEAD_DIM ** (-0.5)
    seq_count = tokens.shape[0]
    span_rows = doc_ids.shape[1]
    heads_here = query_key_value_weight.shape[1]
    full_length = span_rows * lax.axis_size("ctx")
    first_query = lax.axis_index("ctx") * span_rows
    query_pos = first_query + jnp.arange(span_rows, dtype=jnp.int32)
    last_query = first_query + span_rows - 1
    all_ids = lax.all_gather(doc_ids, "ctx", axis=1, tiled=True)

    def allowed_mask(offset, block_width):
        key_pos = offset + jnp.arange(block_width, dtype=jnp.int32)
        key_ids = lax.dynamic_slice_in_dim(all_ids, offset, block_width, 1)
        causal = key_pos[None, :] <= query_pos[:, None]
        same_doc = doc_ids[:, :, None] == key_ids[:, None, :]
        return jnp.logical_and(causal[None], same_doc)[:, None]

    def keep_state(carry_state):
        return carry_state

    gain_first = gain_one.astype(jnp.float32)
    shift_first = shift_one.astype(jnp.float32)
    gain_second = gain_two.astype(jnp.float32)
    shift_second = shift_two.astype(jnp.float32)
    inputs = tokens.astype(jnp.float32)
    first_normed = layer_norm(inputs, gain_first, shift_first)
    rows_one = gather_attn(first_normed.astype(jnp.bfloat16))
    packed_values = jnp.einsum(
        "scd,dhe->sche", rows_one, query_key_value_weight, preferred_element_type=jnp.float32
    )
    bias_pair = qv_bias.astype(jnp.float32)
    queries = (packed_values[..., :HEAD_DIM] + bias_pair[:, :HEAD_DIM]).astype(jnp.bfloat16)
    keys_here = packed_values[..., HEAD_DIM : 2 * HEAD_DIM].astype(jnp.bfloat16)
    values_here = (packed_values[..., 2 * HEAD_DIM :] + bias_pair[:, HEAD_DIM:]).astype(
        jnp.bfloat16
    )
    key_value = jnp.concatenate([keys_here, values_here], axis=-1)
    start_state = (
        jnp.full((seq_count, heads_here, span_rows), neg_fill, jnp.float32),
        jnp.zeros((seq_count, heads_here, span_rows), jnp.float32),
        jnp.zeros((seq_count, heads_here, span_rows, HEAD_DIM), jnp.float32),
    )
    folded = start_state
    piece_rows = lax.all_gather(key_value, "ctx", axis=1, tiled=True)
    piece_len = piece_rows.shape[1]
    block_width = min(piece_len, span_rows)

    def attend_block(carry_state, block_index):
        offset = block_index * block_width

        def attend_compute(inner_state):
            row_best, row_total, weighted = inner_state
            one_block = lax.dynamic_slice_in_dim(
                piece_rows, block_index * block_width, block_width, 1
            )
            scores = (
                jnp.einsum(
                    "sqhe,skhe->shqk",
                    queries,
                    one_block[..., :HEAD_DIM],
                    preferred_element_type=jnp.float32,
                )
                * score_scale
            )
            allowed = allowed_mask(offset, block_width)
            row_top = jnp.max(jnp.where(allowed, scores, neg_fill), axis=-1)
            new_best = jnp.maximum(row_best, row_top)
            soft_terms = jnp.where(allowed, jnp.exp(scores - new_best[..., None]), 0.0)
            rescale = jnp.exp(row_best - new_best)
            row_total = row_total * rescale + jnp.sum(soft_terms, axis=-1)
            weighted = weighted * rescale[..., None] + jnp.einsum(
                "shqk,skhe->shqe",
                soft_terms.astype(jnp.bfloat16),
                one_block[..., HEAD_DIM:],
                preferred_element_type=jnp.float32,
            )
            return (new_best, row_total, weighted)

        return (lax.cond(offset <= last_query, attend_compute, keep_state, carry_state), None)

    folded, _ = lax.scan(
        attend_block, folded, jnp.arange(piece_len // block_width, dtype=jnp.int32)
    )
    row_best, row_total, weighted = folded
    mixed_exact = weighted / row_total[..., None]
    log_total = row_best + jnp.log(row_total)
    mixed_low = jnp.transpose(mixed_exact, (0, 2, 1, 3)).astype(jnp.bfloat16)
    attn_part = jnp.einsum(
        "sche,hed->scd", mixed_low, attention_out_weight, preferred_element_type=jnp.float32
    )
    residual_one = inputs + reduce_attn(attn_part) + attention_out_bias.astype(jnp.float32)
    second_normed = layer_norm(residual_one, gain_second, shift_second)
    normed_low = second_normed.astype(jnp.bfloat16)
    grad_rows = out_grad.astype(jnp.float32)
    grad_low = grad_rows.astype(jnp.bfloat16)
    rows_two = gather_mlp(normed_low)
    grad_gathered = gather_mlp(grad_low)
    branch_part, normed_grad, fc_grad, fcb_grad, proj_grad = feed_forward(
        rows_two, expand_weight, expand_bias, contract_weight, grad_gathered
    )
    feedforward_branch = reduce_mlp(branch_part)
    dnormed_two = reduce_mlp(normed_grad)
    layer_out = (residual_one + feedforward_branch + contract_bias.astype(jnp.float32)).astype(
        jnp.bfloat16
    )
    pull_two = jax.vjp(layer_norm, residual_one, gain_second, shift_second)[1]
    res_extra, gain_two_grad, shift_two_grad = pull_two(dnormed_two)
    grad_res = grad_rows + res_extra
    attn_grad_rows = gather_attn(grad_res.astype(jnp.bfloat16))
    dmixed = jnp.einsum(
        "scd,hed->sche", attn_grad_rows, attention_out_weight, preferred_element_type=jnp.float32
    ).astype(jnp.bfloat16)
    outw_grad = jnp.einsum(
        "sche,scd->hed", mixed_low, attn_grad_rows, preferred_element_type=jnp.float32
    )
    dmixed_heads = jnp.transpose(dmixed, (0, 2, 1, 3))
    row_delta = jnp.sum(dmixed_heads.astype(jnp.float32) * mixed_exact, axis=-1)
    back_start = (
        jnp.zeros((seq_count, heads_here, span_rows, HEAD_DIM), jnp.float32),
        jnp.zeros((seq_count, full_length, heads_here, 2 * HEAD_DIM), jnp.float32),
    )
    folded = back_start
    back_piece_rows = lax.all_gather(key_value, "ctx", axis=1, tiled=True)
    piece_len = back_piece_rows.shape[1]
    back_block_width = min(piece_len, span_rows)

    def back_block(carry_state, block_index):
        offset = block_index * back_block_width

        def back_compute(inner_state):
            query_grad, pair_grads = inner_state
            one_block = lax.dynamic_slice_in_dim(
                back_piece_rows, block_index * back_block_width, back_block_width, 1
            )
            keys_block = one_block[..., :HEAD_DIM]
            values_block = one_block[..., HEAD_DIM:]
            scores = (
                jnp.einsum(
                    "sqhe,skhe->shqk", queries, keys_block, preferred_element_type=jnp.float32
                )
                * score_scale
            )
            allowed = allowed_mask(offset, back_block_width)
            soft_terms = jnp.where(allowed, jnp.exp(scores - log_total[..., None]), 0.0)
            soft_grad = jnp.einsum(
                "shqe,skhe->shqk", dmixed_heads, values_block, preferred_element_type=jnp.float32
            )
            score_grad = (soft_terms * (soft_grad - row_delta[..., None])).astype(jnp.bfloat16)
            query_grad = query_grad + score_scale * jnp.einsum(
                "shqk,skhe->shqe", score_grad, keys_block, preferred_element_type=jnp.float32
            )
            key_grad = score_scale * jnp.einsum(
                "shqk,sqhe->skhe", score_grad, queries, preferred_element_type=jnp.float32
            )
            value_grad = jnp.einsum(
                "shqk,shqe->skhe",
                soft_terms.astype(jnp.bfloat16),
                dmixed_heads,
                preferred_element_type=jnp.float32,
            )
            earlier = lax.dynamic_slice_in_dim(pair_grads, offset, back_block_width, 1)
            pair_grads = lax.dynamic_update_slice_in_dim(
                pair_grads, earlier + jnp.concatenate([key_grad, value_grad], axis=-1), offset, 1
            )
            return (query_grad, pair_grads)

        return (lax.cond(offset <= last_query, back_compute, keep_state, carry_state), None)

    folded, _ = lax.scan(
        back_block, folded, jnp.arange(piece_len // back_block_width, dtype=jnp.int32)
    )
    query_grad, pair_grads = folded
    pair_mine = lax.psum_scatter(
        pair_grads.astype(jnp.bfloat16), "ctx", scatter_dimension=1, tiled=True
    )
    query_low = jnp.transpose(query_grad, (0, 2, 1, 3)).astype(jnp.bfloat16)
    packed_grad = jnp.concatenate([query_low, pair_mine], axis=-1)
    qkv_grad = jnp.einsum(
        "scd,sche->dhe", rows_one, packed_grad, preferred_element_type=jnp.float32
    )
    qvb_grad = jnp.concatenate(
        [
            jnp.sum(query_low, axis=(0, 1), dtype=jnp.float32),
            jnp.sum(pair_mine[..., HEAD_DIM:], axis=(0, 1), dtype=jnp.float32),
        ],
        axis=-1,
    )
    normed_one_grad = reduce_attn(
        jnp.einsum(
            "sche,dhe->scd", packed_grad, query_key_value_weight, preferred_element_type=jnp.float32
        )
    )
    pull_one = jax.vjp(layer_norm, inputs, gain_first, shift_first)[1]
    input_extra, gain_one_grad, shift_one_grad = pull_one(normed_one_grad)
    grad_tokens = grad_res + input_extra
    small_sums = lax.psum(
        (
            gain_one_grad,
            shift_one_grad,
            jnp.sum(grad_res, axis=(0, 1)),
            gain_two_grad,
            shift_two_grad,
            jnp.sum(grad_rows, axis=(0, 1)),
        ),
        ("ctx", "tp"),
    )
    qkv_grad, qvb_grad, outw_grad, fc_grad, fcb_grad, proj_grad = (
        lax.psum(qkv_grad.astype(jnp.bfloat16), "ctx").astype(jnp.float32),
        lax.psum(qvb_grad.astype(jnp.bfloat16), "ctx").astype(jnp.float32),
        lax.psum(outw_grad.astype(jnp.bfloat16), "ctx").astype(jnp.float32),
        lax.psum(fc_grad.astype(jnp.bfloat16), "ctx").astype(jnp.float32),
        lax.psum(fcb_grad.astype(jnp.bfloat16), "ctx").astype(jnp.float32),
        lax.psum(proj_grad.astype(jnp.bfloat16), "ctx").astype(jnp.float32),
    )
    return (
        layer_out,
        grad_tokens,
        small_sums[0],
        small_sums[1],
        qkv_grad,
        qvb_grad,
        outw_grad,
        small_sums[2],
        small_sums[3],
        small_sums[4],
        fc_grad,
        fcb_grad,
        proj_grad,
        small_sums[5],
    )


bf16 = jnp.bfloat16
f32 = jnp.float32
BLK = 512
PAIR = 2 * HEAD_DIM
DOC_FAR = -(2.0**100)
CAUSAL_FAR = -2e30

TP_CORE = [(i, i ^ 1) for i in range(4)]
TP_ROW = [(i, i ^ 2) for i in range(4)]
CTX_X = [(i, i ^ 1) for i in range(8)]
CTX_Z1 = [(i, i ^ 2) for i in range(8)]
CTX_Z2 = [(i, i ^ 4) for i in range(8)]
CTX_PLANES = [[0, 2, 4, 6], [1, 3, 5, 7]]


def tie(*values):
    return lax.optimization_barrier(values)


def contract(a, b, dims):
    return lax.dot_general(a, b, (dims, ((), ())), preferred_element_type=f32)


def head_pair(packed, part):
    low = part * HEAD_DIM
    high = (part + 3) * HEAD_DIM
    return jnp.concatenate(
        [packed[:, low : low + HEAD_DIM], packed[:, high : high + HEAD_DIM]], axis=1
    )


def lane_half(rows, head):
    lanes = lax.broadcasted_iota(jnp.int32, (rows, PAIR), 1)
    return (lanes >= HEAD_DIM) if head else (lanes < HEAD_DIM)


def attend_kernel(
    first_ref, mine_ref, other_ref, qdoc_ref, kdoc_ref, bias_ref,
    out_mine_ref, out_other_ref, exact_ref, log_ref, key_ref, value_ref, best_ref, total_ref, acc_ref,
):
    i = pl.program_id(0)
    half = BLK // 2
    block = pl.ds(pl.multiple_of(i * BLK, BLK), BLK)
    packed = jnp.concatenate([mine_ref[...], other_ref[...]], axis=0)
    queries = head_pair(packed, 0) * jnp.asarray(HEAD_DIM**-0.5, bf16)
    key_ref[block, :PAIR] = head_pair(packed, 1)
    key_ref[block, PAIR:] = kdoc_ref[...]
    value_ref[block, :] = head_pair(packed, 2)
    qdoc = qdoc_ref[...]
    query_heads = [
        jnp.concatenate([jnp.where(lane_half(BLK, h), queries, jnp.zeros_like(queries)), qdoc], axis=1)
        for h in range(2)
    ]
    best_ref[...] = jnp.full_like(best_ref, neg_fill)
    total_ref[...] = jnp.zeros_like(total_ref)
    acc_ref[...] = jnp.zeros_like(acc_ref)

    def visit(j, bias):
        keys = pl.ds(pl.multiple_of(j * BLK, BLK), BLK)
        key_block = key_ref[keys, :]
        value_block = value_ref[keys, :]
        for h in range(2):
            scores = contract(key_block, query_heads[h], ((1,), (1,)))
            if bias is not None:
                scores = scores + bias.astype(f32)
            old = best_ref[h : h + 1, :]
            new = jnp.maximum(old, jnp.max(scores, axis=0, keepdims=True))
            weights = jnp.exp(scores - new)
            fade = jnp.exp(old - new)
            total_ref[h : h + 1, :] = total_ref[h : h + 1, :] * fade + jnp.sum(
                weights, axis=0, keepdims=True
            )
            product = contract(value_block, weights.astype(bf16), ((0,), (0,)))
            part = slice(h * HEAD_DIM, (h + 1) * HEAD_DIM)
            acc_ref[part, :] = acc_ref[part, :] * fade + product[part, :]
            best_ref[h : h + 1, :] = new

    def step(j, carry):
        visit(j, None)
        return carry

    lax.fori_loop(first_ref[i], i, step, 0)
    visit(i, bias_ref[...])
    for h in range(2):
        part = slice(h * HEAD_DIM, (h + 1) * HEAD_DIM)
        acc_ref[part, :] = acc_ref[part, :] / total_ref[h : h + 1, :]
        log_ref[h : h + 1, :] = best_ref[h : h + 1, :] + jnp.log(total_ref[h : h + 1, :])
    mixed = acc_ref[...]
    exact_ref[...] = mixed
    low = jnp.transpose(mixed).astype(bf16)
    out_mine_ref[...] = low[:half]
    out_other_ref[...] = low[half:]


def attend_back_kernel(
    first_ref, mine_ref, other_ref, qdoc_ref, kdoc_ref, bias_ref, exact_ref, log_ref, dmine_ref, dother_ref,
    out_mine_ref, out_other_ref, key_ref, value_ref, dkey_ref, dvalue_ref, dquery_ref, dquery_all_ref,
):
    i = pl.program_id(0)
    half = BLK // 2
    block = pl.ds(pl.multiple_of(i * BLK, BLK), BLK)
    packed = jnp.concatenate([mine_ref[...], other_ref[...]], axis=0)
    scale = HEAD_DIM**-0.5
    queries = head_pair(packed, 0) * jnp.asarray(scale, bf16)
    key_ref[block, :PAIR] = head_pair(packed, 1)
    key_ref[block, PAIR:] = kdoc_ref[...]
    value_ref[block, :] = head_pair(packed, 2)
    dkey_ref[block, :] = jnp.zeros((BLK, PAIR), f32)
    dvalue_ref[block, :] = jnp.zeros((BLK, PAIR), f32)
    dquery_ref[...] = jnp.zeros_like(dquery_ref)
    dmixed = jnp.concatenate([dmine_ref[...], dother_ref[...]], axis=0)
    qdoc = qdoc_ref[...]
    masked = [jnp.where(lane_half(BLK, h), queries, jnp.zeros_like(queries)) for h in range(2)]
    dmasked = [jnp.where(lane_half(BLK, h), dmixed, jnp.zeros_like(dmixed)) for h in range(2)]
    query_heads = [jnp.concatenate([masked[h], qdoc], axis=1) for h in range(2)]
    product = jnp.transpose(dmixed.astype(f32)) * exact_ref[...]
    deltas = [
        jnp.sum(product[h * HEAD_DIM : (h + 1) * HEAD_DIM, :], axis=0, keepdims=True) for h in range(2)
    ]
    logs = [log_ref[h : h + 1, :] for h in range(2)]

    def visit(j, bias):
        keys = pl.ds(pl.multiple_of(j * BLK, BLK), BLK)
        key_block = key_ref[keys, :]
        value_block = value_ref[keys, :]
        dkey = dkey_ref[keys, :]
        dvalue = dvalue_ref[keys, :]
        for h in range(2):
            scores = contract(key_block, query_heads[h], ((1,), (1,)))
            if bias is not None:
                scores = scores + bias.astype(f32)
            weights = jnp.exp(scores - logs[h])
            dweights = contract(value_block, dmasked[h], ((1,), (1,)))
            dscores = (weights * (dweights - deltas[h])).astype(bf16)
            dvalue = dvalue + contract(weights.astype(bf16), dmasked[h], ((1,), (0,)))
            dkey = dkey + contract(dscores, masked[h], ((1,), (0,)))
            part = slice(h * HEAD_DIM, (h + 1) * HEAD_DIM)
            turned = contract(key_block[:, :PAIR], dscores, ((0,), (0,)))
            dquery_ref[part, :] = dquery_ref[part, :] + turned[part, :]
        dkey_ref[keys, :] = dkey
        dvalue_ref[keys, :] = dvalue

    def step(j, carry):
        visit(j, None)
        return carry

    lax.fori_loop(first_ref[i], i, step, 0)
    visit(i, bias_ref[...])
    dquery_all_ref[block, :] = jnp.transpose(dquery_ref[...] * scale)

    @pl.when(i == pl.num_programs(0) - 1)
    def _():
        for b in range(4):
            for side, out in ((0, out_mine_ref), (1, out_other_ref)):
                source = slice(b * BLK + side * half, b * BLK + (side + 1) * half)
                target = slice(b * half, (b + 1) * half)
                grads = [ref[source, :] for ref in (dquery_all_ref, dkey_ref, dvalue_ref)]
                out[target, :] = jnp.concatenate(
                    [g[:, h * HEAD_DIM : (h + 1) * HEAD_DIM] for h in range(2) for g in grads], axis=1
                ).astype(bf16)


def whole(shape):
    return pl.BlockSpec(shape, lambda i: (0,) * len(shape))


def down(rows, cols):
    return pl.BlockSpec((rows, cols), lambda i: (i, 0))


def along(rows, cols):
    return pl.BlockSpec((rows, cols), lambda i: (0, i))


def attend(first, mine, other, qdoc, kdoc, bias):
    length = qdoc.shape[0]
    half = length // 2
    return pl.pallas_call(
        attend_kernel,
        grid=(length // BLK,),
        in_specs=[
            pl.BlockSpec(memory_space=pltpu.SMEM),
            down(BLK // 2, 3 * PAIR), down(BLK // 2, 3 * PAIR), down(BLK, PAIR), down(BLK, PAIR),
            whole(bias.shape),
        ],
        out_specs=[down(BLK // 2, PAIR), down(BLK // 2, PAIR), along(PAIR, BLK), along(2, BLK)],
        out_shape=[
            jax.ShapeDtypeStruct((half, PAIR), bf16),
            jax.ShapeDtypeStruct((half, PAIR), bf16),
            jax.ShapeDtypeStruct((PAIR, length), f32),
            jax.ShapeDtypeStruct((2, length), f32),
        ],
        scratch_shapes=[
            pltpu.VMEM((length, 2 * PAIR), bf16),
            pltpu.VMEM((length, PAIR), bf16),
            pltpu.VMEM((2, BLK), f32),
            pltpu.VMEM((2, BLK), f32),
            pltpu.VMEM((PAIR, BLK), f32),
        ],
        compiler_params=pltpu.CompilerParams(
            dimension_semantics=("arbitrary",), vmem_limit_bytes=40 << 20
        ),
        name="attend",
    )(first, mine, other, qdoc, kdoc, bias)


def attend_back(first, mine, other, qdoc, kdoc, bias, exact, log_total, dmine, dother):
    length = qdoc.shape[0]
    half = length // 2
    operands = (mine, other, qdoc, kdoc, bias, exact, log_total, dmine, dother)
    return pl.pallas_call(
        attend_back_kernel,
        grid=(length // BLK,),
        in_specs=[
            pl.BlockSpec(memory_space=pltpu.SMEM),
            down(BLK // 2, 3 * PAIR), down(BLK // 2, 3 * PAIR), down(BLK, PAIR), down(BLK, PAIR),
            whole(bias.shape), along(PAIR, BLK), along(2, BLK), down(BLK // 2, PAIR), down(BLK // 2, PAIR),
        ],
        out_specs=[whole((half, 3 * PAIR)), whole((half, 3 * PAIR))],
        out_shape=[jax.ShapeDtypeStruct((half, 3 * PAIR), bf16)] * 2,
        scratch_shapes=[
            pltpu.VMEM((length, 2 * PAIR), bf16),
            pltpu.VMEM((length, PAIR), bf16),
            pltpu.VMEM((length, PAIR), f32),
            pltpu.VMEM((length, PAIR), f32),
            pltpu.VMEM((PAIR, BLK), f32),
            pltpu.VMEM((length, PAIR), f32),
        ],
        compiler_params=pltpu.CompilerParams(
            dimension_semantics=("arbitrary",), vmem_limit_bytes=48 << 20
        ),
        name="attend_back",
    )(first, *operands)


def planes_swap(values):
    return lax.all_to_all(values, "ctx", 0, 0, axis_index_groups=CTX_PLANES, tiled=False)


def tp_gather(values):
    core = lax.ppermute(values, "tp", TP_CORE)
    row = lax.ppermute(values, "tp", TP_ROW)
    both = lax.ppermute(row, "tp", TP_CORE)
    return [values, core, row, both]


def tp_gather_rows(values):
    return jnp.stack(tp_gather(values), axis=1)


def tp_scatter_rows(make_part, meanwhile):
    away = jnp.stack([make_part(3), make_part(1)]).astype(bf16)
    came = lax.ppermute(away, "tp", TP_CORE)
    across = (make_part(2) + came[0].astype(f32)).astype(bf16)
    across, filler = meanwhile(across)
    arrived = lax.ppermute(across, "tp", TP_ROW)
    own, filler = tie(make_part(0) + came[1].astype(f32), filler)
    return own + arrived.astype(f32), filler


def tp_swap(pieces):
    return [
        pieces[0],
        lax.ppermute(pieces[1], "tp", TP_CORE),
        lax.ppermute(pieces[2], "tp", TP_ROW),
        lax.ppermute(pieces[3], "tp", [(i, i ^ 3) for i in range(4)]),
    ]


def sum_ctx(values):
    for perm in (CTX_X, CTX_Z1, CTX_Z2):
        values = values + lax.ppermute(values, "ctx", perm)
    return values


def sum_tp(values):
    for perm in (TP_CORE, TP_ROW):
        values = values + lax.ppermute(values, "tp", perm)
    return values


def sum_all(values):
    return sum_ctx(sum_tp(values))


def norm_stats(values):
    centred = values - jnp.mean(values, axis=-1, keepdims=True)
    rate = lax.rsqrt(jnp.mean(centred * centred, axis=-1, keepdims=True) + eps)
    return centred * rate, rate


def norm_back(hat, rate, gain, grad):
    dhat = grad * gain
    return rate * (
        dhat
        - jnp.mean(dhat, axis=-1, keepdims=True)
        - hat * jnp.mean(dhat * hat, axis=-1, keepdims=True)
    )


def order_pair(values, swapped, axis):
    first, second = jnp.split(values, 2, axis=axis)
    return jnp.where(
        swapped,
        jnp.concatenate([second, first], axis=axis),
        jnp.concatenate([first, second], axis=axis),
    )


def shards(
    tokens,
    gain_one,
    shift_one,
    query_key_value_weight,
    qv_bias,
    attention_out_weight,
    attention_out_bias,
    gain_two,
    shift_two,
    expand_weight,
    expand_bias,
    contract_weight,
    contract_bias,
    doc_ids,
    out_grad,
):
    width = tokens.shape[2]
    span = doc_ids.shape[1]
    piece = tokens.shape[1]
    planes = tokens.shape[0]
    here = planes * piece
    group = here * 4
    ctx_at = lax.axis_index("ctx")
    tp_at = lax.axis_index("tp")
    side = ctx_at % 2
    plane = ctx_at // 2
    swapped = side == 1
    gain_first, shift_first = gain_one.astype(f32), shift_one.astype(f32)
    gain_second, shift_second = gain_two.astype(f32), shift_two.astype(f32)

    ids = jnp.pad(doc_ids.astype(bf16), ((0, 0), (0, width - span)))
    ids = jnp.broadcast_to(ids[:, None], (planes, 16, width))
    arrived = planes_swap(jnp.concatenate([tokens, ids], axis=1))
    inputs = arrived[:, :piece].astype(f32)
    ids = arrived[:, piece, :span]
    ids = jnp.stack([ids, lax.ppermute(ids, "ctx", CTX_X)], axis=1).astype(jnp.int32)

    qkv_rel = jnp.transpose(query_key_value_weight, (1, 2, 0)).reshape(12 * HEAD_DIM, width)
    qkv_rel = order_pair(qkv_rel, swapped, 0)
    zero_key = jnp.zeros((4, HEAD_DIM), f32)
    bias_all = qv_bias.astype(f32)
    bias_rel = jnp.concatenate([bias_all[:, :HEAD_DIM], zero_key, bias_all[:, HEAD_DIM:]], axis=1)
    bias_rel = order_pair(bias_rel.reshape(12 * HEAD_DIM), swapped, 0)
    out_rel = order_pair(attention_out_weight.reshape(4 * HEAD_DIM, width), swapped, 0)
    hat_one, rate_one = norm_stats(inputs)
    rows_one = tp_gather_rows((hat_one * gain_first + shift_first).astype(bf16)).reshape(group, width)

    rows_one, out_rel = tie(rows_one, out_rel)

    def project(rows, j):
        part = slice(j * 6 * HEAD_DIM, (j + 1) * 6 * HEAD_DIM)
        return (contract(rows, qkv_rel[part], ((1,), (1,))) + bias_rel[part]).astype(bf16)

    qkv_away, rows_one = tie(project(rows_one, 1), rows_one)
    qkv_other = lax.ppermute(qkv_away, "ctx", CTX_X)
    qkv_mine, out_grad = tie(project(rows_one, 0), out_grad)

    ids = ids.reshape(planes, 2, 2, 2, piece)
    ids = jnp.where(tp_at % 2 == 1, jnp.flip(ids, 3), ids)
    ids = jnp.where(tp_at // 2 == 1, jnp.flip(ids, 2), ids).reshape(planes, 2 * span)
    low_id, high_id = jnp.min(ids, axis=1), jnp.max(ids, axis=1)
    first_block = jnp.sum((high_id[None, :] < low_id[:, None]).astype(jnp.int32), axis=1)
    lanes = jnp.arange(PAIR, dtype=jnp.int32)
    same = ids.reshape(-1, 1) == lanes[None, :]
    kdoc = same.astype(bf16)
    qdoc = jnp.where(same, 0.0, DOC_FAR).astype(bf16)
    place = (
        ((side ^ jnp.arange(2, dtype=jnp.int32)) * span)[:, None, None]
        + ((tp_at ^ jnp.arange(4, dtype=jnp.int32)) * piece)[None, :, None]
        + jnp.arange(piece, dtype=jnp.int32)[None, None, :]
    ).reshape(-1)
    bias = jnp.where(place[:, None] <= place[None, :], 0.0, CAUSAL_FAR).astype(bf16)

    grad_rows = planes_swap(out_grad)
    out_full = tp_gather(out_rel)
    grad_gathered = tp_gather_rows(grad_rows).reshape(group, width)
    grad_rows = grad_rows.astype(f32)
    act_grad = contract(grad_gathered, contract_weight, ((1,), (1,)))

    mixed_mine, mixed_other, exact, log_total = attend(
        first_block, qkv_mine, qkv_other, qdoc, kdoc, bias
    )
    mixed_arrived = lax.ppermute(mixed_other, "ctx", CTX_X)
    mixed_arrived, rows_one = tie(mixed_arrived, rows_one)
    mixed_heads = jnp.concatenate([mixed_mine, mixed_arrived], axis=1)
    rows_one_x = lax.ppermute(rows_one, "ctx", CTX_X)
    by_tp = mixed_heads.reshape(planes, 4, piece, 2 * PAIR)
    mixed_pieces = tp_swap([by_tp[:, k] for k in range(4)])
    attn_branch = sum(
        contract(mixed_pieces[k].reshape(here, 2 * PAIR), out_full[k], ((1,), (0,))) for k in range(4)
    ).reshape(planes, piece, width)
    residual_one = inputs + attn_branch + attention_out_bias.astype(f32)

    hat_two, rate_two = norm_stats(residual_one)
    rows_two = tp_gather_rows((hat_two * gain_second + shift_second).astype(bf16)).reshape(group, width)
    pre_act = jnp.dot(rows_two, expand_weight, preferred_element_type=f32) + expand_bias.astype(f32)
    active, pull_gelu = jax.vjp(gelu_tanh, pre_act)
    active = active.astype(bf16)
    dpre = pull_gelu(act_grad)[0].astype(bf16)
    fc_grad = contract(rows_two, dpre, ((0,), (0,))).astype(bf16)
    proj_grad = contract(active, grad_gathered, ((0,), (0,))).astype(bf16)
    fc_grad, proj_grad, dpre = tie(fc_grad, proj_grad, dpre)
    dpre_parts = dpre.reshape(planes, 4, piece, -1)
    dnormed_two, _ = tp_scatter_rows(
        lambda k: contract(
            dpre_parts[:, k].reshape(here, -1), expand_weight, ((1,), (1,))
        ).reshape(planes, piece, width),
        lambda sent: (sent, ()),
    )
    fcb_grad = jnp.sum(dpre, axis=0, dtype=f32)
    proj_grad, fc_grad = lax.psum((proj_grad, fc_grad), "ctx")

    grad_res = grad_rows + norm_back(hat_two, rate_two, gain_second, dnormed_two)
    attn_grad = grad_res.astype(bf16)
    attn_rows = attn_grad.reshape(here, width)
    dmixed = tp_swap(
        [
            contract(attn_rows, out_full[k], ((1,), (1,))).astype(bf16).reshape(planes, piece, 2 * PAIR)
            for k in range(4)
        ]
    )
    dmixed = jnp.stack(dmixed, axis=1).reshape(group, 2 * PAIR)
    dmixed, attn_grad, active = tie(dmixed, attn_grad, active)
    dmixed_other = lax.ppermute(dmixed[:, PAIR:], "ctx", CTX_X)
    grad_mine, grad_other = attend_back(
        first_block, qkv_mine, qkv_other, qdoc, kdoc, bias, exact, log_total, dmixed[:, :PAIR], dmixed_other
    )
    grad_mine, grad_other, mixed_heads = tie(grad_mine, grad_other, mixed_heads)
    packed_grad = jnp.concatenate([grad_mine, lax.ppermute(grad_other, "ctx", CTX_X)], axis=1)

    branch_in = active.reshape(planes, 4, piece, -1)
    feedforward_branch, _ = tp_scatter_rows(
        lambda k: jnp.dot(
            branch_in[:, k].reshape(here, -1), contract_weight, preferred_element_type=f32
        ).reshape(planes, piece, width),
        lambda sent: (sent, ()),
    )
    layer_low = (residual_one + feedforward_branch + contract_bias.astype(f32)).astype(bf16)

    attn_grad_rows = tp_gather_rows(attn_grad).reshape(group, width)
    outw = contract(mixed_heads, attn_grad_rows, ((0,), (0,)))
    outw_came = lax.ppermute(outw[PAIR:].astype(bf16), "ctx", CTX_X)
    qkv_part = contract(grad_mine, rows_one, ((0,), (0,))) + contract(grad_other, rows_one_x, ((0,), (0,)))
    outw_part = outw[:PAIR] + outw_came.astype(f32)
    parts = jnp.concatenate([qkv_part.astype(bf16), outw_part.astype(bf16)], axis=0)

    packed_parts = packed_grad.reshape(planes, 4, piece, 6 * PAIR)
    dnormed_one, parts = tp_scatter_rows(
        lambda k: jnp.dot(
            packed_parts[:, k].reshape(here, -1), qkv_rel, preferred_element_type=f32
        ).reshape(planes, piece, width),
        lambda sent: tie(sent, parts),
    )
    parts = parts.reshape(4, PAIR, width)
    moves = [[(i, i ^ (2 * d)) for i in range(8)] for d in range(4)]
    came = [
        lax.ppermute(lax.dynamic_index_in_dim(parts, plane ^ d, 0, keepdims=False), "ctx", moves[d])
        for d in range(1, 4)
    ]
    own = lax.dynamic_index_in_dim(parts, plane, 0, keepdims=False)
    grad_tokens = grad_res + norm_back(hat_one, rate_one, gain_first, dnormed_one)
    grad_tokens = planes_swap(grad_tokens.astype(bf16))
    grad_tokens, layer_low, own, came = tie(grad_tokens, layer_low, own, came)
    grad_tokens = grad_tokens.astype(f32)
    total = (own.astype(f32) + sum(c.astype(f32) for c in came)).astype(bf16)
    small = sum_tp(
        jnp.stack(
            [
                jnp.sum(dnormed_one * hat_one, axis=(0, 1)),
                jnp.sum(dnormed_one, axis=(0, 1)),
                jnp.sum(grad_res, axis=(0, 1)),
                jnp.sum(dnormed_two * hat_two, axis=(0, 1)),
                jnp.sum(dnormed_two, axis=(0, 1)),
                jnp.sum(grad_rows, axis=(0, 1)),
            ]
        )
    )
    total, small = tie(total, small)
    layer_out = planes_swap(layer_low)

    wide = jnp.zeros((2, 4, PAIR, width), bf16)
    for d in range(4):
        near = total if d == 0 else lax.ppermute(total, "ctx", moves[d])
        far = lax.ppermute(near, "ctx", CTX_X)
        wide = lax.dynamic_update_slice(wide, near[None, None], (side, plane ^ d, 0, 0))
        wide = lax.dynamic_update_slice(wide, far[None, None], (1 - side, plane ^ d, 0, 0))
    qkv_grad = wide[:, :3].astype(f32).reshape(4, 3 * HEAD_DIM, width)
    qkv_grad = jnp.transpose(qkv_grad, (2, 0, 1))
    outw_grad = wide[:, 3].astype(f32)
    bias_sums = jnp.sum(packed_grad, axis=0, dtype=f32)[None]
    bias_sums = order_pair(bias_sums, swapped, 1)
    bias_sums = jnp.pad(bias_sums, ((0, 0), (0, width - 12 * HEAD_DIM)))
    small = sum_ctx(jnp.concatenate([small, fcb_grad[None], bias_sums]))
    bias_sums = small[7, : 12 * HEAD_DIM].reshape(4, 3, HEAD_DIM)
    qvb_grad = jnp.concatenate([bias_sums[:, 0], bias_sums[:, 2]], axis=-1)
    return (
        layer_out,
        grad_tokens,
        small[0],
        small[1],
        qkv_grad,
        qvb_grad,
        outw_grad.reshape(4, HEAD_DIM, width),
        small[2],
        small[3],
        small[4],
        fc_grad.astype(f32),
        small[6],
        proj_grad.astype(f32),
        small[5],
    )


def solution(mesh):
    sizes = dict(zip(mesh.axis_names, mesh.devices.shape))
    body = shards if (sizes["ctx"], sizes["tp"]) == (8, 4) else shards_plain
    return jax.shard_map(
        body,
        mesh=mesh,
        in_specs=(
            P(None, ("ctx", "tp"), None),
            P(),
            P(),
            P(None, "tp", None),
            P("tp", None),
            P("tp", None, None),
            P(),
            P(),
            P(),
            P(None, "tp"),
            P("tp"),
            P("tp", None),
            P(),
            P(None, "ctx"),
            P(None, ("ctx", "tp"), None),
        ),
        out_specs=(
            P(None, ("ctx", "tp"), None),
            P(None, ("ctx", "tp"), None),
            P(),
            P(),
            P(None, "tp", None),
            P("tp", None),
            P("tp", None, None),
            P(),
            P(),
            P(),
            P(None, "tp"),
            P("tp"),
            P("tp", None),
            P(),
        ),
        check_vma=False,
    )
```
